32 devices in a mesh: row: 8 (over z, core), col: 4 (over y, x).
Axes of the slice: x: 2, y: 2, z: 4, core: 2. Of those that a mesh axis runs over, the one named last changes fastest.
Arguments:
- inputs: bfloat16 [8192, 2048], P('row', 'col'), may hold values from -6 to 6
- cotangent: bfloat16 [8192, 2048], P('row', 'col'), may hold values from -6 to 6
- lengths: int32 [2, 8], replicated, may hold values from 1 to 512, 2048 in all within a row
- query_key_value_weight: bfloat16 [2048, 3, 2048], P('row', None, 'col'), may hold values from -0.1875 to 0.1875
- out_weight: bfloat16 [2048, 2048], P('col', 'row'), may hold values from -1 to 1
- gate_weight: bfloat16 [2048, 8192], P('row', 'col'), may hold values from -0.125 to 0.125
- up_weight: bfloat16 [2048, 8192], P('row', 'col'), may hold values from -0.125 to 0.125
- down_weight: bfloat16 [8192, 2048], P('col', 'row'), may hold values from -0.09375 to 0.09375
Outputs:
- output: bfloat16 [8192, 2048], P('row', 'col')
- input_grad: float32 [8192, 2048], P('row', 'col')
- qkv_grad: float32 [2048, 3, 2048], P('row', None, 'col')
- out_grad: float32 [2048, 2048], P('col', 'row')
- gate_grad: float32 [2048, 8192], P('row', 'col')
- up_grad: float32 [2048, 8192], P('row', 'col')
- down_grad: float32 [8192, 2048], P('col', 'row')
The draws below stay inside these ranges and needn't reach their ends.
Inputs may be any that keep to these rules, and one draw needn't show every extreme that they name: `lengths`: row g gives, in order, the tokens of the 8 continuations of group g; each row sums to 2048 and its largest entry is 512.
All inputs are finite; a program needn't handle non-finite values.
Results may differ from the reference program's by a relative error of at most 0.02.
Values may be sent and summed in bfloat16 or wider, within the bound.
A program may use at most 256 MiB of HBM per device.

```python
import math
import jax
import jax.numpy as jnp
import numpy as np
from jax import lax

D = 2048
HEADS = 16
HEAD = 128
FF = 8192
PROMPT = 2048
CONT = 8
CLEN = 256
TOK_DEV = 1024
GROUP_LEN = 4096
TOKENS = 8192
GROUPS = 2


def steps_of(key, extent, split, smallest, high):
    def one(dim, blocks):
        draws = jax.random.uniform(jax.random.fold_in(jax.random.fold_in(key, 6), dim), (blocks,), jnp.float32, smallest / len(split), high / len(split))
        return jnp.repeat(jnp.exp(draws), extent[dim] // blocks).reshape((-1,) + (1,) * (len(extent) - dim - 1))

    factor_of = one(*split[0])
    for cut in split[1:]:
        factor_of = factor_of * one(*cut)
    return factor_of


def split_up(amount, total, limit, slope):
    loads = [(1 << 20) // math.isqrt(grade ** slope) + 1 for grade in range(2, amount + 1)]
    surplus, holding = total - limit - (amount - 1), [1] * (amount - 1)
    while surplus > 0:
        free = [i for i in range(amount - 1) if holding[i] < limit]
        mass, remaining = sum([loads[i] for i in free]), surplus
        for i in free:
            extra = min(limit - holding[i], max(1, remaining * loads[i] // mass), surplus)
            holding[i] = holding[i] + extra
            surplus = surplus - extra
    return np.array([limit] + holding)


def ragged(stream_key, amount, total, limit, slope):
    if amount == 2:
        one = jax.random.randint(stream_key, (), max(1, total - limit), min(limit, total - 1) + 1)
        return jnp.stack([one, total - one])
    sizes = jnp.asarray(split_up(amount, total, limit, slope), jnp.int32)
    pairs = (amount - 1) // 2
    source_of, receiver = sizes[1:1 + 2 * pairs:2], sizes[2:2 + 2 * pairs:2]
    room = jnp.minimum(source_of - 1, limit - receiver)
    shifted = jax.random.randint(jax.random.fold_in(stream_key, 1), (pairs,), 0, 1 << 20) % (room + 1)
    sizes = sizes.at[1:1 + 2 * pairs:2].set(source_of - shifted).at[2:2 + 2 * pairs:2].set(receiver + shifted)
    return sizes[jax.random.permutation(jax.random.fold_in(stream_key, 2), amount)]


def gaussian(rng, dims, width, bound, split=(), kind=jnp.bfloat16):
    drawn = jax.random.normal(rng, dims, jnp.float32) * width
    if len(split) > 0:
        drawn = steps_of(rng, dims, split, -0.22, 0.18) * drawn
    return jnp.clip(drawn, min=-bound, max=bound).astype(kind)


def setup_inputs(seed: int = 0) -> dict:
    streams_of = jax.random.split(jax.random.key(seed), 9)
    inputs = gaussian(streams_of[0], (TOKENS, D), 1.0, 6.0, ((0, 8), (1, 4)))
    cotangent = gaussian(streams_of[1], (TOKENS, D), 1.0, 6.0, ((0, 8), (1, 4)))
    lengths = jax.vmap(lambda own: ragged(own, CONT, CONT * CLEN, 2 * CLEN, 1))(jax.random.split(streams_of[2], GROUPS)).reshape((GROUPS, CONT)).astype(jnp.int32)
    query_key_value_weight = gaussian(streams_of[3], (D, 3, D), (D // 2) ** -0.5, 0.1875, ((0, 8), (2, 4)))
    out_weight = gaussian(streams_of[4], (D, D), (D // 64) ** -0.5, 1.0, ((0, 4), (1, 8)))
    gate_weight = gaussian(streams_of[5], (D, FF), D ** -0.5, 0.125, ((0, 8), (1, 4)))
    up_weight = gaussian(streams_of[6], (D, FF), D ** -0.5, 0.125, ((0, 8), (1, 4)))
    down_weight = gaussian(streams_of[7], (FF, D), (FF // 2) ** -0.5, 0.09375, ((0, 4), (1, 8)))
    return dict(inputs=inputs, cotangent=cotangent, lengths=lengths, query_key_value_weight=query_key_value_weight, out_weight=out_weight, gate_weight=gate_weight, up_weight=up_weight, down_weight=down_weight)


@jax.custom_vjp
def low(v):
    return lax.optimization_barrier(v.astype(jnp.bfloat16)).astype(jnp.float32)

@jax.custom_vjp
def low_back(v):
    return v

def low_keep(v):
    return (low(v), None)

def low_pass(kept, grad):
    return (grad,)

def back_keep(v):
    return (v, None)

def back_low(kept, grad):
    return (low(grad),)
low.defvjp(low_keep, low_pass)
low_back.defvjp(back_keep, back_low)
rope_base = 10000.0
norm_eps = 1e-05
masked_score = -1e+30
highest_precision = lax.Precision.HIGHEST

def normalize_rows(values):
    centre = values - lax.optimization_barrier(jnp.mean(values, axis=-1, keepdims=True))
    spread = lax.optimization_barrier(jnp.mean(centre * centre, axis=-1, keepdims=True))
    return centre * lax.rsqrt(spread + norm_eps)

def group_layout(row_lengths):
    local_index = jnp.arange(GROUP_LEN, dtype=jnp.int32)
    after_prompt = local_index - PROMPT
    seg_ends = jnp.cumsum(row_lengths).astype(jnp.int32)
    in_prompt = local_index < PROMPT
    counted = lax.optimization_barrier(jnp.sum((after_prompt[:, None] >= seg_ends[None, :]).astype(jnp.int32), axis=1)).astype(jnp.int32)
    segment = jnp.where(in_prompt, 0, 1 + counted).astype(jnp.int32)
    seg_starts = (seg_ends - row_lengths).astype(jnp.int32)
    picked = (segment - 1)[:, None] == jnp.arange(CONT, dtype=jnp.int32)[None, :]
    seg_start = lax.optimization_barrier(jnp.sum(jnp.where(picked, seg_starts[None, :], 0), axis=1)).astype(jnp.int32)
    position = jnp.where(in_prompt, local_index, PROMPT + after_prompt - seg_start).astype(jnp.int32)
    return (segment, position)

def rotation_angles(position):
    half_size = HEAD // 2
    frequency = jnp.exp(-math.log(rope_base) * (2.0 * jnp.arange(half_size, dtype=jnp.float32) / HEAD))
    angles = position.astype(jnp.float32)[:, None] * frequency[None, :]
    return (jnp.cos(angles)[:, None, :], jnp.sin(angles)[:, None, :])

def rotate(values, cosine, sine):
    half_size = values.shape[-1] // 2
    first_half = values[..., :half_size]
    second_half = values[..., half_size:]
    return jnp.concatenate([first_half * cosine - second_half * sine, second_half * cosine + first_half * sine], axis=-1)

def attention(queries, key_rows, value_rows, segment):
    block_rows = min(512, GROUP_LEN)
    block_count = GROUP_LEN // block_rows
    key_index = jnp.arange(GROUP_LEN, dtype=jnp.int32)
    score_scale = HEAD ** (-0.5)

    def one_block(block_id):
        start_row = (block_id * block_rows).astype(jnp.int32)
        query_block = lax.dynamic_slice_in_dim(queries, start_row, block_rows, 0)
        query_segment = lax.dynamic_slice_in_dim(segment, start_row, block_rows, 0)
        query_index = start_row + jnp.arange(block_rows, dtype=jnp.int32)
        scores = low_back(jnp.einsum('qhd,khd->hqk', query_block, key_rows, precision=highest_precision) * score_scale)
        allowed = (key_index[None, :] <= query_index[:, None]) & ((segment[None, :] == 0) | (segment[None, :] == query_segment[:, None]))
        scores = jnp.where(allowed[None], scores, masked_score)
        top_rows = lax.optimization_barrier(jnp.max(scores, axis=-1, keepdims=True))
        exponent = jnp.exp(scores - top_rows)
        probs = exponent / lax.optimization_barrier(jnp.sum(exponent, axis=-1, keepdims=True))
        return jnp.einsum('hqk,khd->qhd', low(probs), value_rows, precision=highest_precision)
    blocks = lax.map(jax.checkpoint(one_block), jnp.arange(block_count, dtype=jnp.int32))
    return blocks.reshape(GROUP_LEN, HEADS, HEAD)

def group_forward(group_inputs, row_lengths, query_key_value_weight, out_weight, gate_weight, up_weight, down_weight):
    segment, position = group_layout(row_lengths)
    cosine, sine = rotation_angles(position)
    first_normed_input = low(normalize_rows(group_inputs))
    raw_projection_output = low_back(jnp.einsum('cu,ufk->cfk', first_normed_input, query_key_value_weight, precision=highest_precision))
    raw_projection_output = raw_projection_output.reshape(GROUP_LEN, 3, HEADS, HEAD)
    queries = low(rotate(raw_projection_output[:, 0], cosine, sine))
    key_rows = low(rotate(raw_projection_output[:, 1], cosine, sine))
    value_rows = low(raw_projection_output[:, 2])
    attended = low(low_back(attention(queries, key_rows, value_rows, segment).reshape(GROUP_LEN, D)))
    middle = group_inputs + low_back(jnp.dot(attended, out_weight, precision=highest_precision))
    normed_two = low(normalize_rows(middle))
    gate = low_back(jnp.dot(normed_two, gate_weight, precision=highest_precision))
    up_proj = low_back(jnp.dot(normed_two, up_weight, precision=highest_precision))
    hidden = low(jax.nn.silu(gate) * up_proj)
    return middle + low_back(jnp.dot(hidden, down_weight, precision=highest_precision))

def to_groups(values):
    span = GROUP_LEN // TOK_DEV
    return values.reshape(span, GROUPS, TOK_DEV, D).transpose(1, 0, 2, 3).reshape(GROUPS, GROUP_LEN, D)

def from_groups(values):
    span = GROUP_LEN // TOK_DEV
    return values.reshape(GROUPS, span, TOK_DEV, D).transpose(1, 0, 2, 3).reshape(TOKENS, D)

def reference(inputs, cotangent, lengths, query_key_value_weight, out_weight, gate_weight, up_weight, down_weight):
    weight_list = tuple((weight.astype(jnp.float32) for weight in (query_key_value_weight, out_weight, gate_weight, up_weight, down_weight)))
    grouped = to_groups(inputs.astype(jnp.float32))

    def forward(group_rows, qkv_w, out_w, gate_w, up_w, down_w):

        def group_step(carried, group_item):
            return (carried, group_forward(group_item[0], group_item[1], qkv_w, out_w, gate_w, up_w, down_w))
        _, stacked = lax.scan(group_step, None, (group_rows, lengths))
        return stacked
    result, pullback = jax.vjp(forward, grouped, *weight_list)
    gradients = pullback(to_groups(cotangent.astype(jnp.float32)))
    output = from_groups(result).astype(jnp.bfloat16)
    return (output, from_groups(gradients[0]), gradients[1], gradients[2], gradients[3], gradients[4], gradients[5])
```

```python
import functools
import math

import jax
import jax.numpy as jnp
from jax import lax
from jax.experimental import pallas as pl
from jax.experimental.pallas import tpu as pltpu
from jax.sharding import PartitionSpec as P

HEAD = 128
PROMPT = 2048
GROUP_LEN = 4096


rope_base = 10000.0
norm_eps = 1e-05
masked_score = -1e30


def passed_along(shard, axis, by):
    size = lax.axis_size(axis)
    pairs = [(i, i + by) for i in range(size) if 0 <= i + by < size]
    return lax.ppermute(shard, axis, pairs)


def normalize_rows(values):
    centre = values - jnp.mean(values, axis=-1, keepdims=True)
    spread = jnp.mean(centre * centre, axis=-1, keepdims=True)
    inverse = lax.rsqrt(spread + norm_eps)
    return (centre * inverse, inverse)


def normalize_back(grad_rows, sum_grad, sum_cross, unit_rows, inverse, row_width):
    return inverse * (grad_rows - sum_grad / row_width - unit_rows * (sum_cross / row_width))


def spread_cols(values, copies):
    return jnp.broadcast_to(values[:, None], (values.shape[0], copies))


def token_layout(lengths, source_row, groups_count, row_count):
    valid_source = source_row >= 0
    safe_source = jnp.maximum(source_row, 0)
    group_id = jnp.where(valid_source, safe_source % groups_count, -1)
    place_here = safe_source // groups_count
    safe_group = jnp.clip(group_id, 0, lengths.shape[0] - 1)
    row_lengths = lax.dynamic_slice_in_dim(lengths, safe_group, 1, 0)[0]
    local_index = place_here * row_count + jnp.arange(row_count, dtype=jnp.int32)
    after_prompt = local_index - PROMPT
    seg_ends = jnp.cumsum(row_lengths)
    in_prompt = local_index < PROMPT
    counted = jnp.sum((after_prompt[:, None] >= seg_ends[None, :]).astype(jnp.int32), axis=1)
    segment = jnp.where(in_prompt, 0, 1 + counted)
    seg_starts = seg_ends - row_lengths
    picked = (segment - 1)[:, None] == jnp.arange(row_lengths.shape[0], dtype=jnp.int32)[None, :]
    seg_start = jnp.sum(jnp.where(picked, seg_starts[None, :], 0), axis=1)
    position = jnp.where(in_prompt, local_index, PROMPT + after_prompt - seg_start)
    return (group_id, local_index, segment, position)


def rotation_angles(position, head_size):
    half_size = head_size // 2
    frequency = jnp.exp(
        -math.log(rope_base) * (2.0 * jnp.arange(half_size, dtype=jnp.float32) / head_size)
    )
    angles = position.astype(jnp.float32)[:, None] * frequency[None, :]
    return (jnp.cos(angles)[:, None, :], jnp.sin(angles)[:, None, :])


def rotate(values, cosine, sine, inverse_turn):
    half_size = values.shape[-1] // 2
    first_half = values[..., :half_size]
    second_half = values[..., half_size:]
    if inverse_turn:
        sine = -sine
    return jnp.concatenate(
        [first_half * cosine - second_half * sine, second_half * cosine + first_half * sine],
        axis=-1,
    )


def visible_mask(query_meta, key_meta):
    query_group, query_index, query_segment, query_position = query_meta
    key_group, key_index, key_segment, key_position = key_meta
    causal = key_index[None, :] <= query_index[:, None]
    shared = (key_segment[None, :] == 0) | (key_segment[None, :] == query_segment[:, None])
    return (query_group == key_group) & causal & shared


def score_block(queries, key_part, allowed, score_scale):
    raw_scores = (
        jnp.einsum("qhd,khd->hqk", queries, key_part, preferred_element_type=jnp.float32)
        * score_scale
    )
    return jnp.where(allowed[None], raw_scores, masked_score)


BLOCK = 512
log2e = 1.4426950408889634


def swap_col(shard, by):
    size = lax.axis_size("col")
    return lax.ppermute(shard, "col", [(i, i ^ by) for i in range(size)])


def swap_place(shard, by, groups_here):
    size = lax.axis_size("row")
    pairs = [(i, (i // groups_here ^ by) * groups_here + i % groups_here) for i in range(size)]
    return lax.ppermute(shard, "row", pairs)


def gather_cols(shard, dim):
    count = lax.axis_size("col")
    index = lax.axis_index("col")
    width = shard.shape[dim]
    shape = list(shard.shape)
    shape[dim] = width * count
    full = jnp.zeros(shape, shard.dtype)
    for by in range(count):
        piece = shard if by == 0 else swap_col(shard, by)
        full = lax.dynamic_update_slice_in_dim(full, piece, (index ^ by) * width, dim)
    return full


def scatter_cols(terms, width):
    count = lax.axis_size("col")
    index = lax.axis_index("col")
    total = None
    for by in range(count):
        piece = lax.dynamic_slice_in_dim(terms, (index ^ by) * width, width, 1)
        if by:
            piece = swap_col(piece.astype(jnp.bfloat16), by)
        piece = piece.astype(jnp.float32)
        total = piece if total is None else total + piece
    return total


def sum_cols(values):
    count = lax.axis_size("col")
    total = values
    for by in range(1, count):
        total = total + swap_col(values, by)
    return total


def turn(values, cosine, sine):
    return values * cosine + pltpu.roll(values, values.shape[1] // 2, 1) * sine


def block_mask(key_block, query_block, start_row):
    key_index = key_block * BLOCK + lax.broadcasted_iota(jnp.int32, (BLOCK, BLOCK), 0)
    query_index = query_block * BLOCK + lax.broadcasted_iota(jnp.int32, (BLOCK, BLOCK), 1)
    return (key_index <= query_index) & (key_index >= start_row)


def each_block(block, visit):
    prompt_blocks = PROMPT // BLOCK

    def whole(j, carry):
        visit(j, False)
        return carry

    lax.fori_loop(0, jnp.minimum(block, prompt_blocks), whole, 0)

    @pl.when(block > prompt_blocks)
    def _():
        visit(block - 1, True)

    visit(block, True)


def attend_kernel(q_ref, k_ref, v_ref, start_ref, o_ref, lse_ref, top_ref, total_ref, sum_ref):
    block = pl.program_id(1)
    scale = HEAD**-0.5 * log2e
    top_ref[...] = jnp.full_like(top_ref, masked_score)
    total_ref[...] = jnp.zeros_like(total_ref)
    sum_ref[...] = jnp.zeros_like(sum_ref)
    queries = q_ref[0]
    start_row = start_ref[0]

    def visit(j, masked):
        rows = pl.ds(pl.multiple_of(j * BLOCK, BLOCK), BLOCK)
        scores = scale * lax.dot_general(
            k_ref[0, rows, :], queries, (((1,), (1,)), ((), ())), preferred_element_type=jnp.float32
        )
        if masked:
            scores = jnp.where(block_mask(j, block, start_row), scores, masked_score)
        old_top = top_ref[...]
        new_top = jnp.maximum(old_top, jnp.max(scores, axis=0, keepdims=True))
        shrink = jnp.exp2(old_top - new_top)
        probs = jnp.exp2(scores - new_top)
        if masked:
            probs = jnp.where(scores > 0.5 * masked_score, probs, 0.0)
        total_ref[...] = total_ref[...] * shrink + jnp.sum(probs, axis=0, keepdims=True)
        sum_ref[...] = sum_ref[...] * shrink + lax.dot_general(
            v_ref[0, rows, :],
            probs.astype(jnp.bfloat16),
            (((0,), (0,)), ((), ())),
            preferred_element_type=jnp.float32,
        )
        top_ref[...] = new_top

    each_block(block, visit)
    total = total_ref[...]
    o_ref[0] = (sum_ref[...] / total).T.astype(jnp.bfloat16)
    lse_ref[0, 0] = top_ref[...] + jnp.log2(total)


def attend(queries, keys, values, start_rows):
    heads, length, size = queries.shape
    blocks = length // BLOCK
    whole = pl.BlockSpec((1, length, size), lambda h, i: (h, 0, 0))
    part = pl.BlockSpec((1, BLOCK, size), lambda h, i: (h, i, 0))
    return pl.pallas_call(
        attend_kernel,
        grid=(heads, blocks),
        in_specs=[part, whole, whole, pl.BlockSpec((1, 1, BLOCK), lambda h, i: (i, 0, 0))],
        out_specs=[part, pl.BlockSpec((1, 1, 1, BLOCK), lambda h, i: (h, i, 0, 0))],
        out_shape=[
            jax.ShapeDtypeStruct((heads, length, size), jnp.bfloat16),
            jax.ShapeDtypeStruct((heads, blocks, 1, BLOCK), jnp.float32),
        ],
        scratch_shapes=[
            pltpu.VMEM((1, BLOCK), jnp.float32),
            pltpu.VMEM((1, BLOCK), jnp.float32),
            pltpu.VMEM((size, BLOCK), jnp.float32),
        ],
        compiler_params=pltpu.CompilerParams(vmem_limit_bytes=32 * 2**20),
        cost_estimate=pl.CostEstimate(
            flops=heads * length * length * size * 2, bytes_accessed=heads * length * size * 8,
            transcendentals=heads * length * length // 2,
        ),
        name="attend",
    )(queries, keys, values, start_rows)


def attend_back_kernel(
    q_ref, k_ref, v_ref, do_ref, o_ref, lse_ref, start_ref, cos_ref, sin_ref,
    dq_ref, dk_ref, dv_ref, dq_sum, dk_sum, dv_sum,
):
    block = pl.program_id(1)
    scale = HEAD**-0.5

    @pl.when(block == 0)
    def _():
        dk_sum[...] = jnp.zeros_like(dk_sum)
        dv_sum[...] = jnp.zeros_like(dv_sum)

    dq_sum[...] = jnp.zeros_like(dq_sum)
    queries = q_ref[0]
    d_out = do_ref[0]
    lse = lse_ref[0, 0]
    start_row = start_ref[0]
    delta = jnp.sum(
        (d_out.astype(jnp.float32) * o_ref[0].astype(jnp.float32)).T, axis=0, keepdims=True
    )

    def visit(j, masked):
        rows = pl.ds(pl.multiple_of(j * BLOCK, BLOCK), BLOCK)
        key_part = k_ref[0, rows, :]
        scores = (scale * log2e) * lax.dot_general(
            key_part, queries, (((1,), (1,)), ((), ())), preferred_element_type=jnp.float32
        )
        if masked:
            scores = jnp.where(block_mask(j, block, start_row), scores, masked_score)
        probs = jnp.exp2(scores - lse)
        d_probs = lax.dot_general(
            v_ref[0, rows, :], d_out, (((1,), (1,)), ((), ())), preferred_element_type=jnp.float32
        )
        d_scores = (probs * (d_probs - delta)).astype(jnp.bfloat16)
        dv_sum[rows, :] += jnp.dot(
            probs.astype(jnp.bfloat16), d_out, preferred_element_type=jnp.float32
        )
        dk_sum[rows, :] += jnp.dot(d_scores, queries, preferred_element_type=jnp.float32)
        dq_sum[...] += lax.dot_general(
            key_part, d_scores, (((0,), (0,)), ((), ())), preferred_element_type=jnp.float32
        )

    each_block(block, visit)
    here = pl.ds(pl.multiple_of(block * BLOCK, BLOCK), BLOCK)
    dq_ref[0] = turn(dq_sum[...].T * scale, cos_ref[here, :], sin_ref[here, :]).astype(jnp.bfloat16)

    @pl.when(block == pl.num_programs(1) - 1)
    def _():
        def finish(j, carry):
            rows = pl.ds(pl.multiple_of(j * BLOCK, BLOCK), BLOCK)
            dk_ref[0, rows, :] = turn(
                dk_sum[rows, :] * scale, cos_ref[rows, :], sin_ref[rows, :]
            ).astype(jnp.bfloat16)
            dv_ref[0, rows, :] = dv_sum[rows, :].astype(jnp.bfloat16)
            return carry

        lax.fori_loop(0, dk_sum.shape[0] // BLOCK, finish, 0)


def attend_back(queries, keys, values, d_out, out, lse, start_rows, cosine, sine):
    heads, length, size = queries.shape
    blocks = length // BLOCK
    whole = pl.BlockSpec((1, length, size), lambda h, i: (h, 0, 0))
    part = pl.BlockSpec((1, BLOCK, size), lambda h, i: (h, i, 0))
    table = pl.BlockSpec((length, size), lambda h, i: (0, 0))
    return pl.pallas_call(
        attend_back_kernel,
        grid=(heads, blocks),
        in_specs=[
            part, whole, whole, part, part,
            pl.BlockSpec((1, 1, 1, BLOCK), lambda h, i: (h, i, 0, 0)),
            pl.BlockSpec((1, 1, BLOCK), lambda h, i: (i, 0, 0)),
            table, table,
        ],
        out_specs=[part, whole, whole],
        out_shape=[jax.ShapeDtypeStruct((heads, length, size), jnp.bfloat16)] * 3,
        scratch_shapes=[
            pltpu.VMEM((size, BLOCK), jnp.float32),
            pltpu.VMEM((length, size), jnp.float32),
            pltpu.VMEM((length, size), jnp.float32),
        ],
        compiler_params=pltpu.CompilerParams(vmem_limit_bytes=48 * 2**20),
        cost_estimate=pl.CostEstimate(
            flops=heads * length * length * size * 5, bytes_accessed=heads * length * size * 16,
            transcendentals=heads * length * length // 2,
        ),
        name="attend_back",
    )(queries, keys, values, d_out, out, lse, start_rows, cosine, sine)


def group_tables(lengths, group):
    row_lengths = lax.dynamic_slice_in_dim(lengths, group, 1, 0)[0]
    local_index = jnp.arange(GROUP_LEN, dtype=jnp.int32)
    seg_ends = jnp.cumsum(row_lengths)
    seg_starts = seg_ends - row_lengths
    after_prompt = local_index - PROMPT
    inside = (after_prompt[:, None] >= seg_starts[None, :]) & (
        after_prompt[:, None] < seg_ends[None, :]
    )
    start = jnp.sum(jnp.where(inside, seg_starts[None, :], 0), axis=1)
    in_prompt = local_index < PROMPT
    start_row = jnp.where(in_prompt, 0, PROMPT + start)
    position = jnp.where(in_prompt, local_index, PROMPT + after_prompt - start)
    half = HEAD // 2
    frequency = jnp.exp(
        -math.log(rope_base) * (2.0 * jnp.arange(half, dtype=jnp.float32) / HEAD)
    )
    angles = position.astype(jnp.float32)[:, None] * frequency[None, :]
    cosine, sine = jnp.cos(angles), jnp.sin(angles)
    return (
        start_row.reshape(GROUP_LEN // BLOCK, 1, BLOCK),
        jnp.concatenate([cosine, cosine], axis=1),
        jnp.concatenate([sine, -sine], axis=1),
    )


def to_heads(rows, span, place, groups_here):
    heads, kinds, tokens, size = rows.shape
    mine = heads // span
    full = jnp.zeros((mine, kinds, span * tokens, size), rows.dtype)
    for by in range(span):
        piece = lax.dynamic_slice_in_dim(rows, (place ^ by) * mine, mine, 0)
        if by:
            piece = swap_place(piece, by, groups_here)
        full = lax.dynamic_update_slice_in_dim(full, piece, (place ^ by) * tokens, 2)
    return full


def to_tokens(rows, span, place, groups_here):
    mine, kinds, length, size = rows.shape
    tokens = length // span
    full = jnp.zeros((mine * span, kinds, tokens, size), rows.dtype)
    for by in range(span):
        piece = lax.dynamic_slice_in_dim(rows, (place ^ by) * tokens, tokens, 2)
        if by:
            piece = swap_place(piece, by, groups_here)
        full = lax.dynamic_update_slice_in_dim(full, piece, (place ^ by) * mine, 0)
    return full


def fast_body(
    inputs,
    cotangent,
    lengths,
    query_key_value_weight,
    out_weight,
    gate_weight,
    up_weight,
    down_weight,
):
    tok_rows, part_width = inputs.shape
    col_count = lax.axis_size("col")
    col_index = lax.axis_index("col")
    row_index = lax.axis_index("row")
    full_width = float(part_width * col_count)
    span = GROUP_LEN // tok_rows
    groups_here = lax.axis_size("row") // span
    heads_here = part_width // HEAD
    place = row_index // groups_here
    group = row_index % groups_here

    def own_cols(values):
        return lax.dynamic_slice_in_dim(values, col_index * part_width, part_width, 1)

    projection = lax.all_gather(query_key_value_weight, "row", axis=0, tiled=True)
    out_rows = lax.all_gather(out_weight, "row", axis=1, tiled=True)
    gate_full = lax.all_gather(gate_weight, "row", axis=0, tiled=True)
    up_full = lax.all_gather(up_weight, "row", axis=0, tiled=True)
    down_full = lax.all_gather(down_weight, "row", axis=1, tiled=True)

    full_inputs = gather_cols(inputs, 1)
    full_cotangent = gather_cols(cotangent, 1)
    out_full = gather_cols(out_rows, 0)

    start_rows, cosine, sine = group_tables(lengths, group)
    own_cos = lax.dynamic_slice_in_dim(cosine, place * tok_rows, tok_rows, 0)[:, : HEAD // 2]
    own_sin = lax.dynamic_slice_in_dim(sine, place * tok_rows, tok_rows, 0)[:, : HEAD // 2]

    unit_one, inverse_one = normalize_rows(full_inputs.astype(jnp.float32))
    normed_one = unit_one.astype(jnp.bfloat16)
    raw = jnp.einsum(
        "cu,ufk->cfk", normed_one, projection, preferred_element_type=jnp.float32
    ).reshape(tok_rows, 3, heads_here, HEAD)
    own_cos, own_sin = own_cos[:, None, :], own_sin[:, None, :]
    sent = jnp.stack(
        [
            rotate(raw[:, 0], own_cos, own_sin, False),
            rotate(raw[:, 1], own_cos, own_sin, False),
            raw[:, 2],
        ],
        axis=0,
    ).astype(jnp.bfloat16)
    sent = sent.transpose(2, 0, 1, 3)
    held = to_heads(sent, span, place, groups_here)
    queries, keys, values = held[:, 0], held[:, 1], held[:, 2]
    attended_head, lse = attend(queries, keys, values, start_rows)
    attended = to_tokens(attended_head[:, None], span, place, groups_here)[:, 0]
    attended = attended.transpose(1, 0, 2).reshape(tok_rows, part_width)
    attended_full = gather_cols(attended, 1)
    middle_full = full_inputs.astype(jnp.float32) + jnp.dot(
        attended_full, out_full, preferred_element_type=jnp.float32
    )
    middle = own_cols(middle_full)
    unit_two, inverse_two = normalize_rows(middle_full)
    normed_two = unit_two.astype(jnp.bfloat16)

    gate = jnp.dot(normed_two, gate_full, preferred_element_type=jnp.float32)
    up_proj = jnp.dot(normed_two, up_full, preferred_element_type=jnp.float32)
    sigmoid_gate = jax.nn.sigmoid(gate)
    silu_gate = gate * sigmoid_gate
    hidden = (silu_gate * up_proj).astype(jnp.bfloat16)
    d_hidden = jnp.einsum(
        "td,fd->tf", full_cotangent, down_full, preferred_element_type=jnp.float32
    )
    d_gate = (d_hidden * up_proj * sigmoid_gate * (1.0 + gate * (1.0 - sigmoid_gate))).astype(
        jnp.bfloat16
    )
    d_up = (d_hidden * silu_gate).astype(jnp.bfloat16)
    d_normed_two = jnp.einsum(
        "tf,df->td", d_gate, gate_full, preferred_element_type=jnp.float32
    ) + jnp.einsum("tf,df->td", d_up, up_full, preferred_element_type=jnp.float32)
    grad_two = scatter_cols(d_normed_two, part_width)
    stats_two = sum_cols(
        jnp.stack([jnp.sum(d_normed_two, axis=1), jnp.sum(d_normed_two * unit_two, axis=1)])
    )
    ffn_terms = jnp.dot(hidden, down_full, preferred_element_type=jnp.float32)
    output = (middle + scatter_cols(ffn_terms, part_width)).astype(jnp.bfloat16)

    down_part = jnp.einsum("tf,td->fd", hidden, full_cotangent, preferred_element_type=jnp.float32)
    gate_part = jnp.einsum("td,tf->df", normed_two, d_gate, preferred_element_type=jnp.float32)
    up_part = jnp.einsum("td,tf->df", normed_two, d_up, preferred_element_type=jnp.float32)

    d_middle = cotangent.astype(jnp.float32) + normalize_back(
        grad_two, stats_two[0][:, None], stats_two[1][:, None], own_cols(unit_two), inverse_two, full_width
    )
    d_branch_full = gather_cols(d_middle.astype(jnp.bfloat16), 1)
    out_part = jnp.einsum("tc,td->cd", attended, d_branch_full, preferred_element_type=jnp.float32)
    d_attended = jnp.einsum(
        "td,cd->tc", d_branch_full, out_rows, preferred_element_type=jnp.float32
    ).astype(jnp.bfloat16)
    d_attended = d_attended.reshape(tok_rows, heads_here, HEAD).transpose(1, 0, 2)
    d_head = to_heads(d_attended[:, None], span, place, groups_here)[:, 0]
    d_queries, d_keys, d_values = attend_back(
        queries, keys, values, d_head, attended_head, lse, start_rows, cosine, sine
    )
    d_raw = to_tokens(
        jnp.stack([d_queries, d_keys, d_values], axis=1), span, place, groups_here
    )
    d_raw = d_raw.transpose(2, 1, 0, 3).reshape(tok_rows, 3, part_width)
    projection_part = jnp.einsum(
        "lo,lbw->obw", normed_one, d_raw, preferred_element_type=jnp.float32
    )
    d_normed_one = jnp.einsum(
        "xzq,vzq->xv", d_raw, projection, preferred_element_type=jnp.float32
    )
    grad_one = scatter_cols(d_normed_one, part_width)
    stats_one = sum_cols(
        jnp.stack([jnp.sum(d_normed_one, axis=1), jnp.sum(d_normed_one * unit_one, axis=1)])
    )
    input_grad = d_middle + normalize_back(
        grad_one, stats_one[0][:, None], stats_one[1][:, None], own_cols(unit_one), inverse_one, full_width
    )

    def owned(part, dim):
        return lax.psum_scatter(
            part.astype(jnp.bfloat16), "row", scatter_dimension=dim, tiled=True
        ).astype(jnp.float32)

    return (
        output,
        input_grad,
        owned(projection_part, 0),
        owned(out_part, 1),
        owned(gate_part, 0),
        owned(up_part, 0),
        owned(down_part, 1),
    )


def body(
    inputs,
    cotangent,
    lengths,
    query_key_value_weight,
    out_weight,
    gate_weight,
    up_weight,
    down_weight,
):
    tok_rows = inputs.shape[0]
    part_width = inputs.shape[1]
    col_count = lax.axis_size("col")
    col_index = lax.axis_index("col")
    row_index = lax.axis_index("row")
    full_width = float(part_width * col_count)
    group_span = GROUP_LEN // tok_rows
    groups_here = lax.axis_size("row") // group_span
    head_size = HEAD
    heads_here = part_width // head_size
    score_scale = head_size ** (-0.5)
    block_place = row_index // groups_here
    full_inputs, full_cotangent = (
        lax.all_gather(inputs, "col", axis=1, tiled=True),
        lax.all_gather(cotangent, "col", axis=1, tiled=True),
    )
    projection_full_rows, out_full, gate_full, up_full, down_full = (
        lax.all_gather(query_key_value_weight, "row", axis=0, tiled=True),
        lax.all_gather(out_weight, "row", axis=1, tiled=True),
        lax.all_gather(gate_weight, "row", axis=0, tiled=True),
        lax.all_gather(up_weight, "row", axis=0, tiled=True),
        lax.all_gather(down_weight, "row", axis=1, tiled=True),
    )
    unit_one, inverse_one = normalize_rows(full_inputs.astype(jnp.float32))
    first_normed_input = unit_one.astype(jnp.bfloat16)
    raw_projection_output = jnp.einsum(
        "cu,ufk->cfk", first_normed_input, projection_full_rows, preferred_element_type=jnp.float32
    )
    raw_projection_output = raw_projection_output.reshape(tok_rows, 3, heads_here, head_size)
    own_meta = token_layout(lengths, row_index, groups_here, tok_rows)
    cosine, sine = rotation_angles(own_meta[3], head_size)
    queries = rotate(raw_projection_output[:, 0], cosine, sine, False).astype(jnp.bfloat16)
    key_rows = rotate(raw_projection_output[:, 1], cosine, sine, False).astype(jnp.bfloat16)
    value_rows = raw_projection_output[:, 2].astype(jnp.bfloat16)
    pieces = [(key_rows, value_rows)]
    for shift_by in range(1, group_span):
        pieces.append(passed_along((key_rows, value_rows), "row", shift_by * groups_here))
    visibility = [
        visible_mask(
            own_meta,
            token_layout(lengths, row_index - shift_by * groups_here, groups_here, tok_rows),
        )
        for shift_by in range(group_span)
    ]
    live_piece = [shift_by <= block_place for shift_by in range(group_span)]
    first_scores = score_block(queries, pieces[0][0], visibility[0], score_scale)
    top_rows = jnp.max(first_scores, axis=-1, keepdims=True)
    total_rows = jnp.sum(jnp.exp(first_scores - top_rows), axis=-1, keepdims=True)
    for shift_by in range(1, group_span):

        def add_stats(carry, shift_by=shift_by):
            old_top, old_total = carry
            scores = score_block(queries, pieces[shift_by][0], visibility[shift_by], score_scale)
            new_top = jnp.maximum(old_top, jnp.max(scores, axis=-1, keepdims=True))
            new_total = old_total * jnp.exp(old_top - new_top) + jnp.sum(
                jnp.exp(scores - new_top), axis=-1, keepdims=True
            )
            return (new_top, new_total)

        top_rows, total_rows = lax.cond(
            live_piece[shift_by], add_stats, lambda carry: carry, (top_rows, total_rows)
        )
    log_total = top_rows + jnp.log(total_rows)
    attended = jnp.zeros((tok_rows, heads_here, head_size), jnp.float32)
    for shift_by in range(group_span):

        def add_values(total, shift_by=shift_by):
            scores = score_block(queries, pieces[shift_by][0], visibility[shift_by], score_scale)
            probs_low = jnp.exp(scores - log_total).astype(jnp.bfloat16)
            return total + jnp.einsum(
                "hqk,khd->qhd", probs_low, pieces[shift_by][1], preferred_element_type=jnp.float32
            )

        attended = lax.cond(live_piece[shift_by], add_values, lambda total: total, attended)
    attended_flat = attended.reshape(tok_rows, part_width).astype(jnp.bfloat16)
    branch_terms = jnp.dot(attended_flat, out_full, preferred_element_type=jnp.float32)
    branch_full = lax.psum(branch_terms, "col")
    middle_full = full_inputs.astype(jnp.float32) + branch_full
    middle = lax.dynamic_slice_in_dim(middle_full, col_index * part_width, part_width, 1)
    unit_two, inverse_two = normalize_rows(middle_full)
    normed_two = unit_two.astype(jnp.bfloat16)
    gate = jnp.dot(normed_two, gate_full, preferred_element_type=jnp.float32)
    up_proj = jnp.dot(normed_two, up_full, preferred_element_type=jnp.float32)
    sigmoid_gate = jax.nn.sigmoid(gate)
    silu_gate = gate * sigmoid_gate
    hidden = (silu_gate * up_proj).astype(jnp.bfloat16)
    ffn_terms = jnp.dot(hidden, down_full, preferred_element_type=jnp.float32)
    ffn_part = lax.psum_scatter(
        ffn_terms.astype(jnp.bfloat16), "col", scatter_dimension=1, tiled=True
    ).astype(jnp.float32)
    output = (middle + ffn_part).astype(jnp.bfloat16)
    projection_full_rows, out_full, gate_full, up_full, down_full = (
        lax.all_gather(query_key_value_weight, "row", axis=0, tiled=True),
        lax.all_gather(out_weight, "row", axis=1, tiled=True),
        lax.all_gather(gate_weight, "row", axis=0, tiled=True),
        lax.all_gather(up_weight, "row", axis=0, tiled=True),
        lax.all_gather(down_weight, "row", axis=1, tiled=True),
    )
    d_hidden = jnp.einsum(
        "td,fd->tf", full_cotangent, down_full, preferred_element_type=jnp.float32
    )
    down_part = jnp.einsum("tf,td->fd", hidden, full_cotangent, preferred_element_type=jnp.float32)
    d_gate = (d_hidden * up_proj * sigmoid_gate * (1.0 + gate * (1.0 - sigmoid_gate))).astype(
        jnp.bfloat16
    )
    d_up = (d_hidden * silu_gate).astype(jnp.bfloat16)
    gate_part = jnp.einsum("td,tf->df", normed_two, d_gate, preferred_element_type=jnp.float32)
    up_part = jnp.einsum("td,tf->df", normed_two, d_up, preferred_element_type=jnp.float32)
    d_normed_two = jnp.einsum(
        "tf,df->td", d_gate, gate_full, preferred_element_type=jnp.float32
    ) + jnp.einsum("tf,df->td", d_up, up_full, preferred_element_type=jnp.float32)
    grad_two, sum_two, cross_two = (
        lax.psum_scatter(
            d_normed_two.astype(jnp.bfloat16), "col", scatter_dimension=1, tiled=True
        ).astype(jnp.float32),
        lax.psum_scatter(
            spread_cols(jnp.sum(d_normed_two, axis=1), col_count).astype(jnp.bfloat16),
            "col",
            scatter_dimension=1,
            tiled=True,
        ).astype(jnp.float32),
        lax.psum_scatter(
            spread_cols(jnp.sum(d_normed_two * unit_two, axis=1), col_count).astype(jnp.bfloat16),
            "col",
            scatter_dimension=1,
            tiled=True,
        ).astype(jnp.float32),
    )
    unit_two_here = lax.dynamic_slice_in_dim(unit_two, col_index * part_width, part_width, 1)
    d_middle = cotangent.astype(jnp.float32) + normalize_back(
        grad_two, sum_two, cross_two, unit_two_here, inverse_two, full_width
    )
    d_branch = d_middle.astype(jnp.bfloat16)
    d_branch_full = lax.all_gather(d_branch, "col", axis=1, tiled=True)
    out_part = jnp.einsum(
        "tc,td->cd", attended_flat, d_branch_full, preferred_element_type=jnp.float32
    )
    d_attended = jnp.einsum(
        "td,cd->tc", d_branch_full, out_full, preferred_element_type=jnp.float32
    )
    d_attended = d_attended.astype(jnp.bfloat16).reshape(tok_rows, heads_here, head_size)
    delta_rows = jnp.zeros((heads_here, tok_rows, 1), jnp.float32)
    for shift_by in range(group_span):

        def add_delta(total, shift_by=shift_by):
            scores = score_block(queries, pieces[shift_by][0], visibility[shift_by], score_scale)
            probs_full = jnp.exp(scores - log_total)
            d_probs = jnp.einsum(
                "qhd,khd->hqk", d_attended, pieces[shift_by][1], preferred_element_type=jnp.float32
            )
            return total + jnp.sum(probs_full * d_probs, axis=-1, keepdims=True)

        delta_rows = lax.cond(live_piece[shift_by], add_delta, lambda total: total, delta_rows)
    zero_rows = jnp.zeros((tok_rows, heads_here, head_size), jnp.float32)
    d_queries = zero_rows
    for shift_by in range(group_span):

        def piece_grads(query_total, shift_by=shift_by):
            key_part, value_part = pieces[shift_by]
            scores = score_block(queries, key_part, visibility[shift_by], score_scale)
            probs_full = jnp.exp(scores - log_total)
            d_probs = jnp.einsum(
                "qhd,khd->hqk", d_attended, value_part, preferred_element_type=jnp.float32
            )
            d_scores = (probs_full * (d_probs - delta_rows)).astype(jnp.bfloat16)
            query_total = (
                query_total
                + jnp.einsum("hqk,khd->qhd", d_scores, key_part, preferred_element_type=jnp.float32)
                * score_scale
            )
            d_key_part = (
                jnp.einsum("hqk,qhd->khd", d_scores, queries, preferred_element_type=jnp.float32)
                * score_scale
            )
            d_value_part = jnp.einsum(
                "hqk,qhd->khd",
                probs_full.astype(jnp.bfloat16),
                d_attended,
                preferred_element_type=jnp.float32,
            )
            return (query_total, d_key_part, d_value_part)

        d_queries, d_key_part, d_value_part = lax.cond(
            live_piece[shift_by],
            piece_grads,
            lambda query_total: (query_total, zero_rows, zero_rows),
            d_queries,
        )
        if shift_by == 0:
            d_keys = d_key_part
            d_values = d_value_part
        else:
            back_keys, back_values = (
                passed_along(
                    d_key_part.astype(jnp.bfloat16), "row", -shift_by * groups_here
                ).astype(d_key_part.dtype),
                passed_along(
                    d_value_part.astype(jnp.bfloat16), "row", -shift_by * groups_here
                ).astype(d_value_part.dtype),
            )
            d_keys = d_keys + back_keys
            d_values = d_values + back_values
    raw_score_gradient = jnp.stack(
        [rotate(d_queries, cosine, sine, True), rotate(d_keys, cosine, sine, True), d_values],
        axis=1,
    )
    raw_score_gradient = raw_score_gradient.reshape(tok_rows, 3, part_width).astype(jnp.bfloat16)
    projection_part_rows = jnp.einsum(
        "lo,lbw->obw", first_normed_input, raw_score_gradient, preferred_element_type=jnp.float32
    )
    first_normed_gradient = jnp.einsum(
        "xzq,vzq->xv", raw_score_gradient, projection_full_rows, preferred_element_type=jnp.float32
    )
    grad_one, sum_one, cross_one = (
        lax.psum_scatter(
            first_normed_gradient.astype(jnp.bfloat16), "col", scatter_dimension=1, tiled=True
        ).astype(jnp.float32),
        lax.psum_scatter(
            spread_cols(jnp.sum(first_normed_gradient, axis=1), col_count).astype(jnp.bfloat16),
            "col",
            scatter_dimension=1,
            tiled=True,
        ).astype(jnp.float32),
        lax.psum_scatter(
            spread_cols(jnp.sum(first_normed_gradient * unit_one, axis=1), col_count).astype(
                jnp.bfloat16
            ),
            "col",
            scatter_dimension=1,
            tiled=True,
        ).astype(jnp.float32),
    )
    unit_one_here = lax.dynamic_slice_in_dim(unit_one, col_index * part_width, part_width, 1)
    input_grad = d_middle + normalize_back(
        grad_one, sum_one, cross_one, unit_one_here, inverse_one, full_width
    )
    owned_grads = (
        lax.psum_scatter(
            projection_part_rows.astype(jnp.bfloat16), "row", scatter_dimension=0, tiled=True
        ).astype(jnp.float32),
        lax.psum_scatter(
            out_part.astype(jnp.bfloat16), "row", scatter_dimension=1, tiled=True
        ).astype(jnp.float32),
        lax.psum_scatter(
            gate_part.astype(jnp.bfloat16), "row", scatter_dimension=0, tiled=True
        ).astype(jnp.float32),
        lax.psum_scatter(
            up_part.astype(jnp.bfloat16), "row", scatter_dimension=0, tiled=True
        ).astype(jnp.float32),
        lax.psum_scatter(
            down_part.astype(jnp.bfloat16), "row", scatter_dimension=1, tiled=True
        ).astype(jnp.float32),
    )
    return (
        output,
        input_grad,
        owned_grads[0],
        owned_grads[1],
        owned_grads[2],
        owned_grads[3],
        owned_grads[4],
    )


def step(inputs, *rest):
    span = GROUP_LEN // inputs.shape[0]
    heads_here = inputs.shape[1] // HEAD
    return (body if heads_here % span else fast_body)(inputs, *rest)


def solution(mesh):
    placed = (
        P("row", "col"),
        P("row", "col"),
        P(),
        P("row", None, "col"),
        P("col", "row"),
        P("row", "col"),
        P("row", "col"),
        P("col", "row"),
    )
    return jax.shard_map(
        step,
        mesh=mesh,
        in_specs=placed,
        out_specs=(
            P("row", "col"),
            P("row", "col"),
            P("row", None, "col"),
            P("col", "row"),
            P("row", "col"),
            P("row", "col"),
            P("col", "row"),
        ),
        check_vma=False,
    )
```

```python
import functools
import math

import jax
import jax.numpy as jnp
from jax import lax
from jax.experimental import pallas as pl
from jax.experimental.pallas import tpu as pltpu
from jax.sharding import PartitionSpec as P

HEAD = 128
PROMPT = 2048
GROUP_LEN = 4096


rope_base = 10000.0
norm_eps = 1e-05
masked_score = -1e30


def passed_along(shard, axis, by):
    size = lax.axis_size(axis)
    pairs = [(i, i + by) for i in range(size) if 0 <= i + by < size]
    return lax.ppermute(shard, axis, pairs)


def normalize_rows(values):
    centre = values - jnp.mean(values, axis=-1, keepdims=True)
    spread = jnp.mean(centre * centre, axis=-1, keepdims=True)
    inverse = lax.rsqrt(spread + norm_eps)
    return (centre * inverse, inverse)


def normalize_back(grad_rows, sum_grad, sum_cross, unit_rows, inverse, row_width):
    return inverse * (grad_rows - sum_grad / row_width - unit_rows * (sum_cross / row_width))


def spread_cols(values, copies):
    return jnp.broadcast_to(values[:, None], (values.shape[0], copies))


def token_layout(lengths, source_row, groups_count, row_count):
    valid_source = source_row >= 0
    safe_source = jnp.maximum(source_row, 0)
    group_id = jnp.where(valid_source, safe_source % groups_count, -1)
    place_here = safe_source // groups_count
    safe_group = jnp.clip(group_id, 0, lengths.shape[0] - 1)
    row_lengths = lax.dynamic_slice_in_dim(lengths, safe_group, 1, 0)[0]
    local_index = place_here * row_count + jnp.arange(row_count, dtype=jnp.int32)
    after_prompt = local_index - PROMPT
    seg_ends = jnp.cumsum(row_lengths)
    in_prompt = local_index < PROMPT
    counted = jnp.sum((after_prompt[:, None] >= seg_ends[None, :]).astype(jnp.int32), axis=1)
    segment = jnp.where(in_prompt, 0, 1 + counted)
    seg_starts = seg_ends - row_lengths
    picked = (segment - 1)[:, None] == jnp.arange(row_lengths.shape[0], dtype=jnp.int32)[None, :]
    seg_start = jnp.sum(jnp.where(picked, seg_starts[None, :], 0), axis=1)
    position = jnp.where(in_prompt, local_index, PROMPT + after_prompt - seg_start)
    return (group_id, local_index, segment, position)


def rotation_angles(position, head_size):
    half_size = head_size // 2
    frequency = jnp.exp(
        -math.log(rope_base) * (2.0 * jnp.arange(half_size, dtype=jnp.float32) / head_size)
    )
    angles = position.astype(jnp.float32)[:, None] * frequency[None, :]
    return (jnp.cos(angles)[:, None, :], jnp.sin(angles)[:, None, :])


def rotate(values, cosine, sine, inverse_turn):
    half_size = values.shape[-1] // 2
    first_half = values[..., :half_size]
    second_half = values[..., half_size:]
    if inverse_turn:
        sine = -sine
    return jnp.concatenate(
        [first_half * cosine - second_half * sine, second_half * cosine + first_half * sine],
        axis=-1,
    )


def visible_mask(query_meta, key_meta):
    query_group, query_index, query_segment, query_position = query_meta
    key_group, key_index, key_segment, key_position = key_meta
    causal = key_index[None, :] <= query_index[:, None]
    shared = (key_segment[None, :] == 0) | (key_segment[None, :] == query_segment[:, None])
    return (query_group == key_group) & causal & shared


def score_block(queries, key_part, allowed, score_scale):
    raw_scores = (
        jnp.einsum("qhd,khd->hqk", queries, key_part, preferred_element_type=jnp.float32)
        * score_scale
    )
    return jnp.where(allowed[None], raw_scores, masked_score)


BLOCK = 512
log2e = 1.4426950408889634


def turn(values, cosine, sine):
    return values * cosine + pltpu.roll(values, values.shape[1] // 2, 1) * sine


def block_mask(key_block, query_block, start_row):
    key_index = key_block * BLOCK + lax.broadcasted_iota(jnp.int32, (BLOCK, BLOCK), 0)
    query_index = query_block * BLOCK + lax.broadcasted_iota(jnp.int32, (BLOCK, BLOCK), 1)
    return (key_index <= query_index) & (key_index >= start_row)


def each_block(block, visit):
    prompt_blocks = PROMPT // BLOCK

    def whole(j, carry):
        visit(j, False)
        return carry

    lax.fori_loop(0, jnp.minimum(block, prompt_blocks), whole, 0)

    @pl.when(block > prompt_blocks)
    def _():
        visit(block - 1, True)

    visit(block, True)


MESH = pl.DeviceIdType.MESH


def place_of(place, groups_here):
    row = lax.axis_index("row")
    return (place * groups_here + lax.rem(row, groups_here), lax.axis_index("col"))


def send(source, target, send_sem, recv_sem, device):
    return pltpu.make_async_remote_copy(
        src_ref=source, dst_ref=target, send_sem=send_sem, recv_sem=recv_sem,
        device_id=device, device_id_type=MESH,
    )


def block_rows(block):
    return pl.ds(pl.multiple_of(block * BLOCK, BLOCK), BLOCK)


def col_device(by):
    return (lax.axis_index("row"), lax.axis_index("col") ^ by)


def greet_cols(count):
    barrier = pltpu.get_barrier_semaphore()
    for by in range(1, count):
        pl.semaphore_signal(barrier, inc=1, device_id=col_device(by), device_id_type=MESH)
    pl.semaphore_wait(barrier, count - 1)


class Gather:
    def __init__(self, source, slots, sends, recvs, local):
        me = lax.axis_index("col")
        a, b = source[0], source[1]
        self.own = []
        if local is not None:
            self.own = [
                pltpu.make_async_copy(a, slots(me)[0], local.at[0]),
                pltpu.make_async_copy(b, slots(me)[1], local.at[1]),
            ]

        def copy(i, what, where, by):
            return send(what, where, sends.at[i], recvs.at[i], col_device(by))

        self.first = [
            copy(0, a, slots(me)[0], 1),
            copy(3, b, slots(me)[1], 2),
            copy(1, b, slots(me)[1], 1),
            copy(2, a, slots(me)[0], 2),
        ]
        across, along = me ^ 1, me ^ 2
        self.second = [
            copy(4, slots(across)[0], slots(across)[0], 2),
            copy(5, slots(along)[1], slots(along)[1], 1),
        ]

    def start(self):
        for one in self.own + self.first:
            one.start()

    def forward(self):
        self.first[0].wait_recv()
        self.second[0].start()
        self.first[1].wait_recv()
        self.second[1].start()

    def receive(self):
        for one in self.first[2:] + self.second:
            one.wait_recv()
        for one in self.own:
            one.wait()

    def finish(self):
        for one in self.first + self.second:
            one.wait_send()


def halves(ref, start, size):
    half = size // 2
    return ref.at[pl.ds(start, half)], ref.at[pl.ds(start + half, half)]


def greet_all(me, span, groups_here, count):
    barrier = pltpu.get_barrier_semaphore()
    for by in range(1, span):
        pl.semaphore_signal(
            barrier, inc=1, device_id=place_of(lax.rem(me + by, span), groups_here), device_id_type=MESH
        )
    for by in range(1, count):
        pl.semaphore_signal(barrier, inc=1, device_id=col_device(by), device_id_type=MESH)
    pl.semaphore_wait(barrier, span + count - 2)


def attend_kernel(
    groups_here, sent_ref, start_ref, rider_ref, back_ref, held_ref, o_ref, lse_ref, riders_ref,
    qkv_ref, top_ref, total_ref, sum_ref,
    in_send, in_recv, out_send, out_recv, keep_sem, own_sem, ride_send, ride_recv, ride_local,
):
    span, _, tokens, _ = sent_ref.shape
    me = lax.axis_index("row") // groups_here
    blocks = start_ref.shape[0]
    per_place = tokens // BLOCK
    scale = HEAD**-0.5 * log2e
    greet_all(me, span, groups_here, riders_ref.shape[0])
    depth = rider_ref.shape[0]
    ride = Gather(
        halves(rider_ref, 0, depth), lambda c: halves(riders_ref.at[c], 0, depth),
        ride_send, ride_recv, ride_local,
    )

    def qkv_copy(by):
        peer = lax.rem(me + by, span)
        return send(
            sent_ref.at[peer], qkv_ref.at[:, pl.ds(pl.multiple_of(me * tokens, tokens), tokens)],
            in_send.at[by], in_recv.at[by], place_of(peer, groups_here),
        )

    own_rows = pl.ds(pl.multiple_of(me * tokens, tokens), tokens)
    own_copy = pltpu.make_async_copy(sent_ref.at[me], qkv_ref.at[:, own_rows], in_recv.at[0])
    own_copy.start()
    for by in range(1, span):
        qkv_copy(by).start()
    ride.start()

    def out_copy(block):
        to = block // per_place
        half = lax.rem(block, per_place)
        by = lax.rem(to - me + span, span)
        return send(
            o_ref.at[block_rows(block)], back_ref.at[me, block_rows(half)],
            out_send.at[block], out_recv.at[by, half], place_of(to, groups_here),
        )

    def own_out(block):
        return pltpu.make_async_copy(
            o_ref.at[block_rows(block)],
            back_ref.at[me, block_rows(lax.rem(block, per_place))],
            own_sem.at[lax.rem(block, per_place)],
        )

    def keep_copy(place):
        rows = pl.ds(pl.multiple_of(place * tokens, tokens), tokens)
        return pltpu.make_async_copy(qkv_ref.at[:, rows], held_ref.at[:, rows], keep_sem.at[place])

    def one_block(block, carry):
        place = block // per_place

        @pl.when(lax.rem(block, per_place) == 0)
        def _():
            @pl.when(place == me)
            def _():
                own_copy.wait()

            for by in range(1, span):

                @pl.when(lax.rem(place + by, span) == me)
                def _():
                    qkv_copy(by).wait_recv()

            keep_copy(place).start()

        top_ref[...] = jnp.full_like(top_ref, masked_score)
        total_ref[...] = jnp.zeros_like(total_ref)
        sum_ref[...] = jnp.zeros_like(sum_ref)
        queries = qkv_ref[0, block_rows(block), :]
        start_row = start_ref[block]

        def visit(j, masked):
            rows = block_rows(j)
            scores = scale * matmul_nt(qkv_ref[1, rows, :], queries)
            if masked:
                scores = jnp.where(block_mask(j, block, start_row), scores, masked_score)
            old_top = top_ref[...]
            new_top = jnp.maximum(old_top, jnp.max(scores, axis=0, keepdims=True))
            shrink = jnp.exp2(old_top - new_top)
            probs = jnp.exp2(scores - new_top)
            if masked:
                probs = jnp.where(scores > 0.5 * masked_score, probs, 0.0)
            total_ref[...] = total_ref[...] * shrink + jnp.sum(probs, axis=0, keepdims=True)
            sum_ref[...] = sum_ref[...] * shrink + lax.dot_general(
                qkv_ref[2, rows, :],
                probs.astype(jnp.bfloat16),
                (((0,), (0,)), ((), ())),
                preferred_element_type=jnp.float32,
            )
            top_ref[...] = new_top

        each_block(block, visit)
        total = total_ref[...]
        o_ref[block_rows(block), :] = (sum_ref[...] / total).T.astype(jnp.bfloat16)
        lse_ref[block] = top_ref[...] + jnp.log2(total)

        @pl.when(place == me)
        def _():
            own_out(block).start()

        @pl.when(place != me)
        def _():
            out_copy(block).start()

        @pl.when(block == blocks // 2)
        def _():
            ride.forward()

        return carry

    lax.fori_loop(0, blocks, one_block, 0)
    ride.receive()
    ride.finish()

    for by in range(1, span):
        qkv_copy(by).wait_send()

    def finish(block, carry):
        place = block // per_place

        @pl.when(place == me)
        def _():
            own_out(block).wait()

        @pl.when(place != me)
        def _():
            out_copy(block).wait_send()

        return carry

    lax.fori_loop(0, blocks, finish, 0)
    for by in range(1, span):
        for half in range(per_place):
            send(
                o_ref.at[block_rows(half)], back_ref.at[lax.rem(me - by + span, span), block_rows(half)],
                out_send.at[half], out_recv.at[by, half], place_of(me, groups_here),
            ).wait_recv()
    for place in range(span):
        keep_copy(place).wait()


def attend(sent, start_rows, rider, groups_here, count):
    span, _, tokens, size = sent.shape
    blocks = start_rows.shape[0]
    length = span * tokens
    hbm = pl.BlockSpec(memory_space=pl.ANY)
    vmem = pl.BlockSpec(memory_space=pltpu.VMEM)
    per_place = tokens // BLOCK
    dma = pltpu.SemaphoreType.DMA
    return pl.pallas_call(
        functools.partial(attend_kernel, groups_here),
        in_specs=[hbm, vmem, hbm],
        out_specs=[hbm, hbm, vmem, vmem, hbm],
        out_shape=[
            jax.ShapeDtypeStruct((span, tokens, size), jnp.bfloat16),
            jax.ShapeDtypeStruct((3, length, size), jnp.bfloat16),
            jax.ShapeDtypeStruct((length, size), jnp.bfloat16),
            jax.ShapeDtypeStruct((blocks, 1, BLOCK), jnp.float32),
            jax.ShapeDtypeStruct((count, *rider.shape), jnp.bfloat16),
        ],
        scratch_shapes=[
            pltpu.VMEM((3, length, size), jnp.bfloat16),
            pltpu.VMEM((1, BLOCK), jnp.float32),
            pltpu.VMEM((1, BLOCK), jnp.float32),
            pltpu.VMEM((size, BLOCK), jnp.float32),
            dma((span,)), dma((span,)), dma((blocks,)), dma((span, per_place)), dma((span,)),
            dma((per_place,)), dma((6,)), dma((6,)), dma((2,)),
        ],
        compiler_params=pltpu.CompilerParams(
            vmem_limit_bytes=32 * 2**20, collective_id=1, has_side_effects=True
        ),
        cost_estimate=pl.CostEstimate(
            flops=length * length * size * 2, bytes_accessed=length * size * 200,
            transcendentals=length * length // 2,
        ),
        name="attend",
    )(sent, start_rows, rider)


def attend_back_kernel(
    groups_here, d_sent_ref, qkv_ref, o_ref, lse_ref, start_ref, cos_ref, sin_ref, rider_ref,
    d_raw_ref, riders_ref, do_ref, stage_ref, dq_sum, dk_sum, dv_sum,
    in_send, in_recv, q_send, q_recv, kv_send, kv_recv, own_sem, ride_send, ride_recv,
):
    span, tokens, _ = d_sent_ref.shape
    me = lax.axis_index("row") // groups_here
    blocks = start_ref.shape[0]
    per_place = tokens // BLOCK
    after = blocks - PROMPT // BLOCK
    scale = HEAD**-0.5
    greet_all(me, span, groups_here, rider_ref.shape[0])
    ride = Scatter(
        rider_ref, riders_ref, None, None, pl.ds(0, tokens), ride_send, ride_recv
    )
    own_rows = pl.ds(pl.multiple_of(me * tokens, tokens), tokens)

    def do_copy(by):
        peer = lax.rem(me + by, span)
        return send(
            d_sent_ref.at[peer], do_ref.at[own_rows], in_send.at[by], in_recv.at[by],
            place_of(peer, groups_here),
        )

    own_copy = pltpu.make_async_copy(d_sent_ref.at[me], do_ref.at[own_rows], in_recv.at[0])
    own_copy.start()
    for by in range(1, span):
        do_copy(by).start()
    ride.start()
    dk_sum[...] = jnp.zeros_like(dk_sum)
    dv_sum[...] = jnp.zeros_like(dv_sum)

    def moved(block, which):
        to = block // per_place
        half = lax.rem(block, per_place)
        by = lax.rem(to - me + span, span)
        kinds = pl.ds(1, 2) if which else pl.ds(0, 1)
        source = stage_ref.at[kinds, block_rows(block)]
        target = d_raw_ref.at[me, kinds, block_rows(half)]
        sends, recvs = (kv_send, kv_recv) if which else (q_send, q_recv)
        return (
            to == me,
            pltpu.make_async_copy(source, target, own_sem.at[which, half]),
            send(source, target, sends.at[block], recvs.at[by, half], place_of(to, groups_here)),
        )

    def start_move(block, which):
        mine, local, remote = moved(block, which)

        @pl.when(mine)
        def _():
            local.start()

        @pl.when(jnp.logical_not(mine))
        def _():
            remote.start()

    def close(j):
        rows = block_rows(j)
        stage_ref[1, rows, :] = turn(
            dk_sum[rows, :] * scale, cos_ref[rows, :], sin_ref[rows, :]
        ).astype(jnp.bfloat16)
        stage_ref[2, rows, :] = dv_sum[rows, :].astype(jnp.bfloat16)
        start_move(j, 1)

    def one_block(n, carry):
        block = jnp.where(n < after, blocks - after + n, blocks - 1 - n)
        place = block // per_place

        @pl.when(lax.rem(n, per_place) == 0)
        def _():
            @pl.when(place == me)
            def _():
                own_copy.wait()

            for by in range(1, span):

                @pl.when(lax.rem(place + by, span) == me)
                def _():
                    do_copy(by).wait_recv()

        dq_sum[...] = jnp.zeros_like(dq_sum)
        here = block_rows(block)
        queries = qkv_ref[0, here, :]
        d_out = do_ref[here, :]
        lse = lse_ref[block]
        start_row = start_ref[block]
        delta = jnp.sum(
            (d_out.astype(jnp.float32) * o_ref[here, :].astype(jnp.float32)).T, axis=0, keepdims=True
        )

        def visit(j, masked):
            rows = block_rows(j)
            key_part = qkv_ref[1, rows, :]
            scores = (scale * log2e) * matmul_nt(key_part, queries)
            if masked:
                scores = jnp.where(block_mask(j, block, start_row), scores, masked_score)
            probs = jnp.exp2(scores - lse)
            d_probs = matmul_nt(qkv_ref[2, rows, :], d_out)
            d_scores = (probs * (d_probs - delta)).astype(jnp.bfloat16)
            dv_sum[rows, :] += matmul(probs.astype(jnp.bfloat16), d_out)
            dk_sum[rows, :] += matmul(d_scores, queries)
            dq_sum[...] += lax.dot_general(
                key_part, d_scores, (((0,), (0,)), ((), ())), preferred_element_type=jnp.float32
            )

        each_block(block, visit)
        stage_ref[0, here, :] = turn(
            dq_sum[...].T * scale, cos_ref[here, :], sin_ref[here, :]
        ).astype(jnp.bfloat16)
        start_move(block, 0)

        @pl.when((n >= 1) & (n < after))
        def _():
            close(block - 1)

        @pl.when(n >= after - 1)
        def _():
            close(block)

        return carry

    lax.fori_loop(0, blocks, one_block, 0)
    ride.receive()
    ride.finish()
    for by in range(1, span):
        do_copy(by).wait_send()

    def finish(block, carry):
        for which in range(2):
            mine, local, remote = moved(block, which)

            @pl.when(mine)
            def _():
                local.wait()

            @pl.when(jnp.logical_not(mine))
            def _():
                remote.wait_send()

        return carry

    lax.fori_loop(0, blocks, finish, 0)
    for by in range(1, span):
        source = lax.rem(me - by + span, span)
        for half in range(per_place):
            for which in range(2):
                kinds = pl.ds(1, 2) if which else pl.ds(0, 1)
                sends, recvs = (kv_send, kv_recv) if which else (q_send, q_recv)
                send(
                    stage_ref.at[kinds, block_rows(half)], d_raw_ref.at[source, kinds, block_rows(half)],
                    sends.at[half], recvs.at[by, half], place_of(me, groups_here),
                ).wait_recv()


def attend_back(d_sent, held, out, lse, start_rows, cosine, sine, rider, groups_here):
    span, tokens, size = d_sent.shape
    blocks = start_rows.shape[0]
    length = span * tokens
    hbm = pl.BlockSpec(memory_space=pl.ANY)
    vmem = pl.BlockSpec(memory_space=pltpu.VMEM)
    per_place = tokens // BLOCK
    dma = pltpu.SemaphoreType.DMA
    return pl.pallas_call(
        functools.partial(attend_back_kernel, groups_here),
        in_specs=[hbm] + [vmem] * 6 + [hbm],
        out_specs=[hbm, hbm],
        out_shape=[
            jax.ShapeDtypeStruct((span, 3, tokens, size), jnp.bfloat16),
            jax.ShapeDtypeStruct((rider.shape[0] - 1, *rider.shape[1:]), jnp.bfloat16),
        ],
        scratch_shapes=[
            pltpu.VMEM((length, size), jnp.bfloat16),
            pltpu.VMEM((3, length, size), jnp.bfloat16),
            pltpu.VMEM((size, BLOCK), jnp.float32),
            pltpu.VMEM((length, size), jnp.float32),
            pltpu.VMEM((length, size), jnp.float32),
            dma((span,)), dma((span,)), dma((blocks,)), dma((span, per_place)), dma((blocks,)),
            dma((span, per_place)), dma((2, per_place)), dma((1, rider.shape[0] - 1)),
            dma((1, rider.shape[0] - 1)),
        ],
        compiler_params=pltpu.CompilerParams(
            vmem_limit_bytes=48 * 2**20, collective_id=2, has_side_effects=True
        ),
        cost_estimate=pl.CostEstimate(
            flops=length * length * size * 5, bytes_accessed=length * size * 200,
            transcendentals=length * length // 2,
        ),
        name="attend_back",
    )(d_sent, held, out, lse, start_rows, cosine, sine, rider)


def matmul(a, b):
    return jnp.dot(a, b, preferred_element_type=jnp.float32)


def matmul_nt(a, b):
    return lax.dot_general(a, b, (((1,), (1,)), ((), ())), preferred_element_type=jnp.float32)


def resident(shape):
    zeros = (0,) * len(shape)
    return pl.BlockSpec(shape, lambda *_: zeros, pipeline_mode=pl.Buffered(1))


def own_width(ref, width, col):
    return ref[:, pl.ds(pl.multiple_of(col * width, width), width)]


def enter_kernel(
    inputs_ref, cot_ref, pieces_ref, cots_ref, unit_ref, unit_t_ref, own_ref, inverse_ref,
    held_ref, rows_ref, sends, recvs, local, keep,
):
    count, rows, piece = held_ref.shape
    col = lax.axis_index("col")
    greet_cols(count)
    first = Gather(
        halves(inputs_ref, 0, rows), lambda c: halves(held_ref.at[c], 0, rows),
        sends.at[0], recvs.at[0], local.at[0],
    )
    second = Gather(
        halves(cot_ref, 0, rows), lambda c: halves(cots_ref.at[c], 0, rows),
        sends.at[1], recvs.at[1], local.at[1],
    )
    first.start()
    first.forward()
    second.start()
    first.receive()
    out = pltpu.make_async_copy(held_ref, pieces_ref, keep)
    out.start()

    def norm(t, carry):
        here = pl.ds(pl.multiple_of(t * 128, 128), 128)
        parts = [held_ref[c, here, :].astype(jnp.float32) for c in range(count)]
        unit, inverse = normalize_rows(jnp.concatenate(parts, axis=1))
        rows_ref[...] = unit
        unit = unit.astype(jnp.bfloat16)
        unit_ref[here, :] = unit
        unit_t_ref[:, here] = unit.T
        own_ref[here, :] = own_width(rows_ref, piece, col)
        inverse_ref[here, :] = jnp.broadcast_to(inverse, (128, 128))
        return carry

    for t in range(rows // 128):
        norm(t, 0)
    second.forward()
    second.receive()
    first.finish()
    second.finish()
    out.wait()


def enter(inputs, cotangent, count):
    rows, piece = inputs.shape
    width = count * piece
    hbm = pl.BlockSpec(memory_space=pl.ANY)
    vmem = pl.BlockSpec(memory_space=pltpu.VMEM)
    dma = pltpu.SemaphoreType.DMA
    shape = jax.ShapeDtypeStruct
    return pl.pallas_call(
        enter_kernel,
        in_specs=[hbm, hbm],
        out_specs=[hbm, hbm, vmem, vmem, vmem, vmem],
        out_shape=[
            shape((count, rows, piece), jnp.bfloat16),
            shape((count, rows, piece), jnp.bfloat16),
            shape((rows, width), jnp.bfloat16),
            shape((width, rows), jnp.bfloat16),
            shape((rows, piece), jnp.float32),
            shape((rows, 128), jnp.float32),
        ],
        scratch_shapes=[
            pltpu.VMEM((count, rows, piece), jnp.bfloat16),
            pltpu.VMEM((128, width), jnp.float32),
            dma((2, 6)), dma((2, 6)), dma((2, 2)), dma,
        ],
        compiler_params=pltpu.CompilerParams(
            vmem_limit_bytes=40 * 2**20, collective_id=3, has_side_effects=True
        ),
        cost_estimate=pl.CostEstimate(
            flops=10 * rows * width, bytes_accessed=100 * rows * width, transcendentals=0
        ),
        name="enter",
    )(inputs, cotangent)


def own_width(ref, width, col):
    return ref[:, pl.ds(pl.multiple_of(col * width, width), width)]


def project_kernel(unit_ref, weight_ref, cos_ref, sin_ref, out_ref):
    kind = pl.program_id(0)
    rows, width = unit_ref.shape
    heads = out_ref.shape[0]
    weight = weight_ref[:, 0].reshape(width, heads * HEAD)
    step = min(256, rows)
    for t in range(0, rows, step):
        here = pl.ds(t, step)
        raw = matmul(unit_ref[here, :], weight)

        @pl.when(kind < 2)
        def _():
            cosine, sine = cos_ref[here, :], sin_ref[here, :]
            for h in range(heads):
                part = turn(raw[:, h * HEAD : (h + 1) * HEAD], cosine, -sine)
                out_ref[h, 0, here, :] = part.astype(jnp.bfloat16)

        @pl.when(kind == 2)
        def _():
            for h in range(heads):
                out_ref[h, 0, here, :] = raw[:, h * HEAD : (h + 1) * HEAD].astype(jnp.bfloat16)


def project(unit, weight, cosine, sine):
    rows, width = unit.shape
    owners, _, depth, columns = weight.shape
    kinds = 3
    heads = columns // HEAD
    return pl.pallas_call(
        project_kernel,
        grid=(kinds,),
        in_specs=[
            resident((rows, width)),
            pl.BlockSpec((owners, 1, depth, columns), lambda k: (0, k, 0, 0)),
            resident((rows, HEAD)),
            resident((rows, HEAD)),
        ],
        out_specs=pl.BlockSpec((heads, 1, rows, HEAD), lambda k: (0, k, 0, 0)),
        out_shape=jax.ShapeDtypeStruct((heads, kinds, rows, HEAD), jnp.bfloat16),
        compiler_params=pltpu.CompilerParams(vmem_limit_bytes=40 * 2**20),
        cost_estimate=pl.CostEstimate(
            flops=2 * rows * width * kinds * columns, bytes_accessed=2 * width * kinds * columns,
            transcendentals=0,
        ),
        name="project",
    )(unit, weight, cosine, sine)


def branch_kernel(
    back_ref, weight_ref, pieces_ref, unit_ref, unit_t_ref, middle_ref, own_ref, inverse_ref,
    heads_ref, flat_ref, rows_ref, terms_ref, sends, recvs, local,
):
    col = lax.axis_index("col")
    count, heads, rows, size = heads_ref.shape
    piece = pieces_ref.shape[2]
    greet_cols(count)
    parts = 2
    span = rows // parts

    def cut(ref, p):
        half = span // 2
        return (
            ref.at[:, pl.ds(p * span, half)],
            ref.at[:, pl.ds(p * span + half, half)],
        )

    gathers = [
        Gather(
            cut(back_ref, p), lambda c, p=p: cut(heads_ref.at[c], p),
            sends.at[p], recvs.at[p], local.at[p],
        )
        for p in range(parts)
    ]
    gathers[0].start()
    for p in range(parts):
        gathers[p].forward()
        if p + 1 < parts:
            gathers[p + 1].start()
        gathers[p].receive()
        for c in range(count):
            for h in range(heads):
                at = (c * heads + h) * size
                flat_ref[:, at : at + size] = heads_ref[c, h, pl.ds(p * span, span), :]
        terms_ref[...] = matmul_nt(flat_ref[:, :piece], weight_ref[0])
        for c in range(1, count):
            terms_ref[...] += matmul_nt(flat_ref[:, c * piece : (c + 1) * piece], weight_ref[c])

        def finish(t, carry):
            inner = pl.ds(pl.multiple_of(t * 128, 128), 128)
            here = pl.ds(pl.multiple_of(p * span + t * 128, 128), 128)
            rest = [pieces_ref[c, here, :].astype(jnp.float32) for c in range(count)]
            middle = jnp.concatenate(rest, axis=1) + terms_ref[inner, :]
            rows_ref[...] = middle
            middle_ref[here, :] = own_width(rows_ref, piece, col)
            unit, inverse = normalize_rows(middle)
            rows_ref[...] = unit
            own_ref[here, :] = own_width(rows_ref, piece, col)
            inverse_ref[here, :] = jnp.broadcast_to(inverse, (128, 128))
            unit = unit.astype(jnp.bfloat16)
            unit_ref[here, :] = unit
            unit_t_ref[:, here] = unit.T
            return carry

        for t in range(span // 128):
            finish(t, 0)
    for one in gathers:
        one.finish()


def branch(back, weight, pieces):
    heads, rows, size = back.shape
    count, _, piece = pieces.shape
    width = count * piece
    hbm = pl.BlockSpec(memory_space=pl.ANY)
    vmem = pl.BlockSpec(memory_space=pltpu.VMEM)
    dma = pltpu.SemaphoreType.DMA
    shape = jax.ShapeDtypeStruct
    return pl.pallas_call(
        branch_kernel,
        in_specs=[hbm, vmem, vmem],
        out_specs=[vmem] * 5,
        out_shape=[
            shape((rows, width), jnp.bfloat16),
            shape((width, rows), jnp.bfloat16),
            shape((rows, piece), jnp.float32),
            shape((rows, piece), jnp.float32),
            shape((rows, 128), jnp.float32),
        ],
        scratch_shapes=[
            pltpu.VMEM((count, heads, rows, size), jnp.bfloat16),
            pltpu.VMEM((rows // 2, width), jnp.bfloat16),
            pltpu.VMEM((128, width), jnp.float32),
            pltpu.VMEM((rows // 2, width), jnp.float32),
            dma((2, 6)), dma((2, 6)), dma((2, 2)),
        ],
        compiler_params=pltpu.CompilerParams(
            vmem_limit_bytes=56 * 2**20, collective_id=4, has_side_effects=True
        ),
        cost_estimate=pl.CostEstimate(
            flops=2 * rows * width * width, bytes_accessed=40 * width * width, transcendentals=0
        ),
        name="branch",
    )(back, weight, pieces)


def project_grad_kernel(unit_t_ref, d_raw_ref, grad_ref, rows_ref):
    owners, _, depth, _ = grad_ref.shape
    for h in range(d_raw_ref.shape[0]):
        rows_ref[:, h * HEAD : (h + 1) * HEAD] = d_raw_ref[h, 0]
    for owner in range(owners):
        grad_ref[owner, 0] = matmul(
            unit_t_ref[owner * depth : (owner + 1) * depth, :], rows_ref[...]
        ).astype(jnp.bfloat16)


def project_grad(unit_t, d_raw, owners):
    width, rows = unit_t.shape
    heads, kinds = d_raw.shape[:2]
    columns, depth = heads * HEAD, width // owners
    return pl.pallas_call(
        project_grad_kernel,
        grid=(kinds,),
        in_specs=[
            resident((width, rows)),
            pl.BlockSpec((heads, 1, rows, HEAD), lambda k: (0, k, 0, 0)),
        ],
        out_specs=pl.BlockSpec((owners, 1, depth, columns), lambda k: (0, k, 0, 0)),
        out_shape=jax.ShapeDtypeStruct((owners, kinds, depth, columns), jnp.bfloat16),
        scratch_shapes=[pltpu.VMEM((rows, columns), jnp.bfloat16)],
        compiler_params=pltpu.CompilerParams(vmem_limit_bytes=40 * 2**20),
        cost_estimate=pl.CostEstimate(
            flops=2 * rows * width * kinds * columns, bytes_accessed=2 * width * kinds * columns,
            transcendentals=0,
        ),
        name="project_grad",
    )(unit_t, d_raw)


def stats_of(values, unit):
    rows = values.shape[0]
    lane = lax.broadcasted_iota(jnp.int32, (rows, 128), 1)
    both = jnp.where(
        lane % 8 < 4,
        jnp.sum(values, axis=1, keepdims=True),
        jnp.sum(values * unit, axis=1, keepdims=True),
    )
    return both.T[:8]


def columns_of(stats):
    back = jnp.concatenate([stats] * 16, axis=0).T
    return back[:, :1], back[:, 4:5]


class Scatter:
    def __init__(self, pieces, slots, stats, stat_slots, here, sends, recvs):
        me = lax.axis_index("col")
        self.copies = []
        for by in range(1, pieces.shape[0]):
            device = col_device(by)
            self.copies.append(
                send(pieces.at[me ^ by, here], slots.at[by - 1, here],
                     sends.at[0, by - 1], recvs.at[0, by - 1], device)
            )
            if stats is not None:
                self.copies.append(
                    send(stats.at[:, here], stat_slots.at[by - 1, :, here],
                         sends.at[1, by - 1], recvs.at[1, by - 1], device)
                )

    def start(self):
        for one in self.copies:
            one.start()

    def receive(self):
        for one in self.copies:
            one.wait_recv()

    def finish(self):
        for one in self.copies:
            one.wait_send()


def split_rows(sum_ref, unit_ref, pieces_ref, stats_ref, start, size):
    count, _, width = pieces_ref.shape
    for t in range(start, start + size, 128):
        here = pl.ds(t, 128)
        values = sum_ref[here, :]
        stats_ref[:, here] = stats_of(values, unit_ref[here, :].astype(jnp.float32))
        for c in range(count):
            pieces_ref[c, here, :] = values[:, c * width : (c + 1) * width].astype(jnp.bfloat16)


def normed_grad(sum_ref, slots, stats_ref, stat_slots, own_ref, inverse_ref, here, width, col):
    piece = slots.shape[2]
    grad = sum_ref[here, pl.ds(pl.multiple_of(col * piece, piece), piece)]
    stats = stats_ref[:, here]
    for by in range(slots.shape[0]):
        grad = grad + slots[by, here, :].astype(jnp.float32)
        stats = stats + stat_slots[by, :, here]
    sums, cross = columns_of(stats)
    return normalize_back(grad, sums, cross, own_ref[here, :], inverse_ref[here, :1], float(width))


def leave_kernel(
    d_raw_ref, weight_ref, unit_ref, own_ref, inverse_ref, d_middle_ref, out_ref,
    rows_ref, sum_ref, pieces_ref, slots_ref, stats_ref, stat_slots_ref, weights_ref,
    sends, recvs, load,
):
    col = lax.axis_index("col")
    rows, width = unit_ref.shape
    heads, kinds = d_raw_ref.shape[:2]
    columns = heads * HEAD
    loads = [
        pltpu.make_async_copy(weight_ref.at[:, k], weights_ref.at[k], load.at[k]) for k in range(kinds)
    ]
    for one in loads:
        one.start()
    greet_cols(pieces_ref.shape[0])
    for k in range(kinds):
        for h in range(heads):
            rows_ref[k, :, h * HEAD : (h + 1) * HEAD] = d_raw_ref[h, k]
    for one in loads:
        one.wait()
    parts = 2
    span = rows // parts
    moves = []
    for p in range(parts):
        here = pl.ds(p * span, span)
        sum_ref[here, :] = matmul_nt(rows_ref[0, here, :], weights_ref[0].reshape(width, columns))
        for k in range(1, kinds):
            sum_ref[here, :] += matmul_nt(
                rows_ref[k, here, :], weights_ref[k].reshape(width, columns)
            )
        split_rows(sum_ref, unit_ref, pieces_ref, stats_ref, p * span, span)
        moves.append(
            Scatter(pieces_ref, slots_ref, stats_ref, stat_slots_ref, here, sends.at[p], recvs.at[p])
        )
        moves[p].start()
    for p in range(parts):
        moves[p].receive()
        for t in range(p * span, (p + 1) * span, 128):
            here = pl.ds(t, 128)
            out_ref[here, :] = d_middle_ref[here, :] + normed_grad(
                sum_ref, slots_ref, stats_ref, stat_slots_ref, own_ref, inverse_ref, here, width, col
            )
    for one in moves:
        one.finish()


def leave(d_raw, weight, unit, own, inverse, d_middle, count):
    rows, width = unit.shape
    heads, kinds = d_raw.shape[:2]
    owners, _, depth, columns = weight.shape
    piece = width // count
    hbm = pl.BlockSpec(memory_space=pl.ANY)
    vmem = pl.BlockSpec(memory_space=pltpu.VMEM)
    dma = pltpu.SemaphoreType.DMA
    return pl.pallas_call(
        leave_kernel,
        in_specs=[vmem, hbm] + [vmem] * 4,
        out_specs=vmem,
        out_shape=jax.ShapeDtypeStruct((rows, piece), jnp.float32),
        scratch_shapes=[
            pltpu.VMEM((kinds, rows, columns), jnp.bfloat16),
            pltpu.VMEM((rows, width), jnp.float32),
            pltpu.VMEM((count, rows, piece), jnp.bfloat16),
            pltpu.VMEM((count - 1, rows, piece), jnp.bfloat16),
            pltpu.VMEM((8, rows), jnp.float32),
            pltpu.VMEM((count - 1, 8, rows), jnp.float32),
            pltpu.VMEM((kinds, owners, depth, columns), jnp.bfloat16),
            dma((2, 2, count - 1)), dma((2, 2, count - 1)), dma((kinds,)),
        ],
        compiler_params=pltpu.CompilerParams(
            vmem_limit_bytes=60 * 2**20, collective_id=5, has_side_effects=True
        ),
        cost_estimate=pl.CostEstimate(
            flops=2 * rows * width * kinds * columns, bytes_accessed=100 * rows * width, transcendentals=0
        ),
        name="leave",
    )(d_raw, weight, unit, own, inverse, d_middle)


def feed_front(unit_ref, cot_ref, weight_ref, two_ref, act):
    owners, _, _, depth, cols = weight_ref.shape
    rows, width = unit_ref.shape
    count, _, piece = cot_ref.shape
    gate_weight = weight_ref[:, 0, 0].reshape(width, cols)
    up_weight = weight_ref[:, 0, 1].reshape(width, cols)
    down_weight = weight_ref[:, 0, 2].reshape(width, cols)
    step = min(256, rows)
    for t in range(0, rows, step):
        here = pl.ds(t, step)
        unit = unit_ref[here, :]
        gate = matmul(unit, gate_weight)
        up_proj = matmul(unit, up_weight)
        d_hidden = sum(
            matmul(cot_ref[c, here, :], down_weight[c * piece : (c + 1) * piece])
            for c in range(count)
        )
        sigmoid_gate = jax.nn.sigmoid(gate)
        silu_gate = gate * sigmoid_gate
        act[0, here, :] = (silu_gate * up_proj).astype(jnp.bfloat16)
        act[1, here, :] = (
            d_hidden * up_proj * sigmoid_gate * (1.0 + gate * (1.0 - sigmoid_gate))
        ).astype(jnp.bfloat16)
        act[2, here, :] = (d_hidden * silu_gate).astype(jnp.bfloat16)
    for t in range(0, rows, step):
        here = pl.ds(t, step)
        two_ref[here, :] += matmul_nt(act[1, here, :], gate_weight) + matmul_nt(
            act[2, here, :], up_weight
        )


def feed_rear(unit_t_ref, cot_t_ref, down_weight, grad_ref, out_ref, act):
    owners, _, _, depth, cols = grad_ref.shape
    if out_ref is not None:
        rows = out_ref.shape[0]
        step = min(256, rows)
        for t in range(0, rows, step):
            here = pl.ds(t, step)
            out_ref[here, :] += matmul_nt(act[0, here, :], down_weight)
    hidden, d_gate, d_up = act[0], act[1], act[2]
    for owner in range(owners):
        here = pl.ds(owner * depth, depth)
        unit_t = unit_t_ref[here, :]
        grad_ref[owner, 0, 0] = matmul(unit_t, d_gate).astype(jnp.bfloat16)
        grad_ref[owner, 0, 1] = matmul(unit_t, d_up).astype(jnp.bfloat16)
        grad_ref[owner, 0, 2] = matmul(cot_t_ref[here, :], hidden).astype(jnp.bfloat16)


def feed_all_kernel(
    unit_ref, unit_t_ref, cot_ref, cot_t_ref, weight_ref, *refs
):
    old = refs[:-7]
    grad_ref, new_two_ref, new_out_ref, two_ref, out_ref, act_ref, sem = refs[-7:]
    tile = pl.program_id(0)

    @pl.when(tile == 0)
    def _():
        if old:
            loads = [
                pltpu.make_async_copy(old[0], two_ref, sem.at[0]),
                pltpu.make_async_copy(old[1], out_ref, sem.at[1]),
            ]
            for load in loads:
                load.start()
            for load in loads:
                load.wait()
        else:
            two_ref[...] = jnp.zeros_like(two_ref)
            out_ref[...] = jnp.zeros_like(out_ref)

    feed_front(unit_ref, cot_ref, weight_ref, two_ref, act_ref)
    final = tile == pl.num_programs(0) - 1
    copies = [
        pltpu.make_async_copy(two_ref, new_two_ref, sem.at[0]),
        pltpu.make_async_copy(out_ref, new_out_ref, sem.at[1]),
    ]

    @pl.when(final)
    def _():
        copies[0].start()

    down_weight = weight_ref[:, 0, 2].reshape(unit_ref.shape[1], weight_ref.shape[4])
    feed_rear(unit_t_ref, cot_t_ref, down_weight, grad_ref, out_ref, act_ref)

    @pl.when(final)
    def _():
        copies[1].start()
        for copy in copies:
            copy.wait()


def feed_cost(rows, width, owners, tiles, depth, cols, matmuls):
    return pl.CostEstimate(
        flops=2 * matmuls * rows * width * tiles * cols,
        bytes_accessed=12 * owners * tiles * depth * cols,
        transcendentals=rows * tiles * cols,
    )


def feed_all(unit, unit_t, cot, cot_t, weights, old):
    rows, width = unit.shape
    owners, tiles, _, depth, cols = weights.shape
    block = pl.BlockSpec((owners, 1, 3, depth, cols), lambda i: (0, i, 0, 0, 0))
    hbm = pl.BlockSpec(memory_space=pl.ANY)
    return pl.pallas_call(
        feed_all_kernel,
        grid=(tiles,),
        in_specs=[
            resident((rows, width)), resident((width, rows)), resident(cot.shape),
            resident((width, rows)), block,
        ] + [hbm] * len(old),
        out_specs=[block, hbm, hbm],
        out_shape=[jax.ShapeDtypeStruct(weights.shape, jnp.bfloat16)]
        + [jax.ShapeDtypeStruct((rows, width), jnp.float32)] * 2,
        scratch_shapes=[
            pltpu.VMEM((rows, width), jnp.float32),
            pltpu.VMEM((rows, width), jnp.float32),
            pltpu.VMEM((3, rows, cols), jnp.bfloat16),
            pltpu.SemaphoreType.DMA((2,)),
        ],
        compiler_params=pltpu.CompilerParams(vmem_limit_bytes=62 * 2**20),
        cost_estimate=feed_cost(rows, width, owners, tiles, depth, cols, 9),
        name="feed_all",
    )(unit, unit_t, cot, cot_t, weights, *old)


def feed_last_kernel(
    unit_hbm, unit_t_hbm, cots_hbm, cot_t_hbm, weight_hbm, old_two_hbm, old_out_hbm, own_ref,
    inverse_ref, out_t_ref, back_ref,
    grad_ref, ffn_ref, d_middle_ref, d_sent_ref, out_grad_ref,
    unit_ref, turned_ref, cots_ref, weight_ref, two_ref, sum_ref, act_ref, pieces_ref, slots_ref,
    stats_ref, stat_slots_ref, d_pieces_ref,
    load, sends, recvs, g_sends, g_recvs,
):
    col = lax.axis_index("col")
    rows, width = unit_ref.shape
    count, _, piece = pieces_ref.shape
    owners, tiles, _, depth, cols = weight_ref.shape
    heads, _, size = back_ref.shape

    def fetch(i, source, target):
        copy = pltpu.make_async_copy(source, target, load.at[i])
        copy.start()
        return copy

    loads = [
        fetch(0, unit_hbm, unit_ref), fetch(1, weight_hbm, weight_ref), fetch(2, cots_hbm, cots_ref),
        fetch(3, old_two_hbm, two_ref), fetch(4, unit_t_hbm, turned_ref.at[0]),
        fetch(5, cot_t_hbm, turned_ref.at[1]), fetch(6, old_out_hbm.at[: rows // 2], sum_ref),
    ]
    greet_cols(count)
    for i in range(4):
        loads[i].wait()
    for tile in range(tiles):
        feed_front(unit_ref, cots_ref, weight_ref.at[:, tile : tile + 1], two_ref, act_ref.at[tile])
    parts = 2
    span = rows // parts
    moves, gathers = [], []
    for p in range(parts):
        split_rows(two_ref, unit_ref, pieces_ref, stats_ref, p * span, span)
        moves.append(
            Scatter(pieces_ref, slots_ref, stats_ref, stat_slots_ref, pl.ds(p * span, span),
                    sends.at[p], recvs.at[p])
        )
        moves[p].start()
        own = d_pieces_ref.at[col]
        gathers.append(
            Gather(
                halves(own, p * span, span),
                lambda c, p=p: halves(d_pieces_ref.at[c], p * span, span),
                g_sends.at[p], g_recvs.at[p], None,
            )
        )
    for p in range(2):
        loads[6 + p].wait()
        for tile in range(tiles):
            down_weight = weight_ref[:, tile, 2].reshape(width, cols)
            sum_ref[...] += matmul_nt(act_ref[tile, 0, pl.ds(p * span, span), :], down_weight)
        for c in range(count):
            ffn_ref[c, pl.ds(p * span, span), :] = sum_ref[
                :, c * piece : (c + 1) * piece
            ].astype(jnp.bfloat16)
        if p == 0:
            loads.append(fetch(7, old_out_hbm.at[rows // 2 :], sum_ref))
    for i in range(4, 6):
        loads[i].wait()
    for tile in range(tiles):
        feed_rear(
            turned_ref.at[0], turned_ref.at[1], None, grad_ref.at[:, tile : tile + 1], None,
            act_ref.at[tile],
        )
    own_cot = cots_ref.at[col]
    for p in range(parts):
        moves[p].receive()
        for t in range(p * span, (p + 1) * span, 128):
            here = pl.ds(t, 128)
            d_middle = own_cot[here, :].astype(jnp.float32) + normed_grad(
                two_ref, slots_ref, stats_ref, stat_slots_ref, own_ref, inverse_ref, here, width, col
            )
            d_middle_ref[here, :] = d_middle
            d_pieces_ref[col, here, :] = d_middle.astype(jnp.bfloat16)
        gathers[p].start()
    for p in range(parts):
        gathers[p].forward()
        gathers[p].receive()
        here = pl.ds(p * span, span)
        d_attended = matmul(d_pieces_ref[0, here, :], out_t_ref[:piece, :])
        for c in range(1, count):
            d_attended += matmul(
                d_pieces_ref[c, here, :], out_t_ref[c * piece : (c + 1) * piece, :]
            )
        for h in range(heads):
            d_sent_ref[h, here, :] = d_attended[:, h * size : (h + 1) * size].astype(jnp.bfloat16)
    per_piece = piece // depth
    for owner in range(owners):
        at = (owner % per_piece) * depth
        d_branch = d_pieces_ref[owner // per_piece, :, at : at + depth]
        for h in range(heads):
            out_grad_ref[owner, h * size : (h + 1) * size, :] = lax.dot_general(
                back_ref[h], d_branch, (((0,), (0,)), ((), ())), preferred_element_type=jnp.float32
            ).astype(jnp.bfloat16)
    for one in moves + gathers:
        one.finish()


def feed_last(unit, unit_t, cots, cot_t, weights, old, own, inverse, out_t, back):
    rows, width = unit.shape
    count, _, piece = cots.shape
    owners, tiles, _, depth, cols = weights.shape
    heads, _, size = back.shape
    hbm = pl.BlockSpec(memory_space=pl.ANY)
    vmem = pl.BlockSpec(memory_space=pltpu.VMEM)
    dma = pltpu.SemaphoreType.DMA
    shape = jax.ShapeDtypeStruct
    return pl.pallas_call(
        feed_last_kernel,
        in_specs=[hbm] * 7 + [vmem] * 4,
        out_specs=[vmem] * 5,
        out_shape=[
            shape(weights.shape, jnp.bfloat16),
            shape((count, rows, piece), jnp.bfloat16),
            shape((rows, piece), jnp.float32),
            shape((heads, rows, size), jnp.bfloat16),
            shape((owners, heads * size, depth), jnp.bfloat16),
        ],
        scratch_shapes=[
            pltpu.VMEM((rows, width), jnp.bfloat16),
            pltpu.VMEM((2, width, rows), jnp.bfloat16),
            pltpu.VMEM((count, rows, piece), jnp.bfloat16),
            pltpu.VMEM(weights.shape, jnp.bfloat16),
            pltpu.VMEM((rows, width), jnp.float32),
            pltpu.VMEM((rows // 2, width), jnp.float32),
            pltpu.VMEM((tiles, 3, rows, cols), jnp.bfloat16),
            pltpu.VMEM((count, rows, piece), jnp.bfloat16),
            pltpu.VMEM((count - 1, rows, piece), jnp.bfloat16),
            pltpu.VMEM((8, rows), jnp.float32),
            pltpu.VMEM((count - 1, 8, rows), jnp.float32),
            pltpu.VMEM((count, rows, piece), jnp.bfloat16),
            dma((8,)), dma((2, 2, count - 1)), dma((2, 2, count - 1)), dma((2, 6)), dma((2, 6)),
        ],
        compiler_params=pltpu.CompilerParams(
            vmem_limit_bytes=63 * 2**20 + 2**19, collective_id=6, has_side_effects=True
        ),
        cost_estimate=pl.CostEstimate(
            flops=18 * rows * width * tiles * cols, bytes_accessed=100 * rows * width,
            transcendentals=rows * cols,
        ),
        name="feed_last",
    )(unit, unit_t, cots, cot_t, weights, *old, own, inverse, out_t, back)


def group_tables(lengths, group):
    row_lengths = lax.dynamic_slice_in_dim(lengths, group, 1, 0)[0]
    local_index = jnp.arange(GROUP_LEN, dtype=jnp.int32)
    seg_ends = jnp.cumsum(row_lengths)
    seg_starts = seg_ends - row_lengths
    after_prompt = local_index - PROMPT
    inside = (after_prompt[:, None] >= seg_starts[None, :]) & (
        after_prompt[:, None] < seg_ends[None, :]
    )
    start = jnp.sum(jnp.where(inside, seg_starts[None, :], 0), axis=1)
    in_prompt = local_index < PROMPT
    start_row = jnp.where(in_prompt, 0, PROMPT + start)
    position = jnp.where(in_prompt, local_index, PROMPT + after_prompt - start)
    half = HEAD // 2
    frequency = jnp.exp(
        -math.log(rope_base) * (2.0 * jnp.arange(half, dtype=jnp.float32) / HEAD)
    )
    angles = position.astype(jnp.float32)[:, None] * frequency[None, :]
    cosine, sine = jnp.cos(angles), jnp.sin(angles)
    return (
        start_row.reshape(GROUP_LEN // BLOCK, 1, BLOCK),
        jnp.concatenate([cosine, cosine], axis=1),
        jnp.concatenate([sine, -sine], axis=1),
    )


def fast_body(
    inputs,
    cotangent,
    lengths,
    query_key_value_weight,
    out_weight,
    gate_weight,
    up_weight,
    down_weight,
):
    tok_rows, part_width = inputs.shape
    col_count = lax.axis_size("col")
    col_index = lax.axis_index("col")
    row_index = lax.axis_index("row")
    span = GROUP_LEN // tok_rows
    groups_here = lax.axis_size("row") // span
    heads_here = part_width // HEAD
    place = row_index // groups_here
    group = row_index % groups_here
    depth = gate_weight.shape[0]
    hidden_here = gate_weight.shape[1]
    tiles = hidden_here // min(256, depth)
    tile = hidden_here // tiles

    def gather(shard, after=None):
        if after is not None:
            shard, after = tied(shard, after)
        return lax.all_gather(shard, "row"), after

    def tied(value, *others):
        return lax.optimization_barrier((value, *others))

    mixed = jnp.concatenate([query_key_value_weight.transpose(1, 0, 2), out_weight.T[None]])
    weights, _ = gather(mixed)
    packed = jnp.stack([gate_weight, up_weight, down_weight.T]).reshape(3, depth, tiles, tile)
    packed = packed.transpose(2, 0, 1, 3)
    last = max(1, tiles // 8)
    first = tiles // 2
    start_rows, cosine, sine = lax.optimization_barrier(group_tables(lengths, group))
    own_cos = lax.dynamic_slice_in_dim(
        cosine.reshape(span, tok_rows, HEAD), place, 1, 0
    )[0]
    own_sin = lax.dynamic_slice_in_dim(sine.reshape(span, tok_rows, HEAD), place, 1, 0)[0]

    early_inputs, own_cos = tied(inputs, own_cos)
    pieces, cots, normed_one, unit_one_t, unit_one, inverse_one = enter(
        early_inputs, cotangent, col_count
    )
    normed_one, weights = tied(normed_one, weights)
    feed_one, weights = gather(packed[:first], weights)
    sent = project(normed_one, weights, own_cos, own_sin)
    out_rows_t = weights[:, 3].reshape(-1, part_width)
    back, held, attended_head, lse, out_t = attend(
        sent, start_rows, out_rows_t, groups_here, col_count
    )
    back, feed_one = tied(back, feed_one)
    feed_two, feed_one = gather(packed[first:-last], feed_one)
    normed_two, unit_t, middle, unit_two, inverse_two = branch(back, out_t, pieces)
    cot_t = cots.transpose(0, 2, 1).reshape(-1, tok_rows)
    rows_two = (normed_two, unit_t, cots, cot_t)

    def owned(part):
        return lax.psum_scatter(part, "row", scatter_dimension=0, tiled=True)[0]

    grads_one, *sums = feed_all(*rows_two, feed_one, ())
    sums[0], feed_two = tied(sums[0], feed_two)
    feed_three, feed_two = gather(packed[-last:], feed_two)
    grads_two, *sums = feed_all(*rows_two, feed_two, sums)
    sums[0], grads_one, feed_three = tied(sums[0], grads_one, feed_three)
    grads_one = owned(grads_one)
    grads_three, ffn_pieces, d_middle, d_sent, out_part = feed_last(
        *rows_two, feed_three, sums, unit_two, inverse_two, out_rows_t, back
    )
    d_sent, grads_one = tied(d_sent, grads_one)
    grads_two, grads_one = tied(grads_two, grads_one)
    grads_two = owned(grads_two)
    d_raw, ffn_others = attend_back(
        d_sent, held, attended_head, lse, start_rows, cosine, sine, ffn_pieces, groups_here
    )
    projection_part = project_grad(unit_one_t, d_raw, weights.shape[0])
    projection_part, grads_two = tied(projection_part, grads_two)
    blocks = out_part.reshape(out_part.shape[0], -1, tile, depth)
    late = jnp.concatenate(
        [grads_three.reshape(out_part.shape[0], -1, depth, tile), blocks], axis=1
    )
    late, grads_two = tied(late, grads_two)
    late = owned(late)
    input_grad = leave(
        d_raw, weights, normed_one, unit_one, inverse_one, d_middle, col_count
    )
    projection_part, late, input_grad = tied(projection_part, late, input_grad)
    own_grads = owned(projection_part)
    own_ffn = lax.dynamic_slice_in_dim(ffn_pieces, col_index, 1, 0)[0]
    output = middle + own_ffn.astype(jnp.float32) + jnp.sum(ffn_others.astype(jnp.float32), axis=0)
    output = output.astype(jnp.bfloat16)
    qkv_grad = own_grads.astype(jnp.float32).transpose(1, 0, 2)
    grads_three = late[: 3 * last].reshape(last, 3, depth, tile)
    out_grad = late[3 * last :].reshape(part_width, depth).astype(jnp.float32)
    grads = jnp.concatenate([grads_one, grads_two, grads_three]).astype(jnp.float32)
    grads = grads.transpose(1, 2, 0, 3).reshape(3, depth, hidden_here)
    return (output, input_grad, qkv_grad, out_grad, grads[0], grads[1], grads[2].T)


def body(
    inputs,
    cotangent,
    lengths,
    query_key_value_weight,
    out_weight,
    gate_weight,
    up_weight,
    down_weight,
):
    tok_rows = inputs.shape[0]
    part_width = inputs.shape[1]
    col_count = lax.axis_size("col")
    col_index = lax.axis_index("col")
    row_index = lax.axis_index("row")
    full_width = float(part_width * col_count)
    group_span = GROUP_LEN // tok_rows
    groups_here = lax.axis_size("row") // group_span
    head_size = HEAD
    heads_here = part_width // head_size
    score_scale = head_size ** (-0.5)
    block_place = row_index // groups_here
    full_inputs, full_cotangent = (
        lax.all_gather(inputs, "col", axis=1, tiled=True),
        lax.all_gather(cotangent, "col", axis=1, tiled=True),
    )
    projection_full_rows, out_full, gate_full, up_full, down_full = (
        lax.all_gather(query_key_value_weight, "row", axis=0, tiled=True),
        lax.all_gather(out_weight, "row", axis=1, tiled=True),
        lax.all_gather(gate_weight, "row", axis=0, tiled=True),
        lax.all_gather(up_weight, "row", axis=0, tiled=True),
        lax.all_gather(down_weight, "row", axis=1, tiled=True),
    )
    unit_one, inverse_one = normalize_rows(full_inputs.astype(jnp.float32))
    first_normed_input = unit_one.astype(jnp.bfloat16)
    raw_projection_output = jnp.einsum(
        "cu,ufk->cfk", first_normed_input, projection_full_rows, preferred_element_type=jnp.float32
    )
    raw_projection_output = raw_projection_output.reshape(tok_rows, 3, heads_here, head_size)
    own_meta = token_layout(lengths, row_index, groups_here, tok_rows)
    cosine, sine = rotation_angles(own_meta[3], head_size)
    queries = rotate(raw_projection_output[:, 0], cosine, sine, False).astype(jnp.bfloat16)
    key_rows = rotate(raw_projection_output[:, 1], cosine, sine, False).astype(jnp.bfloat16)
    value_rows = raw_projection_output[:, 2].astype(jnp.bfloat16)
    pieces = [(key_rows, value_rows)]
    for shift_by in range(1, group_span):
        pieces.append(passed_along((key_rows, value_rows), "row", shift_by * groups_here))
    visibility = [
        visible_mask(
            own_meta,
            token_layout(lengths, row_index - shift_by * groups_here, groups_here, tok_rows),
        )
        for shift_by in range(group_span)
    ]
    live_piece = [shift_by <= block_place for shift_by in range(group_span)]
    first_scores = score_block(queries, pieces[0][0], visibility[0], score_scale)
    top_rows = jnp.max(first_scores, axis=-1, keepdims=True)
    total_rows = jnp.sum(jnp.exp(first_scores - top_rows), axis=-1, keepdims=True)
    for shift_by in range(1, group_span):

        def add_stats(carry, shift_by=shift_by):
            old_top, old_total = carry
            scores = score_block(queries, pieces[shift_by][0], visibility[shift_by], score_scale)
            new_top = jnp.maximum(old_top, jnp.max(scores, axis=-1, keepdims=True))
            new_total = old_total * jnp.exp(old_top - new_top) + jnp.sum(
                jnp.exp(scores - new_top), axis=-1, keepdims=True
            )
            return (new_top, new_total)

        top_rows, total_rows = lax.cond(
            live_piece[shift_by], add_stats, lambda carry: carry, (top_rows, total_rows)
        )
    log_total = top_rows + jnp.log(total_rows)
    attended = jnp.zeros((tok_rows, heads_here, head_size), jnp.float32)
    for shift_by in range(group_span):

        def add_values(total, shift_by=shift_by):
            scores = score_block(queries, pieces[shift_by][0], visibility[shift_by], score_scale)
            probs_low = jnp.exp(scores - log_total).astype(jnp.bfloat16)
            return total + jnp.einsum(
                "hqk,khd->qhd", probs_low, pieces[shift_by][1], preferred_element_type=jnp.float32
            )

        attended = lax.cond(live_piece[shift_by], add_values, lambda total: total, attended)
    attended_flat = attended.reshape(tok_rows, part_width).astype(jnp.bfloat16)
    branch_terms = jnp.dot(attended_flat, out_full, preferred_element_type=jnp.float32)
    branch_full = lax.psum(branch_terms, "col")
    middle_full = full_inputs.astype(jnp.float32) + branch_full
    middle = lax.dynamic_slice_in_dim(middle_full, col_index * part_width, part_width, 1)
    unit_two, inverse_two = normalize_rows(middle_full)
    normed_two = unit_two.astype(jnp.bfloat16)
    gate = jnp.dot(normed_two, gate_full, preferred_element_type=jnp.float32)
    up_proj = jnp.dot(normed_two, up_full, preferred_element_type=jnp.float32)
    sigmoid_gate = jax.nn.sigmoid(gate)
    silu_gate = gate * sigmoid_gate
    hidden = (silu_gate * up_proj).astype(jnp.bfloat16)
    ffn_terms = jnp.dot(hidden, down_full, preferred_element_type=jnp.float32)
    ffn_part = lax.psum_scatter(
        ffn_terms.astype(jnp.bfloat16), "col", scatter_dimension=1, tiled=True
    ).astype(jnp.float32)
    output = (middle + ffn_part).astype(jnp.bfloat16)
    projection_full_rows, out_full, gate_full, up_full, down_full = (
        lax.all_gather(query_key_value_weight, "row", axis=0, tiled=True),
        lax.all_gather(out_weight, "row", axis=1, tiled=True),
        lax.all_gather(gate_weight, "row", axis=0, tiled=True),
        lax.all_gather(up_weight, "row", axis=0, tiled=True),
        lax.all_gather(down_weight, "row", axis=1, tiled=True),
    )
    d_hidden = jnp.einsum(
        "td,fd->tf", full_cotangent, down_full, preferred_element_type=jnp.float32
    )
    down_part = jnp.einsum("tf,td->fd", hidden, full_cotangent, preferred_element_type=jnp.float32)
    d_gate = (d_hidden * up_proj * sigmoid_gate * (1.0 + gate * (1.0 - sigmoid_gate))).astype(
        jnp.bfloat16
    )
    d_up = (d_hidden * silu_gate).astype(jnp.bfloat16)
    gate_part = jnp.einsum("td,tf->df", normed_two, d_gate, preferred_element_type=jnp.float32)
    up_part = jnp.einsum("td,tf->df", normed_two, d_up, preferred_element_type=jnp.float32)
    d_normed_two = jnp.einsum(
        "tf,df->td", d_gate, gate_full, preferred_element_type=jnp.float32
    ) + jnp.einsum("tf,df->td", d_up, up_full, preferred_element_type=jnp.float32)
    grad_two, sum_two, cross_two = (
        lax.psum_scatter(
            d_normed_two.astype(jnp.bfloat16), "col", scatter_dimension=1, tiled=True
        ).astype(jnp.float32),
        lax.psum_scatter(
            spread_cols(jnp.sum(d_normed_two, axis=1), col_count).astype(jnp.bfloat16),
            "col",
            scatter_dimension=1,
            tiled=True,
        ).astype(jnp.float32),
        lax.psum_scatter(
            spread_cols(jnp.sum(d_normed_two * unit_two, axis=1), col_count).astype(jnp.bfloat16),
            "col",
            scatter_dimension=1,
            tiled=True,
        ).astype(jnp.float32),
    )
    unit_two_here = lax.dynamic_slice_in_dim(unit_two, col_index * part_width, part_width, 1)
    d_middle = cotangent.astype(jnp.float32) + normalize_back(
        grad_two, sum_two, cross_two, unit_two_here, inverse_two, full_width
    )
    d_branch = d_middle.astype(jnp.bfloat16)
    d_branch_full = lax.all_gather(d_branch, "col", axis=1, tiled=True)
    out_part = jnp.einsum(
        "tc,td->cd", attended_flat, d_branch_full, preferred_element_type=jnp.float32
    )
    d_attended = jnp.einsum(
        "td,cd->tc", d_branch_full, out_full, preferred_element_type=jnp.float32
    )
    d_attended = d_attended.astype(jnp.bfloat16).reshape(tok_rows, heads_here, head_size)
    delta_rows = jnp.zeros((heads_here, tok_rows, 1), jnp.float32)
    for shift_by in range(group_span):

        def add_delta(total, shift_by=shift_by):
            scores = score_block(queries, pieces[shift_by][0], visibility[shift_by], score_scale)
            probs_full = jnp.exp(scores - log_total)
            d_probs = jnp.einsum(
                "qhd,khd->hqk", d_attended, pieces[shift_by][1], preferred_element_type=jnp.float32
            )
            return total + jnp.sum(probs_full * d_probs, axis=-1, keepdims=True)

        delta_rows = lax.cond(live_piece[shift_by], add_delta, lambda total: total, delta_rows)
    zero_rows = jnp.zeros((tok_rows, heads_here, head_size), jnp.float32)
    d_queries = zero_rows
    for shift_by in range(group_span):

        def piece_grads(query_total, shift_by=shift_by):
            key_part, value_part = pieces[shift_by]
            scores = score_block(queries, key_part, visibility[shift_by], score_scale)
            probs_full = jnp.exp(scores - log_total)
            d_probs = jnp.einsum(
                "qhd,khd->hqk", d_attended, value_part, preferred_element_type=jnp.float32
            )
            d_scores = (probs_full * (d_probs - delta_rows)).astype(jnp.bfloat16)
            query_total = (
                query_total
                + jnp.einsum("hqk,khd->qhd", d_scores, key_part, preferred_element_type=jnp.float32)
                * score_scale
            )
            d_key_part = (
                jnp.einsum("hqk,qhd->khd", d_scores, queries, preferred_element_type=jnp.float32)
                * score_scale
            )
            d_value_part = jnp.einsum(
                "hqk,qhd->khd",
                probs_full.astype(jnp.bfloat16),
                d_attended,
                preferred_element_type=jnp.float32,
            )
            return (query_total, d_key_part, d_value_part)

        d_queries, d_key_part, d_value_part = lax.cond(
            live_piece[shift_by],
            piece_grads,
            lambda query_total: (query_total, zero_rows, zero_rows),
            d_queries,
        )
        if shift_by == 0:
            d_keys = d_key_part
            d_values = d_value_part
        else:
            back_keys, back_values = (
                passed_along(
                    d_key_part.astype(jnp.bfloat16), "row", -shift_by * groups_here
                ).astype(d_key_part.dtype),
                passed_along(
                    d_value_part.astype(jnp.bfloat16), "row", -shift_by * groups_here
                ).astype(d_value_part.dtype),
            )
            d_keys = d_keys + back_keys
            d_values = d_values + back_values
    raw_score_gradient = jnp.stack(
        [rotate(d_queries, cosine, sine, True), rotate(d_keys, cosine, sine, True), d_values],
        axis=1,
    )
    raw_score_gradient = raw_score_gradient.reshape(tok_rows, 3, part_width).astype(jnp.bfloat16)
    projection_part_rows = jnp.einsum(
        "lo,lbw->obw", first_normed_input, raw_score_gradient, preferred_element_type=jnp.float32
    )
    first_normed_gradient = jnp.einsum(
        "xzq,vzq->xv", raw_score_gradient, projection_full_rows, preferred_element_type=jnp.float32
    )
    grad_one, sum_one, cross_one = (
        lax.psum_scatter(
            first_normed_gradient.astype(jnp.bfloat16), "col", scatter_dimension=1, tiled=True
        ).astype(jnp.float32),
        lax.psum_scatter(
            spread_cols(jnp.sum(first_normed_gradient, axis=1), col_count).astype(jnp.bfloat16),
            "col",
            scatter_dimension=1,
            tiled=True,
        ).astype(jnp.float32),
        lax.psum_scatter(
            spread_cols(jnp.sum(first_normed_gradient * unit_one, axis=1), col_count).astype(
                jnp.bfloat16
            ),
            "col",
            scatter_dimension=1,
            tiled=True,
        ).astype(jnp.float32),
    )
    unit_one_here = lax.dynamic_slice_in_dim(unit_one, col_index * part_width, part_width, 1)
    input_grad = d_middle + normalize_back(
        grad_one, sum_one, cross_one, unit_one_here, inverse_one, full_width
    )
    owned_grads = (
        lax.psum_scatter(
            projection_part_rows.astype(jnp.bfloat16), "row", scatter_dimension=0, tiled=True
        ).astype(jnp.float32),
        lax.psum_scatter(
            out_part.astype(jnp.bfloat16), "row", scatter_dimension=1, tiled=True
        ).astype(jnp.float32),
        lax.psum_scatter(
            gate_part.astype(jnp.bfloat16), "row", scatter_dimension=0, tiled=True
        ).astype(jnp.float32),
        lax.psum_scatter(
            up_part.astype(jnp.bfloat16), "row", scatter_dimension=0, tiled=True
        ).astype(jnp.float32),
        lax.psum_scatter(
            down_part.astype(jnp.bfloat16), "row", scatter_dimension=1, tiled=True
        ).astype(jnp.float32),
    )
    return (
        output,
        input_grad,
        owned_grads[0],
        owned_grads[1],
        owned_grads[2],
        owned_grads[3],
        owned_grads[4],
    )


def step(inputs, *rest):
    span = GROUP_LEN // inputs.shape[0]
    heads_here = inputs.shape[1] // HEAD
    fast = heads_here == span and lax.axis_size("col") == 4
    return (fast_body if fast else body)(inputs, *rest)


def solution(mesh):
    placed = (
        P("row", "col"),
        P("row", "col"),
        P(),
        P("row", None, "col"),
        P("col", "row"),
        P("row", "col"),
        P("row", "col"),
        P("col", "row"),
    )
    return jax.shard_map(
        step,
        mesh=mesh,
        in_specs=placed,
        out_specs=(
            P("row", "col"),
            P("row", "col"),
            P("row", None, "col"),
            P("col", "row"),
            P("row", "col"),
            P("row", "col"),
            P("col", "row"),
        ),
        check_vma=False,
    )
```

```python
import functools
import math

import jax
import jax.numpy as jnp
from jax import lax
from jax.experimental import pallas as pl
from jax.experimental.pallas import tpu as pltpu
from jax.sharding import PartitionSpec as P

HEAD = 128
PROMPT = 2048
GROUP_LEN = 4096


rope_base = 10000.0
norm_eps = 1e-05
masked_score = -1e30


def passed_along(shard, axis, by):
    size = lax.axis_size(axis)
    pairs = [(i, i + by) for i in range(size) if 0 <= i + by < size]
    return lax.ppermute(shard, axis, pairs)


def normalize_rows(values):
    centre = values - jnp.mean(values, axis=-1, keepdims=True)
    spread = jnp.mean(centre * centre, axis=-1, keepdims=True)
    inverse = lax.rsqrt(spread + norm_eps)
    return (centre * inverse, inverse)


def normalize_back(grad_rows, sum_grad, sum_cross, unit_rows, inverse, row_width):
    return inverse * (grad_rows - sum_grad / row_width - unit_rows * (sum_cross / row_width))


def spread_cols(values, copies):
    return jnp.broadcast_to(values[:, None], (values.shape[0], copies))


def token_layout(lengths, source_row, groups_count, row_count):
    valid_source = source_row >= 0
    safe_source = jnp.maximum(source_row, 0)
    group_id = jnp.where(valid_source, safe_source % groups_count, -1)
    place_here = safe_source // groups_count
    safe_group = jnp.clip(group_id, 0, lengths.shape[0] - 1)
    row_lengths = lax.dynamic_slice_in_dim(lengths, safe_group, 1, 0)[0]
    local_index = place_here * row_count + jnp.arange(row_count, dtype=jnp.int32)
    after_prompt = local_index - PROMPT
    seg_ends = jnp.cumsum(row_lengths)
    in_prompt = local_index < PROMPT
    counted = jnp.sum((after_prompt[:, None] >= seg_ends[None, :]).astype(jnp.int32), axis=1)
    segment = jnp.where(in_prompt, 0, 1 + counted)
    seg_starts = seg_ends - row_lengths
    picked = (segment - 1)[:, None] == jnp.arange(row_lengths.shape[0], dtype=jnp.int32)[None, :]
    seg_start = jnp.sum(jnp.where(picked, seg_starts[None, :], 0), axis=1)
    position = jnp.where(in_prompt, local_index, PROMPT + after_prompt - seg_start)
    return (group_id, local_index, segment, position)


def rotation_angles(position, head_size):
    half_size = head_size // 2
    frequency = jnp.exp(
        -math.log(rope_base) * (2.0 * jnp.arange(half_size, dtype=jnp.float32) / head_size)
    )
    angles = position.astype(jnp.float32)[:, None] * frequency[None, :]
    return (jnp.cos(angles)[:, None, :], jnp.sin(angles)[:, None, :])


def rotate(values, cosine, sine, inverse_turn):
    half_size = values.shape[-1] // 2
    first_half = values[..., :half_size]
    second_half = values[..., half_size:]
    if inverse_turn:
        sine = -sine
    return jnp.concatenate(
        [first_half * cosine - second_half * sine, second_half * cosine + first_half * sine],
        axis=-1,
    )


def visible_mask(query_meta, key_meta):
    query_group, query_index, query_segment, query_position = query_meta
    key_group, key_index, key_segment, key_position = key_meta
    causal = key_index[None, :] <= query_index[:, None]
    shared = (key_segment[None, :] == 0) | (key_segment[None, :] == query_segment[:, None])
    return (query_group == key_group) & causal & shared


def score_block(queries, key_part, allowed, score_scale):
    raw_scores = (
        jnp.einsum("qhd,khd->hqk", queries, key_part, preferred_element_type=jnp.float32)
        * score_scale
    )
    return jnp.where(allowed[None], raw_scores, masked_score)


BLOCK = 512
log2e = 1.4426950408889634


def turn(values, cosine, sine):
    return values * cosine + pltpu.roll(values, values.shape[1] // 2, 1) * sine


def block_mask(key_block, query_block, start_row):
    key_index = key_block * BLOCK + lax.broadcasted_iota(jnp.int32, (BLOCK, BLOCK), 0)
    query_index = query_block * BLOCK + lax.broadcasted_iota(jnp.int32, (BLOCK, BLOCK), 1)
    return (key_index <= query_index) & (key_index >= start_row)


def each_block(block, visit):
    prompt_blocks = PROMPT // BLOCK

    def whole(j, carry):
        visit(j, False)
        return carry

    lax.fori_loop(0, jnp.minimum(block, prompt_blocks), whole, 0)

    @pl.when(block > prompt_blocks)
    def _():
        visit(block - 1, True)

    visit(block, True)


MESH = pl.DeviceIdType.MESH


def place_of(place, groups_here):
    row = lax.axis_index("row")
    return (place * groups_here + lax.rem(row, groups_here), lax.axis_index("col"))


def send(source, target, send_sem, recv_sem, device):
    return pltpu.make_async_remote_copy(
        src_ref=source, dst_ref=target, send_sem=send_sem, recv_sem=recv_sem,
        device_id=device, device_id_type=MESH,
    )


def block_rows(block):
    return pl.ds(pl.multiple_of(block * BLOCK, BLOCK), BLOCK)


def col_device(by):
    return (lax.axis_index("row"), lax.axis_index("col") ^ by)


def greet_cols(count):
    barrier = pltpu.get_barrier_semaphore()
    for by in range(1, count):
        pl.semaphore_signal(barrier, inc=1, device_id=col_device(by), device_id_type=MESH)
    pl.semaphore_wait(barrier, count - 1)


class Gather:
    def __init__(self, source, slots, sends, recvs, local):
        me = lax.axis_index("col")
        a, b = source[0], source[1]
        self.own = []
        if local is not None:
            self.own = [
                pltpu.make_async_copy(a, slots(me)[0], local.at[0]),
                pltpu.make_async_copy(b, slots(me)[1], local.at[1]),
            ]

        def copy(i, what, where, by):
            return send(what, where, sends.at[i], recvs.at[i], col_device(by))

        self.first = [
            copy(0, a, slots(me)[0], 1),
            copy(3, b, slots(me)[1], 2),
            copy(1, b, slots(me)[1], 1),
            copy(2, a, slots(me)[0], 2),
        ]
        across, along = me ^ 1, me ^ 2
        self.second = [
            copy(4, slots(across)[0], slots(across)[0], 2),
            copy(5, slots(along)[1], slots(along)[1], 1),
        ]

    def start(self):
        for one in self.own + self.first:
            one.start()

    def forward(self):
        self.first[0].wait_recv()
        self.second[0].start()
        self.first[1].wait_recv()
        self.second[1].start()

    def receive(self):
        for one in self.first[2:] + self.second:
            one.wait_recv()
        for one in self.own:
            one.wait()

    def finish(self):
        for one in self.first + self.second:
            one.wait_send()


def halves(ref, start, size):
    half = size // 2
    return ref.at[pl.ds(start, half)], ref.at[pl.ds(start + half, half)]


def greet_all(me, span, groups_here, count):
    barrier = pltpu.get_barrier_semaphore()
    for by in range(1, span):
        pl.semaphore_signal(
            barrier, inc=1, device_id=place_of(lax.rem(me + by, span), groups_here), device_id_type=MESH
        )
    for by in range(1, count):
        pl.semaphore_signal(barrier, inc=1, device_id=col_device(by), device_id_type=MESH)
    pl.semaphore_wait(barrier, span + count - 2)


def attend_kernel(
    groups_here, sent_ref, start_ref, rider_ref, back_ref, held_ref, o_ref, lse_ref, riders_ref,
    qkv_ref, top_ref, total_ref, sum_ref,
    in_send, in_recv, out_send, out_recv, keep_sem, own_sem, ride_send, ride_recv, ride_local,
):
    span, _, tokens, _ = sent_ref.shape
    me = lax.axis_index("row") // groups_here
    blocks = start_ref.shape[0]
    per_place = tokens // BLOCK
    scale = HEAD**-0.5 * log2e
    greet_all(me, span, groups_here, riders_ref.shape[0])
    depth = rider_ref.shape[0]
    ride = Gather(
        halves(rider_ref, 0, depth), lambda c: halves(riders_ref.at[c], 0, depth),
        ride_send, ride_recv, ride_local,
    )

    def qkv_copy(by):
        peer = lax.rem(me + by, span)
        return send(
            sent_ref.at[peer], qkv_ref.at[:, pl.ds(pl.multiple_of(me * tokens, tokens), tokens)],
            in_send.at[by], in_recv.at[by], place_of(peer, groups_here),
        )

    own_rows = pl.ds(pl.multiple_of(me * tokens, tokens), tokens)
    own_copy = pltpu.make_async_copy(sent_ref.at[me], qkv_ref.at[:, own_rows], in_recv.at[0])
    own_copy.start()
    for by in range(1, span):
        qkv_copy(by).start()
    ride.start()

    def out_copy(block):
        to = block // per_place
        half = lax.rem(block, per_place)
        by = lax.rem(to - me + span, span)
        return send(
            o_ref.at[block_rows(block)], back_ref.at[me, block_rows(half)],
            out_send.at[block], out_recv.at[by, half], place_of(to, groups_here),
        )

    def own_out(block):
        return pltpu.make_async_copy(
            o_ref.at[block_rows(block)],
            back_ref.at[me, block_rows(lax.rem(block, per_place))],
            own_sem.at[lax.rem(block, per_place)],
        )

    def keep_copy(place):
        rows = pl.ds(pl.multiple_of(place * tokens, tokens), tokens)
        return pltpu.make_async_copy(qkv_ref.at[:, rows], held_ref.at[:, rows], keep_sem.at[place])

    def one_block(block, carry):
        place = block // per_place

        @pl.when(lax.rem(block, per_place) == 0)
        def _():
            @pl.when(place == me)
            def _():
                own_copy.wait()

            for by in range(1, span):

                @pl.when(lax.rem(place + by, span) == me)
                def _():
                    qkv_copy(by).wait_recv()

            keep_copy(place).start()

        top_ref[...] = jnp.full_like(top_ref, masked_score)
        total_ref[...] = jnp.zeros_like(total_ref)
        sum_ref[...] = jnp.zeros_like(sum_ref)
        queries = qkv_ref[0, block_rows(block), :]
        start_row = start_ref[block]

        def visit(j, masked):
            rows = block_rows(j)
            scores = scale * matmul_nt(qkv_ref[1, rows, :], queries)
            if masked:
                scores = jnp.where(block_mask(j, block, start_row), scores, masked_score)
            old_top = top_ref[...]
            new_top = jnp.maximum(old_top, jnp.max(scores, axis=0, keepdims=True))
            shrink = jnp.exp2(old_top - new_top)
            probs = jnp.exp2(scores - new_top)
            if masked:
                probs = jnp.where(scores > 0.5 * masked_score, probs, 0.0)
            total_ref[...] = total_ref[...] * shrink + jnp.sum(probs, axis=0, keepdims=True)
            sum_ref[...] = sum_ref[...] * shrink + lax.dot_general(
                qkv_ref[2, rows, :],
                probs.astype(jnp.bfloat16),
                (((0,), (0,)), ((), ())),
                preferred_element_type=jnp.float32,
            )
            top_ref[...] = new_top

        each_block(block, visit)
        total = total_ref[...]
        o_ref[block_rows(block), :] = (sum_ref[...] / total).T.astype(jnp.bfloat16)
        lse_ref[block] = top_ref[...] + jnp.log2(total)

        @pl.when(place == me)
        def _():
            own_out(block).start()

        @pl.when(place != me)
        def _():
            out_copy(block).start()

        @pl.when(block == blocks // 2)
        def _():
            ride.forward()

        return carry

    lax.fori_loop(0, blocks, one_block, 0)
    ride.receive()
    ride.finish()

    for by in range(1, span):
        qkv_copy(by).wait_send()

    def finish(block, carry):
        place = block // per_place

        @pl.when(place == me)
        def _():
            own_out(block).wait()

        @pl.when(place != me)
        def _():
            out_copy(block).wait_send()

        return carry

    lax.fori_loop(0, blocks, finish, 0)
    for by in range(1, span):
        for half in range(per_place):
            send(
                o_ref.at[block_rows(half)], back_ref.at[lax.rem(me - by + span, span), block_rows(half)],
                out_send.at[half], out_recv.at[by, half], place_of(me, groups_here),
            ).wait_recv()
    for place in range(span):
        keep_copy(place).wait()


def attend(sent, start_rows, rider, groups_here, count):
    span, _, tokens, size = sent.shape
    blocks = start_rows.shape[0]
    length = span * tokens
    hbm = pl.BlockSpec(memory_space=pl.ANY)
    vmem = pl.BlockSpec(memory_space=pltpu.VMEM)
    per_place = tokens // BLOCK
    dma = pltpu.SemaphoreType.DMA
    return pl.pallas_call(
        functools.partial(attend_kernel, groups_here),
        in_specs=[hbm, vmem, hbm],
        out_specs=[hbm, hbm, vmem, vmem, hbm],
        out_shape=[
            jax.ShapeDtypeStruct((span, tokens, size), jnp.bfloat16),
            jax.ShapeDtypeStruct((3, length, size), jnp.bfloat16),
            jax.ShapeDtypeStruct((length, size), jnp.bfloat16),
            jax.ShapeDtypeStruct((blocks, 1, BLOCK), jnp.float32),
            jax.ShapeDtypeStruct((count, *rider.shape), jnp.bfloat16),
        ],
        scratch_shapes=[
            pltpu.VMEM((3, length, size), jnp.bfloat16),
            pltpu.VMEM((1, BLOCK), jnp.float32),
            pltpu.VMEM((1, BLOCK), jnp.float32),
            pltpu.VMEM((size, BLOCK), jnp.float32),
            dma((span,)), dma((span,)), dma((blocks,)), dma((span, per_place)), dma((span,)),
            dma((per_place,)), dma((6,)), dma((6,)), dma((2,)),
        ],
        compiler_params=pltpu.CompilerParams(
            vmem_limit_bytes=32 * 2**20, collective_id=1, has_side_effects=True
        ),
        cost_estimate=pl.CostEstimate(
            flops=length * length * size * 2, bytes_accessed=length * size * 200,
            transcendentals=length * length // 2,
        ),
        name="attend",
    )(sent, start_rows, rider)


def attend_back_kernel(
    groups_here, d_sent_ref, qkv_ref, o_ref, lse_ref, start_ref, cos_ref, sin_ref, rider_ref,
    d_raw_ref, riders_ref, do_ref, stage_ref, dq_sum, dk_sum, dv_sum,
    in_send, in_recv, q_send, q_recv, kv_send, kv_recv, own_sem, ride_send, ride_recv,
):
    span, tokens, _ = d_sent_ref.shape
    me = lax.axis_index("row") // groups_here
    blocks = start_ref.shape[0]
    per_place = tokens // BLOCK
    after = blocks - PROMPT // BLOCK
    scale = HEAD**-0.5
    greet_all(me, span, groups_here, rider_ref.shape[0])
    ride = Scatter(
        rider_ref, riders_ref, None, None, pl.ds(0, tokens), ride_send, ride_recv
    )
    own_rows = pl.ds(pl.multiple_of(me * tokens, tokens), tokens)

    def do_copy(by):
        peer = lax.rem(me + by, span)
        return send(
            d_sent_ref.at[peer], do_ref.at[own_rows], in_send.at[by], in_recv.at[by],
            place_of(peer, groups_here),
        )

    own_copy = pltpu.make_async_copy(d_sent_ref.at[me], do_ref.at[own_rows], in_recv.at[0])
    own_copy.start()
    for by in range(1, span):
        do_copy(by).start()
    ride.start()
    dk_sum[...] = jnp.zeros_like(dk_sum)
    dv_sum[...] = jnp.zeros_like(dv_sum)

    def moved(block, which):
        to = block // per_place
        half = lax.rem(block, per_place)
        by = lax.rem(to - me + span, span)
        kinds = pl.ds(1, 2) if which else pl.ds(0, 1)
        source = stage_ref.at[kinds, block_rows(block)]
        target = d_raw_ref.at[me, kinds, block_rows(half)]
        sends, recvs = (kv_send, kv_recv) if which else (q_send, q_recv)
        return (
            to == me,
            pltpu.make_async_copy(source, target, own_sem.at[which, half]),
            send(source, target, sends.at[block], recvs.at[by, half], place_of(to, groups_here)),
        )

    def start_move(block, which):
        mine, local, remote = moved(block, which)

        @pl.when(mine)
        def _():
            local.start()

        @pl.when(jnp.logical_not(mine))
        def _():
            remote.start()

    def close(j):
        rows = block_rows(j)
        stage_ref[1, rows, :] = turn(
            dk_sum[rows, :] * scale, cos_ref[rows, :], sin_ref[rows, :]
        ).astype(jnp.bfloat16)
        stage_ref[2, rows, :] = dv_sum[rows, :].astype(jnp.bfloat16)
        start_move(j, 1)

    def one_block(n, carry):
        block = jnp.where(n < after, blocks - after + n, blocks - 1 - n)
        place = block // per_place

        @pl.when(lax.rem(n, per_place) == 0)
        def _():
            @pl.when(place == me)
            def _():
                own_copy.wait()

            for by in range(1, span):

                @pl.when(lax.rem(place + by, span) == me)
                def _():
                    do_copy(by).wait_recv()

        dq_sum[...] = jnp.zeros_like(dq_sum)
        here = block_rows(block)
        queries = qkv_ref[0, here, :]
        d_out = do_ref[here, :]
        lse = lse_ref[block]
        start_row = start_ref[block]
        delta = jnp.sum(
            (d_out.astype(jnp.float32) * o_ref[here, :].astype(jnp.float32)).T, axis=0, keepdims=True
        )

        def visit(j, masked):
            rows = block_rows(j)
            key_part = qkv_ref[1, rows, :]
            scores = (scale * log2e) * matmul_nt(key_part, queries)
            if masked:
                scores = jnp.where(block_mask(j, block, start_row), scores, masked_score)
            probs = jnp.exp2(scores - lse)
            d_probs = matmul_nt(qkv_ref[2, rows, :], d_out)
            d_scores = (probs * (d_probs - delta)).astype(jnp.bfloat16)
            dv_sum[rows, :] += matmul(probs.astype(jnp.bfloat16), d_out)
            dk_sum[rows, :] += matmul(d_scores, queries)
            dq_sum[...] += lax.dot_general(
                key_part, d_scores, (((0,), (0,)), ((), ())), preferred_element_type=jnp.float32
            )

        each_block(block, visit)
        stage_ref[0, here, :] = turn(
            dq_sum[...].T * scale, cos_ref[here, :], sin_ref[here, :]
        ).astype(jnp.bfloat16)
        start_move(block, 0)

        @pl.when((n >= 1) & (n < after))
        def _():
            close(block - 1)

        @pl.when(n >= after - 1)
        def _():
            close(block)

        return carry

    lax.fori_loop(0, blocks, one_block, 0)
    ride.receive()
    ride.finish()
    for by in range(1, span):
        do_copy(by).wait_send()

    def finish(block, carry):
        for which in range(2):
            mine, local, remote = moved(block, which)

            @pl.when(mine)
            def _():
                local.wait()

            @pl.when(jnp.logical_not(mine))
            def _():
                remote.wait_send()

        return carry

    lax.fori_loop(0, blocks, finish, 0)
    for by in range(1, span):
        source = lax.rem(me - by + span, span)
        for half in range(per_place):
            for which in range(2):
                kinds = pl.ds(1, 2) if which else pl.ds(0, 1)
                sends, recvs = (kv_send, kv_recv) if which else (q_send, q_recv)
                send(
                    stage_ref.at[kinds, block_rows(half)], d_raw_ref.at[source, kinds, block_rows(half)],
                    sends.at[half], recvs.at[by, half], place_of(me, groups_here),
                ).wait_recv()


def attend_back(d_sent, held, out, lse, start_rows, cosine, sine, rider, groups_here):
    span, tokens, size = d_sent.shape
    blocks = start_rows.shape[0]
    length = span * tokens
    hbm = pl.BlockSpec(memory_space=pl.ANY)
    vmem = pl.BlockSpec(memory_space=pltpu.VMEM)
    per_place = tokens // BLOCK
    dma = pltpu.SemaphoreType.DMA
    return pl.pallas_call(
        functools.partial(attend_back_kernel, groups_here),
        in_specs=[hbm] + [vmem] * 6 + [hbm],
        out_specs=[hbm, hbm],
        out_shape=[
            jax.ShapeDtypeStruct((span, 3, tokens, size), jnp.bfloat16),
            jax.ShapeDtypeStruct((rider.shape[0] - 1, *rider.shape[1:]), jnp.bfloat16),
        ],
        scratch_shapes=[
            pltpu.VMEM((length, size), jnp.bfloat16),
            pltpu.VMEM((3, length, size), jnp.bfloat16),
            pltpu.VMEM((size, BLOCK), jnp.float32),
            pltpu.VMEM((length, size), jnp.float32),
            pltpu.VMEM((length, size), jnp.float32),
            dma((span,)), dma((span,)), dma((blocks,)), dma((span, per_place)), dma((blocks,)),
            dma((span, per_place)), dma((2, per_place)), dma((1, rider.shape[0] - 1)),
            dma((1, rider.shape[0] - 1)),
        ],
        compiler_params=pltpu.CompilerParams(
            vmem_limit_bytes=48 * 2**20, collective_id=2, has_side_effects=True
        ),
        cost_estimate=pl.CostEstimate(
            flops=length * length * size * 5, bytes_accessed=length * size * 200,
            transcendentals=length * length // 2,
        ),
        name="attend_back",
    )(d_sent, held, out, lse, start_rows, cosine, sine, rider)


def matmul(a, b):
    return jnp.dot(a, b, preferred_element_type=jnp.float32)


def matmul_nt(a, b):
    return lax.dot_general(a, b, (((1,), (1,)), ((), ())), preferred_element_type=jnp.float32)


def resident(shape):
    zeros = (0,) * len(shape)
    return pl.BlockSpec(shape, lambda *_: zeros, pipeline_mode=pl.Buffered(1))


def own_width(ref, width, col):
    return ref[:, pl.ds(pl.multiple_of(col * width, width), width)]


def enter_kernel(
    inputs_ref, cot_ref, pieces_ref, cots_ref, unit_ref, unit_t_ref, own_ref, inverse_ref,
    held_ref, rows_ref, sends, recvs, local, keep,
):
    count, rows, piece = held_ref.shape
    col = lax.axis_index("col")
    greet_cols(count)
    first = Gather(
        halves(inputs_ref, 0, rows), lambda c: halves(held_ref.at[c], 0, rows),
        sends.at[0], recvs.at[0], local.at[0],
    )
    second = Gather(
        halves(cot_ref, 0, rows), lambda c: halves(cots_ref.at[c], 0, rows),
        sends.at[1], recvs.at[1], local.at[1],
    )
    first.start()
    first.forward()
    second.start()
    first.receive()
    out = pltpu.make_async_copy(held_ref, pieces_ref, keep)
    out.start()

    def norm(t, carry):
        here = pl.ds(pl.multiple_of(t * 128, 128), 128)
        parts = [held_ref[c, here, :].astype(jnp.float32) for c in range(count)]
        unit, inverse = normalize_rows(jnp.concatenate(parts, axis=1))
        rows_ref[...] = unit
        unit = unit.astype(jnp.bfloat16)
        unit_ref[here, :] = unit
        unit_t_ref[:, here] = unit.T
        own_ref[here, :] = own_width(rows_ref, piece, col)
        inverse_ref[here, :] = jnp.broadcast_to(inverse, (128, 128))
        return carry

    lax.fori_loop(0, rows // 128, norm, 0)
    second.forward()
    second.receive()
    first.finish()
    second.finish()
    out.wait()


def enter(inputs, cotangent, count):
    rows, piece = inputs.shape
    width = count * piece
    hbm = pl.BlockSpec(memory_space=pl.ANY)
    vmem = pl.BlockSpec(memory_space=pltpu.VMEM)
    dma = pltpu.SemaphoreType.DMA
    shape = jax.ShapeDtypeStruct
    return pl.pallas_call(
        enter_kernel,
        in_specs=[hbm, hbm],
        out_specs=[hbm, hbm, vmem, vmem, vmem, vmem],
        out_shape=[
            shape((count, rows, piece), jnp.bfloat16),
            shape((count, rows, piece), jnp.bfloat16),
            shape((rows, width), jnp.bfloat16),
            shape((width, rows), jnp.bfloat16),
            shape((rows, piece), jnp.float32),
            shape((rows, 128), jnp.float32),
        ],
        scratch_shapes=[
            pltpu.VMEM((count, rows, piece), jnp.bfloat16),
            pltpu.VMEM((128, width), jnp.float32),
            dma((2, 6)), dma((2, 6)), dma((2, 2)), dma,
        ],
        compiler_params=pltpu.CompilerParams(
            vmem_limit_bytes=40 * 2**20, collective_id=3, has_side_effects=True
        ),
        cost_estimate=pl.CostEstimate(
            flops=10 * rows * width, bytes_accessed=100 * rows * width, transcendentals=0
        ),
        name="enter",
    )(inputs, cotangent)


def own_width(ref, width, col):
    return ref[:, pl.ds(pl.multiple_of(col * width, width), width)]


def project_kernel(unit_ref, weight_ref, cos_ref, sin_ref, out_ref):
    kind = pl.program_id(0)
    rows, width = unit_ref.shape
    heads = out_ref.shape[0]
    weight = weight_ref[:, 0].reshape(width, heads * HEAD)
    step = min(256, rows)
    for t in range(0, rows, step):
        here = pl.ds(t, step)
        raw = matmul(unit_ref[here, :], weight)

        @pl.when(kind < 2)
        def _():
            cosine, sine = cos_ref[here, :], sin_ref[here, :]
            for h in range(heads):
                part = turn(raw[:, h * HEAD : (h + 1) * HEAD], cosine, -sine)
                out_ref[h, 0, here, :] = part.astype(jnp.bfloat16)

        @pl.when(kind == 2)
        def _():
            for h in range(heads):
                out_ref[h, 0, here, :] = raw[:, h * HEAD : (h + 1) * HEAD].astype(jnp.bfloat16)


def project(unit, weight, cosine, sine):
    rows, width = unit.shape
    owners, _, depth, columns = weight.shape
    kinds = 3
    heads = columns // HEAD
    return pl.pallas_call(
        project_kernel,
        grid=(kinds,),
        in_specs=[
            resident((rows, width)),
            pl.BlockSpec((owners, 1, depth, columns), lambda k: (0, k, 0, 0)),
            resident((rows, HEAD)),
            resident((rows, HEAD)),
        ],
        out_specs=pl.BlockSpec((heads, 1, rows, HEAD), lambda k: (0, k, 0, 0)),
        out_shape=jax.ShapeDtypeStruct((heads, kinds, rows, HEAD), jnp.bfloat16),
        compiler_params=pltpu.CompilerParams(vmem_limit_bytes=40 * 2**20),
        cost_estimate=pl.CostEstimate(
            flops=2 * rows * width * kinds * columns, bytes_accessed=2 * width * kinds * columns,
            transcendentals=0,
        ),
        name="project",
    )(unit, weight, cosine, sine)


def branch_kernel(
    back_ref, weight_ref, pieces_ref, unit_ref, unit_t_ref, middle_ref, own_ref, inverse_ref,
    heads_ref, flat_ref, rows_ref, terms_ref, sends, recvs, local,
):
    col = lax.axis_index("col")
    count, heads, rows, size = heads_ref.shape
    piece = pieces_ref.shape[2]
    greet_cols(count)
    parts = 2
    span = rows // parts

    def cut(ref, p):
        half = span // 2
        return (
            ref.at[:, pl.ds(p * span, half)],
            ref.at[:, pl.ds(p * span + half, half)],
        )

    gathers = [
        Gather(
            cut(back_ref, p), lambda c, p=p: cut(heads_ref.at[c], p),
            sends.at[p], recvs.at[p], local.at[p],
        )
        for p in range(parts)
    ]
    gathers[0].start()
    for p in range(parts):
        gathers[p].forward()
        if p + 1 < parts:
            gathers[p + 1].start()
        gathers[p].receive()
        for c in range(count):
            for h in range(heads):
                at = (c * heads + h) * size
                flat_ref[:, at : at + size] = heads_ref[c, h, pl.ds(p * span, span), :]
        terms_ref[...] = matmul_nt(flat_ref[:, :piece], weight_ref[0])
        for c in range(1, count):
            terms_ref[...] += matmul_nt(flat_ref[:, c * piece : (c + 1) * piece], weight_ref[c])

        def finish(t, carry):
            inner = pl.ds(pl.multiple_of(t * 128, 128), 128)
            here = pl.ds(pl.multiple_of(p * span + t * 128, 128), 128)
            rest = [pieces_ref[c, here, :].astype(jnp.float32) for c in range(count)]
            middle = jnp.concatenate(rest, axis=1) + terms_ref[inner, :]
            rows_ref[...] = middle
            middle_ref[here, :] = own_width(rows_ref, piece, col)
            unit, inverse = normalize_rows(middle)
            rows_ref[...] = unit
            own_ref[here, :] = own_width(rows_ref, piece, col)
            inverse_ref[here, :] = jnp.broadcast_to(inverse, (128, 128))
            unit = unit.astype(jnp.bfloat16)
            unit_ref[here, :] = unit
            unit_t_ref[:, here] = unit.T
            return carry

        for t in range(span // 128):
            finish(t, 0)
    for one in gathers:
        one.finish()


def branch(back, weight, pieces):
    heads, rows, size = back.shape
    count, _, piece = pieces.shape
    width = count * piece
    hbm = pl.BlockSpec(memory_space=pl.ANY)
    vmem = pl.BlockSpec(memory_space=pltpu.VMEM)
    dma = pltpu.SemaphoreType.DMA
    shape = jax.ShapeDtypeStruct
    return pl.pallas_call(
        branch_kernel,
        in_specs=[hbm, vmem, vmem],
        out_specs=[vmem] * 5,
        out_shape=[
            shape((rows, width), jnp.bfloat16),
            shape((width, rows), jnp.bfloat16),
            shape((rows, piece), jnp.float32),
            shape((rows, piece), jnp.float32),
            shape((rows, 128), jnp.float32),
        ],
        scratch_shapes=[
            pltpu.VMEM((count, heads, rows, size), jnp.bfloat16),
            pltpu.VMEM((rows // 2, width), jnp.bfloat16),
            pltpu.VMEM((128, width), jnp.float32),
            pltpu.VMEM((rows // 2, width), jnp.float32),
            dma((2, 6)), dma((2, 6)), dma((2, 2)),
        ],
        compiler_params=pltpu.CompilerParams(
            vmem_limit_bytes=56 * 2**20, collective_id=4, has_side_effects=True
        ),
        cost_estimate=pl.CostEstimate(
            flops=2 * rows * width * width, bytes_accessed=40 * width * width, transcendentals=0
        ),
        name="branch",
    )(back, weight, pieces)


def project_grad_kernel(unit_t_ref, d_raw_ref, grad_ref, rows_ref):
    owners, _, depth, _ = grad_ref.shape
    for h in range(d_raw_ref.shape[0]):
        rows_ref[:, h * HEAD : (h + 1) * HEAD] = d_raw_ref[h, 0]
    for owner in range(owners):
        grad_ref[owner, 0] = matmul(
            unit_t_ref[owner * depth : (owner + 1) * depth, :], rows_ref[...]
        ).astype(jnp.bfloat16)


def project_grad(unit_t, d_raw, owners):
    width, rows = unit_t.shape
    heads, kinds = d_raw.shape[:2]
    columns, depth = heads * HEAD, width // owners
    return pl.pallas_call(
        project_grad_kernel,
        grid=(kinds,),
        in_specs=[
            resident((width, rows)),
            pl.BlockSpec((heads, 1, rows, HEAD), lambda k: (0, k, 0, 0)),
        ],
        out_specs=pl.BlockSpec((owners, 1, depth, columns), lambda k: (0, k, 0, 0)),
        out_shape=jax.ShapeDtypeStruct((owners, kinds, depth, columns), jnp.bfloat16),
        scratch_shapes=[pltpu.VMEM((rows, columns), jnp.bfloat16)],
        compiler_params=pltpu.CompilerParams(vmem_limit_bytes=40 * 2**20),
        cost_estimate=pl.CostEstimate(
            flops=2 * rows * width * kinds * columns, bytes_accessed=2 * width * kinds * columns,
            transcendentals=0,
        ),
        name="project_grad",
    )(unit_t, d_raw)


def each_rows(start, size, step, visit):
    def body(t, carry):
        visit(pl.ds(pl.multiple_of(start + t * step, step), step))
        return carry

    lax.fori_loop(0, size // step, body, 0)


def stats_of(values, unit):
    rows = values.shape[0]
    lane = lax.broadcasted_iota(jnp.int32, (rows, 128), 1)
    both = jnp.where(
        lane % 8 < 4,
        jnp.sum(values, axis=1, keepdims=True),
        jnp.sum(values * unit, axis=1, keepdims=True),
    )
    return both.T[:8]


def columns_of(stats):
    back = jnp.concatenate([stats] * 16, axis=0).T
    return back[:, :1], back[:, 4:5]


class Scatter:
    def __init__(self, pieces, slots, stats, stat_slots, here, sends, recvs):
        me = lax.axis_index("col")
        self.copies = []
        for by in range(1, pieces.shape[0]):
            device = col_device(by)
            self.copies.append(
                send(pieces.at[me ^ by, here], slots.at[by - 1, here],
                     sends.at[0, by - 1], recvs.at[0, by - 1], device)
            )
            if stats is not None:
                self.copies.append(
                    send(stats.at[:, here], stat_slots.at[by - 1, :, here],
                         sends.at[1, by - 1], recvs.at[1, by - 1], device)
                )

    def start(self):
        for one in self.copies:
            one.start()

    def receive(self):
        for one in self.copies:
            one.wait_recv()

    def finish(self):
        for one in self.copies:
            one.wait_send()


def split_rows(sum_ref, unit_ref, pieces_ref, stats_ref, start, size):
    count, _, width = pieces_ref.shape

    def part(here):
        values = sum_ref[here, :]
        stats_ref[:, here] = stats_of(values, unit_ref[here, :].astype(jnp.float32))
        for c in range(count):
            pieces_ref[c, here, :] = values[:, c * width : (c + 1) * width].astype(jnp.bfloat16)

    each_rows(start, size, 128, part)


def normed_grad(sum_ref, slots, stats_ref, stat_slots, own_ref, inverse_ref, here, width, col):
    piece = slots.shape[2]
    grad = sum_ref[here, pl.ds(pl.multiple_of(col * piece, piece), piece)]
    stats = stats_ref[:, here]
    for by in range(slots.shape[0]):
        grad = grad + slots[by, here, :].astype(jnp.float32)
        stats = stats + stat_slots[by, :, here]
    sums, cross = columns_of(stats)
    return normalize_back(grad, sums, cross, own_ref[here, :], inverse_ref[here, :1], float(width))


def leave_kernel(
    d_raw_ref, weight_ref, unit_ref, own_ref, inverse_ref, d_middle_ref, out_ref,
    rows_ref, sum_ref, pieces_ref, slots_ref, stats_ref, stat_slots_ref, weights_ref,
    sends, recvs, load,
):
    col = lax.axis_index("col")
    rows, width = unit_ref.shape
    heads, kinds = d_raw_ref.shape[:2]
    columns = heads * HEAD
    loads = [
        pltpu.make_async_copy(weight_ref.at[:, k], weights_ref.at[k], load.at[k]) for k in range(kinds)
    ]
    for one in loads:
        one.start()
    greet_cols(pieces_ref.shape[0])
    for k in range(kinds):
        for h in range(heads):
            rows_ref[k, :, h * HEAD : (h + 1) * HEAD] = d_raw_ref[h, k]
    for one in loads:
        one.wait()
    parts = 2
    span = rows // parts
    moves = []
    for p in range(parts):
        here = pl.ds(p * span, span)
        sum_ref[here, :] = matmul_nt(rows_ref[0, here, :], weights_ref[0].reshape(width, columns))
        for k in range(1, kinds):
            sum_ref[here, :] += matmul_nt(
                rows_ref[k, here, :], weights_ref[k].reshape(width, columns)
            )
        split_rows(sum_ref, unit_ref, pieces_ref, stats_ref, p * span, span)
        moves.append(
            Scatter(pieces_ref, slots_ref, stats_ref, stat_slots_ref, here, sends.at[p], recvs.at[p])
        )
        moves[p].start()
    for p in range(parts):
        moves[p].receive()

        def last_part(here):
            out_ref[here, :] = d_middle_ref[here, :] + normed_grad(
                sum_ref, slots_ref, stats_ref, stat_slots_ref, own_ref, inverse_ref, here, width, col
            )

        each_rows(p * span, span, 128, last_part)
    for one in moves:
        one.finish()


def leave(d_raw, weight, unit, own, inverse, d_middle, count):
    rows, width = unit.shape
    heads, kinds = d_raw.shape[:2]
    owners, _, depth, columns = weight.shape
    piece = width // count
    hbm = pl.BlockSpec(memory_space=pl.ANY)
    vmem = pl.BlockSpec(memory_space=pltpu.VMEM)
    dma = pltpu.SemaphoreType.DMA
    return pl.pallas_call(
        leave_kernel,
        in_specs=[vmem, hbm] + [vmem] * 4,
        out_specs=vmem,
        out_shape=jax.ShapeDtypeStruct((rows, piece), jnp.float32),
        scratch_shapes=[
            pltpu.VMEM((kinds, rows, columns), jnp.bfloat16),
            pltpu.VMEM((rows, width), jnp.float32),
            pltpu.VMEM((count, rows, piece), jnp.bfloat16),
            pltpu.VMEM((count - 1, rows, piece), jnp.bfloat16),
            pltpu.VMEM((8, rows), jnp.float32),
            pltpu.VMEM((count - 1, 8, rows), jnp.float32),
            pltpu.VMEM((kinds, owners, depth, columns), jnp.bfloat16),
            dma((2, 2, count - 1)), dma((2, 2, count - 1)), dma((kinds,)),
        ],
        compiler_params=pltpu.CompilerParams(
            vmem_limit_bytes=60 * 2**20, collective_id=5, has_side_effects=True
        ),
        cost_estimate=pl.CostEstimate(
            flops=2 * rows * width * kinds * columns, bytes_accessed=100 * rows * width, transcendentals=0
        ),
        name="leave",
    )(d_raw, weight, unit, own, inverse, d_middle)


def feed_front(unit_ref, cot_ref, weight_ref, two_ref, act):
    owners, _, _, depth, cols = weight_ref.shape
    rows, width = unit_ref.shape
    count, _, piece = cot_ref.shape
    gate_weight = weight_ref[:, 0, 0].reshape(width, cols)
    up_weight = weight_ref[:, 0, 1].reshape(width, cols)
    down_weight = weight_ref[:, 0, 2].reshape(width, cols)
    step = min(256, rows)
    for t in range(0, rows, step):
        here = pl.ds(t, step)
        unit = unit_ref[here, :]
        gate = matmul(unit, gate_weight)
        up_proj = matmul(unit, up_weight)
        d_hidden = sum(
            matmul(cot_ref[c, here, :], down_weight[c * piece : (c + 1) * piece])
            for c in range(count)
        )
        sigmoid_gate = jax.nn.sigmoid(gate)
        silu_gate = gate * sigmoid_gate
        act[0, here, :] = (silu_gate * up_proj).astype(jnp.bfloat16)
        act[1, here, :] = (
            d_hidden * up_proj * sigmoid_gate * (1.0 + gate * (1.0 - sigmoid_gate))
        ).astype(jnp.bfloat16)
        act[2, here, :] = (d_hidden * silu_gate).astype(jnp.bfloat16)
    for t in range(0, rows, step):
        here = pl.ds(t, step)
        two_ref[here, :] += matmul_nt(act[1, here, :], gate_weight) + matmul_nt(
            act[2, here, :], up_weight
        )


def feed_rear(unit_t_ref, cot_t_ref, grad_ref, act):
    owners, _, depth, cols = grad_ref.shape
    hidden, d_gate, d_up = act[0], act[1], act[2]
    for owner in range(owners):
        here = pl.ds(owner * depth, depth)
        unit_t = unit_t_ref[here, :]
        grad_ref[owner, 0] = matmul(unit_t, d_gate).astype(jnp.bfloat16)
        grad_ref[owner, 1] = matmul(unit_t, d_up).astype(jnp.bfloat16)
        grad_ref[owner, 2] = matmul(cot_t_ref[here, :], hidden).astype(jnp.bfloat16)


def feed_all_kernel(
    unit_ref, unit_t_ref, cot_ref, cot_t_ref, weight_ref, *refs
):
    old = refs[:-7]
    grad_ref, new_two_ref, new_out_ref, two_ref, out_ref, act_ref, sem = refs[-7:]
    tile = pl.program_id(0)

    @pl.when(tile == 0)
    def _():
        if old:
            loads = [
                pltpu.make_async_copy(old[0], two_ref, sem.at[0]),
                pltpu.make_async_copy(old[1], out_ref, sem.at[1]),
            ]
            for load in loads:
                load.start()
            for load in loads:
                load.wait()
        else:
            two_ref[...] = jnp.zeros_like(two_ref)
            out_ref[...] = jnp.zeros_like(out_ref)

    feed_front(unit_ref, cot_ref, weight_ref, two_ref, act_ref)
    final = tile == pl.num_programs(0) - 1
    copies = [
        pltpu.make_async_copy(two_ref, new_two_ref, sem.at[0]),
        pltpu.make_async_copy(out_ref, new_out_ref, sem.at[1]),
    ]

    @pl.when(final)
    def _():
        copies[0].start()

    down_weight = weight_ref[:, 0, 2].reshape(unit_ref.shape[1], weight_ref.shape[4])
    rows = unit_ref.shape[0]
    step = min(256, rows)
    for t in range(0, rows, step):
        here = pl.ds(t, step)
        out_ref[here, :] += matmul_nt(act_ref[0, here, :], down_weight)

    @pl.when(final)
    def _():
        copies[1].start()

    feed_rear(unit_t_ref, cot_t_ref, grad_ref, act_ref)

    @pl.when(final)
    def _():
        for copy in copies:
            copy.wait()


def feed_cost(rows, width, owners, tiles, depth, cols, matmuls):
    return pl.CostEstimate(
        flops=2 * matmuls * rows * width * tiles * cols,
        bytes_accessed=12 * owners * tiles * depth * cols,
        transcendentals=rows * tiles * cols,
    )


def feed_all(unit, unit_t, cot, cot_t, weights, tiles, old, blocks):
    rows, width = unit.shape
    owners, _, _, depth, cols = weights.shape
    hbm = pl.BlockSpec(memory_space=pl.ANY)
    return pl.pallas_call(
        feed_all_kernel,
        grid=(tiles,),
        in_specs=[
            resident((rows, width)), resident((width, rows)), resident(cot.shape),
            resident((width, rows)),
            pl.BlockSpec((owners, 1, 3, depth, cols), lambda i: (0, i, 0, 0, 0)),
        ] + [hbm] * len(old),
        out_specs=[pl.BlockSpec((owners, 3, depth, cols), lambda i: (0, i, 0, 0)), hbm, hbm],
        out_shape=[jax.ShapeDtypeStruct((owners, blocks, depth, cols), jnp.bfloat16)]
        + [jax.ShapeDtypeStruct((rows, width), jnp.float32)] * 2,
        scratch_shapes=[
            pltpu.VMEM((rows, width), jnp.float32),
            pltpu.VMEM((rows, width), jnp.float32),
            pltpu.VMEM((3, rows, cols), jnp.bfloat16),
            pltpu.SemaphoreType.DMA((2,)),
        ],
        compiler_params=pltpu.CompilerParams(vmem_limit_bytes=62 * 2**20),
        cost_estimate=feed_cost(rows, width, owners, tiles, depth, cols, 9),
        name="feed_all",
    )(unit, unit_t, cot, cot_t, weights, *old)


def feed_last_kernel(
    unit_hbm, unit_t_hbm, cots_hbm, cot_t_hbm, weight_hbm, old_two_hbm, old_out_hbm, own_ref,
    inverse_ref, out_t_ref, back_ref, _,
    late_ref, ffn_ref, d_middle_ref, d_sent_ref,
    grad_ref, out_grad_ref, unit_ref, turned_ref, cots_ref, weight_ref, two_ref, sum_ref, act_ref, pieces_ref, slots_ref,
    stats_ref, stat_slots_ref, d_pieces_ref,
    load, sends, recvs, g_sends, g_recvs,
):
    col = lax.axis_index("col")
    rows, width = unit_ref.shape
    count, _, piece = pieces_ref.shape
    owners, _, _, depth, cols = weight_ref.shape
    heads, _, size = back_ref.shape
    tile = weight_hbm.shape[1] - 1
    extra = late_ref.shape[1] - 3 - heads * size // cols

    def fetch(i, source, target):
        copy = pltpu.make_async_copy(source, target, load.at[i])
        copy.start()
        return copy

    loads = [
        fetch(0, unit_hbm, unit_ref), fetch(1, weight_hbm.at[:, pl.ds(tile, 1)], weight_ref), fetch(2, cots_hbm, cots_ref),
        fetch(3, old_two_hbm, two_ref), fetch(4, unit_t_hbm, turned_ref.at[0]),
        fetch(5, cot_t_hbm, turned_ref.at[1]), fetch(6, old_out_hbm.at[: rows // 4], sum_ref),
    ]
    greet_cols(count)
    for i in range(4):
        loads[i].wait()
    feed_front(unit_ref, cots_ref, weight_ref, two_ref, act_ref)
    parts = 2
    span = rows // parts
    moves, gathers = [], []
    for p in range(parts):
        split_rows(two_ref, unit_ref, pieces_ref, stats_ref, p * span, span)
        moves.append(
            Scatter(pieces_ref, slots_ref, stats_ref, stat_slots_ref, pl.ds(p * span, span),
                    sends.at[p], recvs.at[p])
        )
        moves[p].start()
        own = d_pieces_ref.at[col]
        gathers.append(
            Gather(
                halves(own, p * span, span),
                lambda c, p=p: halves(d_pieces_ref.at[c], p * span, span),
                g_sends.at[p], g_recvs.at[p], None,
            )
        )
    quarter = rows // 4
    down_weight = weight_ref[:, 0, 2].reshape(width, cols)
    for p in range(4):
        here = pl.ds(p * quarter, quarter)
        loads[6 + p].wait()
        sum_ref[...] += matmul_nt(act_ref[0, here, :], down_weight)
        for c in range(count):
            ffn_ref[c, here, :] = sum_ref[:, c * piece : (c + 1) * piece].astype(jnp.bfloat16)
        if p < 3:
            loads.append(fetch(7 + p, old_out_hbm.at[pl.ds((p + 1) * quarter, quarter)], sum_ref))
    for i in range(4, 6):
        loads[i].wait()
    feed_rear(turned_ref.at[0], turned_ref.at[1], grad_ref, act_ref)
    stores = [fetch(10, grad_ref, late_ref.at[:, pl.ds(extra, 3)])]
    own_cot = cots_ref.at[col]
    for p in range(parts):
        moves[p].receive()

        def middle_part(here):
            d_middle = own_cot[here, :].astype(jnp.float32) + normed_grad(
                two_ref, slots_ref, stats_ref, stat_slots_ref, own_ref, inverse_ref, here, width, col
            )
            d_middle_ref[here, :] = d_middle
            d_pieces_ref[col, here, :] = d_middle.astype(jnp.bfloat16)

        each_rows(p * span, span, 128, middle_part)
        gathers[p].start()
    for p in range(parts):
        gathers[p].forward()
        gathers[p].receive()
        here = pl.ds(p * span, span)
        d_attended = matmul(d_pieces_ref[0, here, :], out_t_ref[:piece, :])
        for c in range(1, count):
            d_attended += matmul(
                d_pieces_ref[c, here, :], out_t_ref[c * piece : (c + 1) * piece, :]
            )
        for h in range(heads):
            d_sent_ref[h, here, :] = d_attended[:, h * size : (h + 1) * size].astype(jnp.bfloat16)
    per_piece = piece // depth
    for owner in range(owners):
        at = (owner % per_piece) * depth
        d_branch = d_pieces_ref[owner // per_piece, :, at : at + depth]
        for h in range(heads):
            at = (h * size) % cols
            out_grad_ref[owner, h * size // cols, at : at + size, :] = lax.dot_general(
                back_ref[h], d_branch, (((0,), (0,)), ((), ())), preferred_element_type=jnp.float32
            ).astype(jnp.bfloat16)
    stores.append(fetch(11, out_grad_ref, late_ref.at[:, pl.ds(extra + 3, heads * size // cols)]))
    for one in stores:
        one.wait()
    for one in moves + gathers:
        one.finish()


def feed_last(unit, unit_t, cots, cot_t, weights, old, own, inverse, out_t, back, late):
    rows, width = unit.shape
    count, _, piece = cots.shape
    owners, _, _, depth, cols = weights.shape
    heads, _, size = back.shape
    hbm = pl.BlockSpec(memory_space=pl.ANY)
    vmem = pl.BlockSpec(memory_space=pltpu.VMEM)
    dma = pltpu.SemaphoreType.DMA
    shape = jax.ShapeDtypeStruct
    return pl.pallas_call(
        feed_last_kernel,
        in_specs=[hbm] * 7 + [vmem] * 4 + [hbm],
        out_specs=[hbm] + [vmem] * 3,
        input_output_aliases={11: 0},
        out_shape=[
            shape(late.shape, jnp.bfloat16),
            shape((count, rows, piece), jnp.bfloat16),
            shape((rows, piece), jnp.float32),
            shape((heads, rows, size), jnp.bfloat16),
        ],
        scratch_shapes=[
            pltpu.VMEM((owners, 3, depth, cols), jnp.bfloat16),
            pltpu.VMEM((owners, heads * size // cols, cols, depth), jnp.bfloat16),
            pltpu.VMEM((rows, width), jnp.bfloat16),
            pltpu.VMEM((2, width, rows), jnp.bfloat16),
            pltpu.VMEM((count, rows, piece), jnp.bfloat16),
            pltpu.VMEM((owners, 1, 3, depth, cols), jnp.bfloat16),
            pltpu.VMEM((rows, width), jnp.float32),
            pltpu.VMEM((rows // 4, width), jnp.float32),
            pltpu.VMEM((3, rows, cols), jnp.bfloat16),
            pltpu.VMEM((count, rows, piece), jnp.bfloat16),
            pltpu.VMEM((count - 1, rows, piece), jnp.bfloat16),
            pltpu.VMEM((8, rows), jnp.float32),
            pltpu.VMEM((count - 1, 8, rows), jnp.float32),
            pltpu.VMEM((count, rows, piece), jnp.bfloat16),
            dma((12,)), dma((2, 2, count - 1)), dma((2, 2, count - 1)), dma((2, 6)), dma((2, 6)),
        ],
        compiler_params=pltpu.CompilerParams(
            vmem_limit_bytes=63 * 2**20 + 2**19, collective_id=6, has_side_effects=True
        ),
        cost_estimate=pl.CostEstimate(
            flops=18 * rows * width * cols, bytes_accessed=100 * rows * width,
            transcendentals=rows * cols,
        ),
        name="feed_last",
    )(unit, unit_t, cots, cot_t, weights, *old, own, inverse, out_t, back, late)


def group_tables(lengths, group):
    row_lengths = lax.dynamic_slice_in_dim(lengths, group, 1, 0)[0]
    local_index = jnp.arange(GROUP_LEN, dtype=jnp.int32)
    seg_ends = jnp.cumsum(row_lengths)
    seg_starts = seg_ends - row_lengths
    after_prompt = local_index - PROMPT
    inside = (after_prompt[:, None] >= seg_starts[None, :]) & (
        after_prompt[:, None] < seg_ends[None, :]
    )
    start = jnp.sum(jnp.where(inside, seg_starts[None, :], 0), axis=1)
    in_prompt = local_index < PROMPT
    start_row = jnp.where(in_prompt, 0, PROMPT + start)
    position = jnp.where(in_prompt, local_index, PROMPT + after_prompt - start)
    half = HEAD // 2
    frequency = jnp.exp(
        -math.log(rope_base) * (2.0 * jnp.arange(half, dtype=jnp.float32) / HEAD)
    )
    angles = position.astype(jnp.float32)[:, None] * frequency[None, :]
    cosine, sine = jnp.cos(angles), jnp.sin(angles)
    return (
        start_row.reshape(GROUP_LEN // BLOCK, 1, BLOCK),
        jnp.concatenate([cosine, cosine], axis=1),
        jnp.concatenate([sine, -sine], axis=1),
    )


def fast_body(
    inputs,
    cotangent,
    lengths,
    query_key_value_weight,
    out_weight,
    gate_weight,
    up_weight,
    down_weight,
):
    tok_rows, part_width = inputs.shape
    col_count = lax.axis_size("col")
    col_index = lax.axis_index("col")
    row_index = lax.axis_index("row")
    span = GROUP_LEN // tok_rows
    groups_here = lax.axis_size("row") // span
    heads_here = part_width // HEAD
    place = row_index // groups_here
    group = row_index % groups_here
    depth = gate_weight.shape[0]
    hidden_here = gate_weight.shape[1]
    tiles = hidden_here // min(256, depth)
    tile = hidden_here // tiles

    def gather(shard, after=None):
        if after is not None:
            shard, after = tied(shard, after)
        return lax.all_gather(shard, "row"), after

    def tied(value, *others):
        return lax.optimization_barrier((value, *others))

    mixed = jnp.concatenate([query_key_value_weight.transpose(1, 0, 2), out_weight.T[None]])
    weights, _ = gather(mixed)
    packed = jnp.stack([gate_weight, up_weight, down_weight.T]).reshape(3, depth, tiles, tile)
    packed = packed.transpose(2, 0, 1, 3)
    first = max(1, tiles * 5 // 8)
    pieces, cots, normed_one, unit_one_t, unit_one, inverse_one = enter(
        inputs, cotangent, col_count
    )
    normed_one, weights, lengths = tied(normed_one, weights, lengths)
    feed_one, weights = gather(packed[:first], weights)
    start_rows, cosine, sine = lax.optimization_barrier(group_tables(lengths, group))
    own_cos = lax.dynamic_slice_in_dim(
        cosine.reshape(span, tok_rows, HEAD), place, 1, 0
    )[0]
    own_sin = lax.dynamic_slice_in_dim(sine.reshape(span, tok_rows, HEAD), place, 1, 0)[0]

    sent = project(normed_one, weights, own_cos, own_sin)
    out_rows_t = weights[:, 3].reshape(-1, part_width)
    back, held, attended_head, lse, out_t = attend(
        sent, start_rows, out_rows_t, groups_here, col_count
    )
    back, feed_one = tied(back, feed_one)
    feed_two, feed_one = gather(packed[first:], feed_one)
    normed_two, unit_t, middle, unit_two, inverse_two = branch(back, out_t, pieces)
    cot_t = cots.transpose(0, 2, 1).reshape(-1, tok_rows)
    rows_two = (normed_two, unit_t, cots, cot_t)

    def owned(part):
        return lax.psum_scatter(part, "row", scatter_dimension=0, tiled=True)[0]

    grads_one, *sums = feed_all(*rows_two, feed_one, first, (), 3 * first)
    sums[0], grads_one, feed_two = tied(sums[0], grads_one, feed_two)
    grads_one = owned(grads_one)
    rest = tiles - first - 1
    blocks = 3 * (rest + 1) + part_width // tile
    late, *sums = feed_all(*rows_two, feed_two, rest, sums, blocks)
    late, ffn_pieces, d_middle, d_sent = feed_last(
        *rows_two, feed_two, sums, unit_two, inverse_two, out_rows_t, back, late
    )
    d_sent, grads_one = tied(d_sent, grads_one)
    late, grads_one = tied(late, grads_one)
    late = owned(late)
    d_raw, ffn_others = attend_back(
        d_sent, held, attended_head, lse, start_rows, cosine, sine, ffn_pieces, groups_here
    )
    projection_part = project_grad(unit_one_t, d_raw, weights.shape[0])
    projection_part, late, d_raw = tied(projection_part, late, d_raw)
    own_grads = owned(projection_part)
    input_grad = leave(
        d_raw, weights, normed_one, unit_one, inverse_one, d_middle, col_count
    )
    own_ffn = lax.dynamic_slice_in_dim(ffn_pieces, col_index, 1, 0)[0]
    output = middle + own_ffn.astype(jnp.float32) + jnp.sum(ffn_others.astype(jnp.float32), axis=0)
    output = output.astype(jnp.bfloat16)
    qkv_grad = own_grads.astype(jnp.float32).transpose(1, 0, 2)
    out_grad = late[3 * (rest + 1) :].reshape(part_width, depth).astype(jnp.float32)
    grads = jnp.concatenate([grads_one, late[: 3 * (rest + 1)]]).astype(jnp.float32)
    grads = grads.reshape(tiles, 3, depth, tile).transpose(1, 2, 0, 3).reshape(3, depth, hidden_here)
    return (output, input_grad, qkv_grad, out_grad, grads[0], grads[1], grads[2].T)


def body(
    inputs,
    cotangent,
    lengths,
    query_key_value_weight,
    out_weight,
    gate_weight,
    up_weight,
    down_weight,
):
    tok_rows = inputs.shape[0]
    part_width = inputs.shape[1]
    col_count = lax.axis_size("col")
    col_index = lax.axis_index("col")
    row_index = lax.axis_index("row")
    full_width = float(part_width * col_count)
    group_span = GROUP_LEN // tok_rows
    groups_here = lax.axis_size("row") // group_span
    head_size = HEAD
    heads_here = part_width // head_size
    score_scale = head_size ** (-0.5)
    block_place = row_index // groups_here
    full_inputs, full_cotangent = (
        lax.all_gather(inputs, "col", axis=1, tiled=True),
        lax.all_gather(cotangent, "col", axis=1, tiled=True),
    )
    projection_full_rows, out_full, gate_full, up_full, down_full = (
        lax.all_gather(query_key_value_weight, "row", axis=0, tiled=True),
        lax.all_gather(out_weight, "row", axis=1, tiled=True),
        lax.all_gather(gate_weight, "row", axis=0, tiled=True),
        lax.all_gather(up_weight, "row", axis=0, tiled=True),
        lax.all_gather(down_weight, "row", axis=1, tiled=True),
    )
    unit_one, inverse_one = normalize_rows(full_inputs.astype(jnp.float32))
    first_normed_input = unit_one.astype(jnp.bfloat16)
    raw_projection_output = jnp.einsum(
        "cu,ufk->cfk", first_normed_input, projection_full_rows, preferred_element_type=jnp.float32
    )
    raw_projection_output = raw_projection_output.reshape(tok_rows, 3, heads_here, head_size)
    own_meta = token_layout(lengths, row_index, groups_here, tok_rows)
    cosine, sine = rotation_angles(own_meta[3], head_size)
    queries = rotate(raw_projection_output[:, 0], cosine, sine, False).astype(jnp.bfloat16)
    key_rows = rotate(raw_projection_output[:, 1], cosine, sine, False).astype(jnp.bfloat16)
    value_rows = raw_projection_output[:, 2].astype(jnp.bfloat16)
    pieces = [(key_rows, value_rows)]
    for shift_by in range(1, group_span):
        pieces.append(passed_along((key_rows, value_rows), "row", shift_by * groups_here))
    visibility = [
        visible_mask(
            own_meta,
            token_layout(lengths, row_index - shift_by * groups_here, groups_here, tok_rows),
        )
        for shift_by in range(group_span)
    ]
    live_piece = [shift_by <= block_place for shift_by in range(group_span)]
    first_scores = score_block(queries, pieces[0][0], visibility[0], score_scale)
    top_rows = jnp.max(first_scores, axis=-1, keepdims=True)
    total_rows = jnp.sum(jnp.exp(first_scores - top_rows), axis=-1, keepdims=True)
    for shift_by in range(1, group_span):

        def add_stats(carry, shift_by=shift_by):
            old_top, old_total = carry
            scores = score_block(queries, pieces[shift_by][0], visibility[shift_by], score_scale)
            new_top = jnp.maximum(old_top, jnp.max(scores, axis=-1, keepdims=True))
            new_total = old_total * jnp.exp(old_top - new_top) + jnp.sum(
                jnp.exp(scores - new_top), axis=-1, keepdims=True
            )
            return (new_top, new_total)

        top_rows, total_rows = lax.cond(
            live_piece[shift_by], add_stats, lambda carry: carry, (top_rows, total_rows)
        )
    log_total = top_rows + jnp.log(total_rows)
    attended = jnp.zeros((tok_rows, heads_here, head_size), jnp.float32)
    for shift_by in range(group_span):

        def add_values(total, shift_by=shift_by):
            scores = score_block(queries, pieces[shift_by][0], visibility[shift_by], score_scale)
            probs_low = jnp.exp(scores - log_total).astype(jnp.bfloat16)
            return total + jnp.einsum(
                "hqk,khd->qhd", probs_low, pieces[shift_by][1], preferred_element_type=jnp.float32
            )

        attended = lax.cond(live_piece[shift_by], add_values, lambda total: total, attended)
    attended_flat = attended.reshape(tok_rows, part_width).astype(jnp.bfloat16)
    branch_terms = jnp.dot(attended_flat, out_full, preferred_element_type=jnp.float32)
    branch_full = lax.psum(branch_terms, "col")
    middle_full = full_inputs.astype(jnp.float32) + branch_full
    middle = lax.dynamic_slice_in_dim(middle_full, col_index * part_width, part_width, 1)
    unit_two, inverse_two = normalize_rows(middle_full)
    normed_two = unit_two.astype(jnp.bfloat16)
    gate = jnp.dot(normed_two, gate_full, preferred_element_type=jnp.float32)
    up_proj = jnp.dot(normed_two, up_full, preferred_element_type=jnp.float32)
    sigmoid_gate = jax.nn.sigmoid(gate)
    silu_gate = gate * sigmoid_gate
    hidden = (silu_gate * up_proj).astype(jnp.bfloat16)
    ffn_terms = jnp.dot(hidden, down_full, preferred_element_type=jnp.float32)
    ffn_part = lax.psum_scatter(
        ffn_terms.astype(jnp.bfloat16), "col", scatter_dimension=1, tiled=True
    ).astype(jnp.float32)
    output = (middle + ffn_part).astype(jnp.bfloat16)
    projection_full_rows, out_full, gate_full, up_full, down_full = (
        lax.all_gather(query_key_value_weight, "row", axis=0, tiled=True),
        lax.all_gather(out_weight, "row", axis=1, tiled=True),
        lax.all_gather(gate_weight, "row", axis=0, tiled=True),
        lax.all_gather(up_weight, "row", axis=0, tiled=True),
        lax.all_gather(down_weight, "row", axis=1, tiled=True),
    )
    d_hidden = jnp.einsum(
        "td,fd->tf", full_cotangent, down_full, preferred_element_type=jnp.float32
    )
    down_part = jnp.einsum("tf,td->fd", hidden, full_cotangent, preferred_element_type=jnp.float32)
    d_gate = (d_hidden * up_proj * sigmoid_gate * (1.0 + gate * (1.0 - sigmoid_gate))).astype(
        jnp.bfloat16
    )
    d_up = (d_hidden * silu_gate).astype(jnp.bfloat16)
    gate_part = jnp.einsum("td,tf->df", normed_two, d_gate, preferred_element_type=jnp.float32)
    up_part = jnp.einsum("td,tf->df", normed_two, d_up, preferred_element_type=jnp.float32)
    d_normed_two = jnp.einsum(
        "tf,df->td", d_gate, gate_full, preferred_element_type=jnp.float32
    ) + jnp.einsum("tf,df->td", d_up, up_full, preferred_element_type=jnp.float32)
    grad_two, sum_two, cross_two = (
        lax.psum_scatter(
            d_normed_two.astype(jnp.bfloat16), "col", scatter_dimension=1, tiled=True
        ).astype(jnp.float32),
        lax.psum_scatter(
            spread_cols(jnp.sum(d_normed_two, axis=1), col_count).astype(jnp.bfloat16),
            "col",
            scatter_dimension=1,
            tiled=True,
        ).astype(jnp.float32),
        lax.psum_scatter(
            spread_cols(jnp.sum(d_normed_two * unit_two, axis=1), col_count).astype(jnp.bfloat16),
            "col",
            scatter_dimension=1,
            tiled=True,
        ).astype(jnp.float32),
    )
    unit_two_here = lax.dynamic_slice_in_dim(unit_two, col_index * part_width, part_width, 1)
    d_middle = cotangent.astype(jnp.float32) + normalize_back(
        grad_two, sum_two, cross_two, unit_two_here, inverse_two, full_width
    )
    d_branch = d_middle.astype(jnp.bfloat16)
    d_branch_full = lax.all_gather(d_branch, "col", axis=1, tiled=True)
    out_part = jnp.einsum(
        "tc,td->cd", attended_flat, d_branch_full, preferred_element_type=jnp.float32
    )
    d_attended = jnp.einsum(
        "td,cd->tc", d_branch_full, out_full, preferred_element_type=jnp.float32
    )
    d_attended = d_attended.astype(jnp.bfloat16).reshape(tok_rows, heads_here, head_size)
    delta_rows = jnp.zeros((heads_here, tok_rows, 1), jnp.float32)
    for shift_by in range(group_span):

        def add_delta(total, shift_by=shift_by):
            scores = score_block(queries, pieces[shift_by][0], visibility[shift_by], score_scale)
            probs_full = jnp.exp(scores - log_total)
            d_probs = jnp.einsum(
                "qhd,khd->hqk", d_attended, pieces[shift_by][1], preferred_element_type=jnp.float32
            )
            return total + jnp.sum(probs_full * d_probs, axis=-1, keepdims=True)

        delta_rows = lax.cond(live_piece[shift_by], add_delta, lambda total: total, delta_rows)
    zero_rows = jnp.zeros((tok_rows, heads_here, head_size), jnp.float32)
    d_queries = zero_rows
    for shift_by in range(group_span):

        def piece_grads(query_total, shift_by=shift_by):
            key_part, value_part = pieces[shift_by]
            scores = score_block(queries, key_part, visibility[shift_by], score_scale)
            probs_full = jnp.exp(scores - log_total)
            d_probs = jnp.einsum(
                "qhd,khd->hqk", d_attended, value_part, preferred_element_type=jnp.float32
            )
            d_scores = (probs_full * (d_probs - delta_rows)).astype(jnp.bfloat16)
            query_total = (
                query_total
                + jnp.einsum("hqk,khd->qhd", d_scores, key_part, preferred_element_type=jnp.float32)
                * score_scale
            )
            d_key_part = (
                jnp.einsum("hqk,qhd->khd", d_scores, queries, preferred_element_type=jnp.float32)
                * score_scale
            )
            d_value_part = jnp.einsum(
                "hqk,qhd->khd",
                probs_full.astype(jnp.bfloat16),
                d_attended,
                preferred_element_type=jnp.float32,
            )
            return (query_total, d_key_part, d_value_part)

        d_queries, d_key_part, d_value_part = lax.cond(
            live_piece[shift_by],
            piece_grads,
            lambda query_total: (query_total, zero_rows, zero_rows),
            d_queries,
        )
        if shift_by == 0:
            d_keys = d_key_part
            d_values = d_value_part
        else:
            back_keys, back_values = (
                passed_along(
                    d_key_part.astype(jnp.bfloat16), "row", -shift_by * groups_here
                ).astype(d_key_part.dtype),
                passed_along(
                    d_value_part.astype(jnp.bfloat16), "row", -shift_by * groups_here
                ).astype(d_value_part.dtype),
            )
            d_keys = d_keys + back_keys
            d_values = d_values + back_values
    raw_score_gradient = jnp.stack(
        [rotate(d_queries, cosine, sine, True), rotate(d_keys, cosine, sine, True), d_values],
        axis=1,
    )
    raw_score_gradient = raw_score_gradient.reshape(tok_rows, 3, part_width).astype(jnp.bfloat16)
    projection_part_rows = jnp.einsum(
        "lo,lbw->obw", first_normed_input, raw_score_gradient, preferred_element_type=jnp.float32
    )
    first_normed_gradient = jnp.einsum(
        "xzq,vzq->xv", raw_score_gradient, projection_full_rows, preferred_element_type=jnp.float32
    )
    grad_one, sum_one, cross_one = (
        lax.psum_scatter(
            first_normed_gradient.astype(jnp.bfloat16), "col", scatter_dimension=1, tiled=True
        ).astype(jnp.float32),
        lax.psum_scatter(
            spread_cols(jnp.sum(first_normed_gradient, axis=1), col_count).astype(jnp.bfloat16),
            "col",
            scatter_dimension=1,
            tiled=True,
        ).astype(jnp.float32),
        lax.psum_scatter(
            spread_cols(jnp.sum(first_normed_gradient * unit_one, axis=1), col_count).astype(
                jnp.bfloat16
            ),
            "col",
            scatter_dimension=1,
            tiled=True,
        ).astype(jnp.float32),
    )
    unit_one_here = lax.dynamic_slice_in_dim(unit_one, col_index * part_width, part_width, 1)
    input_grad = d_middle + normalize_back(
        grad_one, sum_one, cross_one, unit_one_here, inverse_one, full_width
    )
    owned_grads = (
        lax.psum_scatter(
            projection_part_rows.astype(jnp.bfloat16), "row", scatter_dimension=0, tiled=True
        ).astype(jnp.float32),
        lax.psum_scatter(
            out_part.astype(jnp.bfloat16), "row", scatter_dimension=1, tiled=True
        ).astype(jnp.float32),
        lax.psum_scatter(
            gate_part.astype(jnp.bfloat16), "row", scatter_dimension=0, tiled=True
        ).astype(jnp.float32),
        lax.psum_scatter(
            up_part.astype(jnp.bfloat16), "row", scatter_dimension=0, tiled=True
        ).astype(jnp.float32),
        lax.psum_scatter(
            down_part.astype(jnp.bfloat16), "row", scatter_dimension=1, tiled=True
        ).astype(jnp.float32),
    )
    return (
        output,
        input_grad,
        owned_grads[0],
        owned_grads[1],
        owned_grads[2],
        owned_grads[3],
        owned_grads[4],
    )


def step(inputs, *rest):
    span = GROUP_LEN // inputs.shape[0]
    heads_here = inputs.shape[1] // HEAD
    fast = heads_here == span and lax.axis_size("col") == 4
    return (fast_body if fast else body)(inputs, *rest)


def solution(mesh):
    placed = (
        P("row", "col"),
        P("row", "col"),
        P(),
        P("row", None, "col"),
        P("col", "row"),
        P("row", "col"),
        P("row", "col"),
        P("col", "row"),
    )
    return jax.shard_map(
        step,
        mesh=mesh,
        in_specs=placed,
        out_specs=(
            P("row", "col"),
            P("row", "col"),
            P("row", None, "col"),
            P("col", "row"),
            P("row", "col"),
            P("row", "col"),
            P("col", "row"),
        ),
        check_vma=False,
    )
```

```python
import functools
import math

import jax
import jax.numpy as jnp
from jax import lax
from jax.experimental import pallas as pl
from jax.experimental.pallas import tpu as pltpu
from jax.sharding import PartitionSpec as P

HEAD = 128
PROMPT = 2048
GROUP_LEN = 4096


rope_base = 10000.0
norm_eps = 1e-05
masked_score = -1e30


def passed_along(shard, axis, by):
    size = lax.axis_size(axis)
    pairs = [(i, i + by) for i in range(size) if 0 <= i + by < size]
    return lax.ppermute(shard, axis, pairs)


def normalize_rows(values):
    centre = values - jnp.mean(values, axis=-1, keepdims=True)
    spread = jnp.mean(centre * centre, axis=-1, keepdims=True)
    inverse = lax.rsqrt(spread + norm_eps)
    return (centre * inverse, inverse)


def normalize_back(grad_rows, sum_grad, sum_cross, unit_rows, inverse, row_width):
    return inverse * (grad_rows - sum_grad / row_width - unit_rows * (sum_cross / row_width))


def spread_cols(values, copies):
    return jnp.broadcast_to(values[:, None], (values.shape[0], copies))


def token_layout(lengths, source_row, groups_count, row_count):
    valid_source = source_row >= 0
    safe_source = jnp.maximum(source_row, 0)
    group_id = jnp.where(valid_source, safe_source % groups_count, -1)
    place_here = safe_source // groups_count
    safe_group = jnp.clip(group_id, 0, lengths.shape[0] - 1)
    row_lengths = lax.dynamic_slice_in_dim(lengths, safe_group, 1, 0)[0]
    local_index = place_here * row_count + jnp.arange(row_count, dtype=jnp.int32)
    after_prompt = local_index - PROMPT
    seg_ends = jnp.cumsum(row_lengths)
    in_prompt = local_index < PROMPT
    counted = jnp.sum((after_prompt[:, None] >= seg_ends[None, :]).astype(jnp.int32), axis=1)
    segment = jnp.where(in_prompt, 0, 1 + counted)
    seg_starts = seg_ends - row_lengths
    picked = (segment - 1)[:, None] == jnp.arange(row_lengths.shape[0], dtype=jnp.int32)[None, :]
    seg_start = jnp.sum(jnp.where(picked, seg_starts[None, :], 0), axis=1)
    position = jnp.where(in_prompt, local_index, PROMPT + after_prompt - seg_start)
    return (group_id, local_index, segment, position)


def rotation_angles(position, head_size):
    half_size = head_size // 2
    frequency = jnp.exp(
        -math.log(rope_base) * (2.0 * jnp.arange(half_size, dtype=jnp.float32) / head_size)
    )
    angles = position.astype(jnp.float32)[:, None] * frequency[None, :]
    return (jnp.cos(angles)[:, None, :], jnp.sin(angles)[:, None, :])


def rotate(values, cosine, sine, inverse_turn):
    half_size = values.shape[-1] // 2
    first_half = values[..., :half_size]
    second_half = values[..., half_size:]
    if inverse_turn:
        sine = -sine
    return jnp.concatenate(
        [first_half * cosine - second_half * sine, second_half * cosine + first_half * sine],
        axis=-1,
    )


def visible_mask(query_meta, key_meta):
    query_group, query_index, query_segment, query_position = query_meta
    key_group, key_index, key_segment, key_position = key_meta
    causal = key_index[None, :] <= query_index[:, None]
    shared = (key_segment[None, :] == 0) | (key_segment[None, :] == query_segment[:, None])
    return (query_group == key_group) & causal & shared


def score_block(queries, key_part, allowed, score_scale):
    raw_scores = (
        jnp.einsum("qhd,khd->hqk", queries, key_part, preferred_element_type=jnp.float32)
        * score_scale
    )
    return jnp.where(allowed[None], raw_scores, masked_score)


BLOCK = 512
log2e = 1.4426950408889634


def turn(values, cosine, sine):
    return values * cosine + pltpu.roll(values, values.shape[1] // 2, 1) * sine


def block_mask(key_block, query_block, start_row):
    key_index = key_block * BLOCK + lax.broadcasted_iota(jnp.int32, (BLOCK, BLOCK), 0)
    query_index = query_block * BLOCK + lax.broadcasted_iota(jnp.int32, (BLOCK, BLOCK), 1)
    return (key_index <= query_index) & (key_index >= start_row)


def each_block(block, visit):
    prompt_blocks = PROMPT // BLOCK

    def whole(j, carry):
        visit(j, False)
        return carry

    lax.fori_loop(0, jnp.minimum(block, prompt_blocks), whole, 0)

    @pl.when(block > prompt_blocks)
    def _():
        visit(block - 1, True)

    visit(block, True)


MESH = pl.DeviceIdType.MESH


def place_of(place, groups_here):
    row = lax.axis_index("row")
    return (place * groups_here + lax.rem(row, groups_here), lax.axis_index("col"))


def send(source, target, send_sem, recv_sem, device):
    return pltpu.make_async_remote_copy(
        src_ref=source, dst_ref=target, send_sem=send_sem, recv_sem=recv_sem,
        device_id=device, device_id_type=MESH,
    )


def block_rows(block):
    return pl.ds(pl.multiple_of(block * BLOCK, BLOCK), BLOCK)


def col_device(by):
    return (lax.axis_index("row"), lax.axis_index("col") ^ by)


def greet_cols(count):
    barrier = pltpu.get_barrier_semaphore()
    for by in range(1, count):
        pl.semaphore_signal(barrier, inc=1, device_id=col_device(by), device_id_type=MESH)
    pl.semaphore_wait(barrier, count - 1)


class Gather:
    def __init__(self, source, slots, sends, recvs, local):
        me = lax.axis_index("col")
        a, b = source[0], source[1]
        self.own = []
        if local is not None:
            self.own = [
                pltpu.make_async_copy(a, slots(me)[0], local.at[0]),
                pltpu.make_async_copy(b, slots(me)[1], local.at[1]),
            ]

        def copy(i, what, where, by):
            return send(what, where, sends.at[i], recvs.at[i], col_device(by))

        self.first = [
            copy(0, a, slots(me)[0], 1),
            copy(3, b, slots(me)[1], 2),
            copy(1, b, slots(me)[1], 1),
            copy(2, a, slots(me)[0], 2),
        ]
        across, along = me ^ 1, me ^ 2
        self.second = [
            copy(4, slots(across)[0], slots(across)[0], 2),
            copy(5, slots(along)[1], slots(along)[1], 1),
        ]

    def start(self):
        for one in self.own + self.first:
            one.start()

    def forward(self):
        self.first[0].wait_recv()
        self.second[0].start()
        self.first[1].wait_recv()
        self.second[1].start()

    def receive(self):
        for one in self.first[2:] + self.second:
            one.wait_recv()
        for one in self.own:
            one.wait()

    def finish(self):
        for one in self.first + self.second:
            one.wait_send()


def halves(ref, start, size):
    half = size // 2
    return ref.at[pl.ds(start, half)], ref.at[pl.ds(start + half, half)]


def greet_all(me, span, groups_here, count, others=0):
    barrier = pltpu.get_barrier_semaphore()
    for by in range(1, span):
        pl.semaphore_signal(
            barrier, inc=1, device_id=place_of(lax.rem(me + by, span), groups_here), device_id_type=MESH
        )
    for by in range(1, count):
        pl.semaphore_signal(barrier, inc=1, device_id=col_device(by), device_id_type=MESH)
    pl.semaphore_wait(barrier, span + count - 2 + others)


def attend_kernel(
    groups_here, sent_ref, start_ref, rider_ref, back_ref, held_ref, o_ref, lse_ref, riders_ref,
    qkv_ref, top_ref, total_ref, sum_ref,
    in_send, in_recv, out_send, out_recv, keep_sem, own_sem, ride_send, ride_recv, ride_local,
):
    span, _, tokens, _ = sent_ref.shape
    me = lax.axis_index("row") // groups_here
    blocks = start_ref.shape[0]
    per_place = tokens // BLOCK
    scale = HEAD**-0.5 * log2e
    greet_all(me, span, groups_here, riders_ref.shape[0])
    half = rider_ref.shape[0] // 2
    ride = Gather(
        (rider_ref.at[:half, 3], rider_ref.at[half:, 3]),
        lambda c: (riders_ref.at[c, :half], riders_ref.at[c, half:]),
        ride_send, ride_recv, ride_local,
    )

    def qkv_copy(by):
        peer = lax.rem(me + by, span)
        return send(
            sent_ref.at[peer], qkv_ref.at[:, pl.ds(pl.multiple_of(me * tokens, tokens), tokens)],
            in_send.at[by], in_recv.at[by], place_of(peer, groups_here),
        )

    own_rows = pl.ds(pl.multiple_of(me * tokens, tokens), tokens)
    own_copy = pltpu.make_async_copy(sent_ref.at[me], qkv_ref.at[:, own_rows], in_recv.at[0])
    own_copy.start()
    for by in range(1, span):
        qkv_copy(by).start()
    ride.start()

    def out_copy(block):
        to = block // per_place
        half = lax.rem(block, per_place)
        by = lax.rem(to - me + span, span)
        return send(
            o_ref.at[block_rows(block)], back_ref.at[me, block_rows(half)],
            out_send.at[block], out_recv.at[by, half], place_of(to, groups_here),
        )

    def own_out(block):
        return pltpu.make_async_copy(
            o_ref.at[block_rows(block)],
            back_ref.at[me, block_rows(lax.rem(block, per_place))],
            own_sem.at[lax.rem(block, per_place)],
        )

    def keep_copy(place):
        rows = pl.ds(pl.multiple_of(place * tokens, tokens), tokens)
        return pltpu.make_async_copy(qkv_ref.at[:, rows], held_ref.at[:, rows], keep_sem.at[place])

    def one_block(block, carry):
        place = block // per_place

        @pl.when(lax.rem(block, per_place) == 0)
        def _():
            @pl.when(place == me)
            def _():
                own_copy.wait()

            for by in range(1, span):

                @pl.when(lax.rem(place + by, span) == me)
                def _():
                    qkv_copy(by).wait_recv()

            keep_copy(place).start()

        top_ref[...] = jnp.full_like(top_ref, masked_score)
        total_ref[...] = jnp.zeros_like(total_ref)
        sum_ref[...] = jnp.zeros_like(sum_ref)
        queries = qkv_ref[0, block_rows(block), :]
        start_row = start_ref[block]

        def visit(j, masked):
            rows = block_rows(j)
            scores = scale * matmul_nt(qkv_ref[1, rows, :], queries)
            if masked:
                scores = jnp.where(block_mask(j, block, start_row), scores, masked_score)
            old_top = top_ref[...]
            new_top = jnp.maximum(old_top, jnp.max(scores, axis=0, keepdims=True))
            shrink = jnp.exp2(old_top - new_top)
            probs = jnp.exp2(scores - new_top)
            if masked:
                probs = jnp.where(scores > 0.5 * masked_score, probs, 0.0)
            total_ref[...] = total_ref[...] * shrink + jnp.sum(probs, axis=0, keepdims=True)
            sum_ref[...] = sum_ref[...] * shrink + lax.dot_general(
                qkv_ref[2, rows, :],
                probs.astype(jnp.bfloat16),
                (((0,), (0,)), ((), ())),
                preferred_element_type=jnp.float32,
            )
            top_ref[...] = new_top

        each_block(block, visit)
        total = total_ref[...]
        o_ref[block_rows(block), :] = (sum_ref[...] / total).T.astype(jnp.bfloat16)
        lse_ref[block] = top_ref[...] + jnp.log2(total)

        @pl.when(place == me)
        def _():
            own_out(block).start()

        @pl.when(place != me)
        def _():
            out_copy(block).start()

        @pl.when(block == blocks // 2)
        def _():
            ride.forward()

        return carry

    lax.fori_loop(0, blocks, one_block, 0)
    ride.receive()
    ride.finish()

    for by in range(1, span):
        qkv_copy(by).wait_send()

    def finish(block, carry):
        place = block // per_place

        @pl.when(place == me)
        def _():
            own_out(block).wait()

        @pl.when(place != me)
        def _():
            out_copy(block).wait_send()

        return carry

    lax.fori_loop(0, blocks, finish, 0)
    for by in range(1, span):
        for half in range(per_place):
            send(
                o_ref.at[block_rows(half)], back_ref.at[lax.rem(me - by + span, span), block_rows(half)],
                out_send.at[half], out_recv.at[by, half], place_of(me, groups_here),
            ).wait_recv()
    for place in range(span):
        keep_copy(place).wait()


def attend(sent, start_rows, rider, groups_here, count):
    span, _, tokens, size = sent.shape
    blocks = start_rows.shape[0]
    length = span * tokens
    hbm = pl.BlockSpec(memory_space=pl.ANY)
    vmem = pl.BlockSpec(memory_space=pltpu.VMEM)
    per_place = tokens // BLOCK
    dma = pltpu.SemaphoreType.DMA
    return pl.pallas_call(
        functools.partial(attend_kernel, groups_here),
        in_specs=[hbm, vmem, hbm],
        out_specs=[hbm, hbm, vmem, vmem, hbm],
        out_shape=[
            jax.ShapeDtypeStruct((span, tokens, size), jnp.bfloat16),
            jax.ShapeDtypeStruct((3, length, size), jnp.bfloat16),
            jax.ShapeDtypeStruct((length, size), jnp.bfloat16),
            jax.ShapeDtypeStruct((blocks, 1, BLOCK), jnp.float32),
            jax.ShapeDtypeStruct((count, rider.shape[0], *rider.shape[2:]), jnp.bfloat16),
        ],
        scratch_shapes=[
            pltpu.VMEM((3, length, size), jnp.bfloat16),
            pltpu.VMEM((1, BLOCK), jnp.float32),
            pltpu.VMEM((1, BLOCK), jnp.float32),
            pltpu.VMEM((size, BLOCK), jnp.float32),
            dma((span,)), dma((span,)), dma((blocks,)), dma((span, per_place)), dma((span,)),
            dma((per_place,)), dma((6,)), dma((6,)), dma((2,)),
        ],
        compiler_params=pltpu.CompilerParams(
            vmem_limit_bytes=32 * 2**20, collective_id=1, has_side_effects=True
        ),
        cost_estimate=pl.CostEstimate(
            flops=length * length * size * 2, bytes_accessed=length * size * 200,
            transcendentals=length * length // 2,
        ),
        name="attend",
    )(sent, start_rows, rider)


def attend_back_kernel(
    groups_here, d_sent_ref, qkv_ref, o_ref, lse_ref, start_ref, cos_ref, sin_ref, rider_ref,
    middle_ref, d_raw_ref, output_ref, riders_ref, own_ride_ref, do_ref, stage_ref, dq_sum, dk_sum, dv_sum,
    in_send, in_recv, q_send, q_recv, kv_send, kv_recv, own_sem, ride_send, ride_recv, ride_own,
):
    span, tokens, _ = d_sent_ref.shape
    me = lax.axis_index("row") // groups_here
    blocks = start_ref.shape[0]
    per_place = tokens // BLOCK
    after = blocks - PROMPT // BLOCK
    scale = HEAD**-0.5
    greet_all(me, span, groups_here, rider_ref.shape[0])
    ride = Scatter(
        rider_ref, riders_ref, None, None, pl.ds(0, tokens), ride_send, ride_recv
    )
    own_rows = pl.ds(pl.multiple_of(me * tokens, tokens), tokens)

    def do_copy(by):
        peer = lax.rem(me + by, span)
        return send(
            d_sent_ref.at[peer], do_ref.at[own_rows], in_send.at[by], in_recv.at[by],
            place_of(peer, groups_here),
        )

    own_copy = pltpu.make_async_copy(d_sent_ref.at[me], do_ref.at[own_rows], in_recv.at[0])
    own_copy.start()
    for by in range(1, span):
        do_copy(by).start()
    ride.start()
    own_ride = pltpu.make_async_copy(rider_ref.at[lax.axis_index("col")], own_ride_ref, ride_own)
    own_ride.start()
    dk_sum[...] = jnp.zeros_like(dk_sum)
    dv_sum[...] = jnp.zeros_like(dv_sum)

    def moved(block, which):
        to = block // per_place
        half = lax.rem(block, per_place)
        by = lax.rem(to - me + span, span)
        kinds = pl.ds(1, 2) if which else pl.ds(0, 1)
        source = stage_ref.at[kinds, block_rows(block)]
        target = d_raw_ref.at[me, kinds, block_rows(half)]
        sends, recvs = (kv_send, kv_recv) if which else (q_send, q_recv)
        return (
            to == me,
            pltpu.make_async_copy(source, target, own_sem.at[which, half]),
            send(source, target, sends.at[block], recvs.at[by, half], place_of(to, groups_here)),
        )

    def start_move(block, which):
        mine, local, remote = moved(block, which)

        @pl.when(mine)
        def _():
            local.start()

        @pl.when(jnp.logical_not(mine))
        def _():
            remote.start()

    def close(j):
        rows = block_rows(j)
        stage_ref[1, rows, :] = turn(
            dk_sum[rows, :] * scale, cos_ref[rows, :], sin_ref[rows, :]
        ).astype(jnp.bfloat16)
        stage_ref[2, rows, :] = dv_sum[rows, :].astype(jnp.bfloat16)
        start_move(j, 1)

    def one_block(n, carry):
        block = jnp.where(n < after, blocks - after + n, blocks - 1 - n)
        place = block // per_place

        @pl.when(lax.rem(n, per_place) == 0)
        def _():
            @pl.when(place == me)
            def _():
                own_copy.wait()

            for by in range(1, span):

                @pl.when(lax.rem(place + by, span) == me)
                def _():
                    do_copy(by).wait_recv()

        dq_sum[...] = jnp.zeros_like(dq_sum)
        here = block_rows(block)
        queries = qkv_ref[0, here, :]
        d_out = do_ref[here, :]
        lse = lse_ref[block]
        start_row = start_ref[block]
        delta = jnp.sum(
            (d_out.astype(jnp.float32) * o_ref[here, :].astype(jnp.float32)).T, axis=0, keepdims=True
        )

        def visit(j, masked):
            rows = block_rows(j)
            key_part = qkv_ref[1, rows, :]
            scores = (scale * log2e) * matmul_nt(key_part, queries)
            if masked:
                scores = jnp.where(block_mask(j, block, start_row), scores, masked_score)
            probs = jnp.exp2(scores - lse)
            d_probs = matmul_nt(qkv_ref[2, rows, :], d_out)
            d_scores = (probs * (d_probs - delta)).astype(jnp.bfloat16)
            dv_sum[rows, :] += matmul(probs.astype(jnp.bfloat16), d_out)
            dk_sum[rows, :] += matmul(d_scores, queries)
            dq_sum[...] += lax.dot_general(
                key_part, d_scores, (((0,), (0,)), ((), ())), preferred_element_type=jnp.float32
            )

        each_block(block, visit)
        stage_ref[0, here, :] = turn(
            dq_sum[...].T * scale, cos_ref[here, :], sin_ref[here, :]
        ).astype(jnp.bfloat16)
        start_move(block, 0)

        @pl.when((n >= 1) & (n < after))
        def _():
            close(block - 1)

        @pl.when(n >= after - 1)
        def _():
            close(block)

        return carry

    lax.fori_loop(0, blocks, one_block, 0)
    ride.receive()
    own_ride.wait()

    def add_up(here):
        total = middle_ref[here, :] + own_ride_ref[here, :].astype(jnp.float32)
        for by in range(riders_ref.shape[0]):
            total = total + riders_ref[by, here, :].astype(jnp.float32)
        output_ref[here, :] = total.astype(jnp.bfloat16)

    each_rows(0, tokens, 128, add_up)
    ride.finish()
    for by in range(1, span):
        do_copy(by).wait_send()

    def finish(block, carry):
        for which in range(2):
            mine, local, remote = moved(block, which)

            @pl.when(mine)
            def _():
                local.wait()

            @pl.when(jnp.logical_not(mine))
            def _():
                remote.wait_send()

        return carry

    lax.fori_loop(0, blocks, finish, 0)
    for by in range(1, span):
        source = lax.rem(me - by + span, span)
        for half in range(per_place):
            for which in range(2):
                kinds = pl.ds(1, 2) if which else pl.ds(0, 1)
                sends, recvs = (kv_send, kv_recv) if which else (q_send, q_recv)
                send(
                    stage_ref.at[kinds, block_rows(half)], d_raw_ref.at[source, kinds, block_rows(half)],
                    sends.at[half], recvs.at[by, half], place_of(me, groups_here),
                ).wait_recv()


def attend_back(d_sent, held, out, lse, start_rows, cosine, sine, rider, middle, groups_here):
    span, tokens, size = d_sent.shape
    blocks = start_rows.shape[0]
    length = span * tokens
    hbm = pl.BlockSpec(memory_space=pl.ANY)
    vmem = pl.BlockSpec(memory_space=pltpu.VMEM)
    per_place = tokens // BLOCK
    dma = pltpu.SemaphoreType.DMA
    return pl.pallas_call(
        functools.partial(attend_back_kernel, groups_here),
        in_specs=[hbm] + [vmem] * 6 + [hbm, vmem],
        out_specs=[hbm, vmem],
        out_shape=[
            jax.ShapeDtypeStruct((span, 3, tokens, size), jnp.bfloat16),
            jax.ShapeDtypeStruct(rider.shape[1:], jnp.bfloat16),
        ],
        scratch_shapes=[
            pltpu.VMEM((rider.shape[0] - 1, *rider.shape[1:]), jnp.bfloat16),
            pltpu.VMEM(rider.shape[1:], jnp.bfloat16),
            pltpu.VMEM((length, size), jnp.bfloat16),
            pltpu.VMEM((3, length, size), jnp.bfloat16),
            pltpu.VMEM((size, BLOCK), jnp.float32),
            pltpu.VMEM((length, size), jnp.float32),
            pltpu.VMEM((length, size), jnp.float32),
            dma((span,)), dma((span,)), dma((blocks,)), dma((span, per_place)), dma((blocks,)),
            dma((span, per_place)), dma((2, per_place)), dma((1, rider.shape[0] - 1)),
            dma((1, rider.shape[0] - 1)), dma,
        ],
        compiler_params=pltpu.CompilerParams(
            vmem_limit_bytes=48 * 2**20, collective_id=2, has_side_effects=True
        ),
        cost_estimate=pl.CostEstimate(
            flops=length * length * size * 5, bytes_accessed=length * size * 200,
            transcendentals=length * length // 2,
        ),
        name="attend_back",
    )(d_sent, held, out, lse, start_rows, cosine, sine, rider, middle)


def matmul(a, b):
    return jnp.dot(a, b, preferred_element_type=jnp.float32)


def matmul_nt(a, b):
    return lax.dot_general(a, b, (((1,), (1,)), ((), ())), preferred_element_type=jnp.float32)


def resident(shape):
    zeros = (0,) * len(shape)
    return pl.BlockSpec(shape, lambda *_: zeros, pipeline_mode=pl.Buffered(1))


def own_width(ref, width, col):
    return ref[:, pl.ds(pl.multiple_of(col * width, width), width)]


def enter_kernel(
    inputs_ref, cot_ref, pieces_ref, cots_ref, unit_ref, unit_t_ref, own_ref, inverse_ref,
    held_ref, rows_ref, sends, recvs, local, keep,
):
    count, rows, piece = held_ref.shape
    col = lax.axis_index("col")
    greet_cols(count)
    first = Gather(
        halves(inputs_ref, 0, rows), lambda c: halves(held_ref.at[c], 0, rows),
        sends.at[0], recvs.at[0], local.at[0],
    )
    second = Gather(
        halves(cot_ref, 0, rows), lambda c: halves(cots_ref.at[c], 0, rows),
        sends.at[1], recvs.at[1], local.at[1],
    )
    first.start()
    first.forward()
    second.start()
    first.receive()
    out = pltpu.make_async_copy(held_ref, pieces_ref, keep)
    out.start()

    def norm(t, carry):
        here = pl.ds(pl.multiple_of(t * 128, 128), 128)
        parts = [held_ref[c, here, :].astype(jnp.float32) for c in range(count)]
        unit, inverse = normalize_rows(jnp.concatenate(parts, axis=1))
        rows_ref[...] = unit
        unit = unit.astype(jnp.bfloat16)
        unit_ref[here, :] = unit
        unit_t_ref[:, here] = unit.T
        own_ref[here, :] = own_width(rows_ref, piece, col)
        inverse_ref[here, :] = jnp.broadcast_to(inverse, (128, 128))
        return carry

    lax.fori_loop(0, rows // 128, norm, 0)
    second.forward()
    second.receive()
    first.finish()
    second.finish()
    out.wait()


def enter(inputs, cotangent, count):
    rows, piece = inputs.shape
    width = count * piece
    hbm = pl.BlockSpec(memory_space=pl.ANY)
    vmem = pl.BlockSpec(memory_space=pltpu.VMEM)
    dma = pltpu.SemaphoreType.DMA
    shape = jax.ShapeDtypeStruct
    return pl.pallas_call(
        enter_kernel,
        in_specs=[hbm, hbm],
        out_specs=[hbm, hbm, vmem, vmem, vmem, vmem],
        out_shape=[
            shape((count, rows, piece), jnp.bfloat16),
            shape((count, rows, piece), jnp.bfloat16),
            shape((rows, width), jnp.bfloat16),
            shape((width, rows), jnp.bfloat16),
            shape((rows, piece), jnp.float32),
            shape((rows, 128), jnp.float32),
        ],
        scratch_shapes=[
            pltpu.VMEM((count, rows, piece), jnp.bfloat16),
            pltpu.VMEM((128, width), jnp.float32),
            dma((2, 6)), dma((2, 6)), dma((2, 2)), dma,
        ],
        compiler_params=pltpu.CompilerParams(
            vmem_limit_bytes=40 * 2**20, collective_id=3, has_side_effects=True
        ),
        cost_estimate=pl.CostEstimate(
            flops=10 * rows * width, bytes_accessed=100 * rows * width, transcendentals=0
        ),
        name="enter",
    )(inputs, cotangent)


def own_width(ref, width, col):
    return ref[:, pl.ds(pl.multiple_of(col * width, width), width)]


def project_kernel(unit_ref, weight_ref, cos_ref, sin_ref, out_ref):
    kind = pl.program_id(0)
    rows, width = unit_ref.shape
    heads = out_ref.shape[0]
    weight = weight_ref[:, 0].reshape(width, heads * HEAD)
    step = min(256, rows)
    for t in range(0, rows, step):
        here = pl.ds(t, step)
        raw = matmul(unit_ref[here, :], weight)

        @pl.when(kind < 2)
        def _():
            cosine, sine = cos_ref[here, :], sin_ref[here, :]
            for h in range(heads):
                part = turn(raw[:, h * HEAD : (h + 1) * HEAD], cosine, -sine)
                out_ref[h, 0, here, :] = part.astype(jnp.bfloat16)

        @pl.when(kind == 2)
        def _():
            for h in range(heads):
                out_ref[h, 0, here, :] = raw[:, h * HEAD : (h + 1) * HEAD].astype(jnp.bfloat16)


def project(unit, weight, cosine, sine):
    rows, width = unit.shape
    owners, _, depth, columns = weight.shape
    kinds = 3
    heads = columns // HEAD
    return pl.pallas_call(
        project_kernel,
        grid=(kinds,),
        in_specs=[
            resident((rows, width)),
            pl.BlockSpec((owners, 1, depth, columns), lambda k: (0, k, 0, 0)),
            resident((rows, HEAD)),
            resident((rows, HEAD)),
        ],
        out_specs=pl.BlockSpec((heads, 1, rows, HEAD), lambda k: (0, k, 0, 0)),
        out_shape=jax.ShapeDtypeStruct((heads, kinds, rows, HEAD), jnp.bfloat16),
        compiler_params=pltpu.CompilerParams(vmem_limit_bytes=40 * 2**20),
        cost_estimate=pl.CostEstimate(
            flops=2 * rows * width * kinds * columns, bytes_accessed=2 * width * kinds * columns,
            transcendentals=0,
        ),
        name="project",
    )(unit, weight, cosine, sine)


def branch_kernel(
    back_ref, weight_ref, pieces_ref, unit_ref, unit_t_ref, middle_ref, own_ref, inverse_ref,
    heads_ref, flat_ref, rows_ref, terms_ref, sends, recvs, local,
):
    col = lax.axis_index("col")
    count, heads, rows, size = heads_ref.shape
    piece = pieces_ref.shape[2]
    greet_cols(count)
    parts = 2
    span = rows // parts

    def cut(ref, p):
        half = span // 2
        return (
            ref.at[:, pl.ds(p * span, half)],
            ref.at[:, pl.ds(p * span + half, half)],
        )

    gathers = [
        Gather(
            cut(back_ref, p), lambda c, p=p: cut(heads_ref.at[c], p),
            sends.at[p], recvs.at[p], local.at[p],
        )
        for p in range(parts)
    ]
    gathers[0].start()
    for p in range(parts):
        gathers[p].forward()
        if p + 1 < parts:
            gathers[p + 1].start()
        gathers[p].receive()
        for c in range(count):
            for h in range(heads):
                at = (c * heads + h) * size
                flat_ref[:, at : at + size] = heads_ref[c, h, pl.ds(p * span, span), :]
        terms_ref[...] = matmul_nt(flat_ref[:, :piece], weight_ref[0])
        for c in range(1, count):
            terms_ref[...] += matmul_nt(flat_ref[:, c * piece : (c + 1) * piece], weight_ref[c])

        def finish(t, carry):
            inner = pl.ds(pl.multiple_of(t * 128, 128), 128)
            here = pl.ds(pl.multiple_of(p * span + t * 128, 128), 128)
            rest = [pieces_ref[c, here, :].astype(jnp.float32) for c in range(count)]
            middle = jnp.concatenate(rest, axis=1) + terms_ref[inner, :]
            rows_ref[...] = middle
            middle_ref[here, :] = own_width(rows_ref, piece, col)
            unit, inverse = normalize_rows(middle)
            rows_ref[...] = unit
            own_ref[here, :] = own_width(rows_ref, piece, col)
            inverse_ref[here, :] = jnp.broadcast_to(inverse, (128, 128))
            unit = unit.astype(jnp.bfloat16)
            unit_ref[here, :] = unit
            unit_t_ref[:, here] = unit.T
            return carry

        for t in range(span // 128):
            finish(t, 0)
    for one in gathers:
        one.finish()


def branch(back, weight, pieces):
    heads, rows, size = back.shape
    count, _, piece = pieces.shape
    width = count * piece
    hbm = pl.BlockSpec(memory_space=pl.ANY)
    vmem = pl.BlockSpec(memory_space=pltpu.VMEM)
    dma = pltpu.SemaphoreType.DMA
    shape = jax.ShapeDtypeStruct
    return pl.pallas_call(
        branch_kernel,
        in_specs=[hbm, vmem, vmem],
        out_specs=[vmem] * 5,
        out_shape=[
            shape((rows, width), jnp.bfloat16),
            shape((width, rows), jnp.bfloat16),
            shape((rows, piece), jnp.float32),
            shape((rows, piece), jnp.float32),
            shape((rows, 128), jnp.float32),
        ],
        scratch_shapes=[
            pltpu.VMEM((count, heads, rows, size), jnp.bfloat16),
            pltpu.VMEM((rows // 2, width), jnp.bfloat16),
            pltpu.VMEM((128, width), jnp.float32),
            pltpu.VMEM((rows // 2, width), jnp.float32),
            dma((2, 6)), dma((2, 6)), dma((2, 2)),
        ],
        compiler_params=pltpu.CompilerParams(
            vmem_limit_bytes=56 * 2**20, collective_id=4, has_side_effects=True
        ),
        cost_estimate=pl.CostEstimate(
            flops=2 * rows * width * width, bytes_accessed=40 * width * width, transcendentals=0
        ),
        name="branch",
    )(back, weight, pieces)


def each_rows(start, size, step, visit):
    def body(t, carry):
        visit(pl.ds(pl.multiple_of(start + t * step, step), step))
        return carry

    lax.fori_loop(0, size // step, body, 0)


def stats_of(values, unit):
    rows = values.shape[0]
    lane = lax.broadcasted_iota(jnp.int32, (rows, 128), 1)
    both = jnp.where(
        lane % 8 < 4,
        jnp.sum(values, axis=1, keepdims=True),
        jnp.sum(values * unit, axis=1, keepdims=True),
    )
    return both.T[:8]


def columns_of(stats):
    back = jnp.concatenate([stats] * 16, axis=0).T
    return back[:, :1], back[:, 4:5]


class Scatter:
    def __init__(self, pieces, slots, stats, stat_slots, here, sends, recvs):
        me = lax.axis_index("col")
        self.copies = []
        for by in range(1, pieces.shape[0]):
            device = col_device(by)
            self.copies.append(
                send(pieces.at[me ^ by, here], slots.at[by - 1, here],
                     sends.at[0, by - 1], recvs.at[0, by - 1], device)
            )
            if stats is not None:
                self.copies.append(
                    send(stats.at[:, here], stat_slots.at[by - 1, :, here],
                         sends.at[1, by - 1], recvs.at[1, by - 1], device)
                )

    def start(self):
        for one in self.copies:
            one.start()

    def receive(self):
        for one in self.copies:
            one.wait_recv()

    def finish(self):
        for one in self.copies:
            one.wait_send()


class Fold:
    def __init__(self, pieces, slots, stats, stat_slots, start, size, sends, recvs):
        me = lax.axis_index("col")
        half = size // 2
        self.pieces, self.slots = pieces, slots
        self.firsts, self.sums, self.seconds, self.stats = [], [], [], []

        def copy(i, source, target, by):
            return send(source, target, sends.at[i], recvs.at[i], col_device(by))

        for i, (by, then) in enumerate(((1, 2), (2, 1))):
            here = pl.ds(pl.multiple_of(start + i * half, half), half)
            self.firsts.append(
                [
                    copy(3 * i, pieces.at[me ^ by, here], slots.at[0, here], by),
                    copy(3 * i + 1, pieces.at[me ^ 3, here], slots.at[1, here], by),
                ]
            )
            self.sums.append((me ^ then, here))
            self.seconds.append(copy(3 * i + 2, pieces.at[me ^ then, here], slots.at[2, here], then))
        rows = pl.ds(pl.multiple_of(start, size), size)
        for by in (1, 2, 3):
            self.stats.append(copy(5 + by, stats.at[:, rows], stat_slots.at[by - 1, :, rows], by))

    def start(self):
        for one in self.firsts[0] + self.firsts[1] + self.stats:
            one.start()

    def forward(self):
        for first, (to, here), second in zip(self.firsts, self.sums, self.seconds):
            for one in first:
                one.wait_recv()
            total = self.pieces[to, here, :].astype(jnp.float32) + self.slots[1, here, :].astype(
                jnp.float32
            )
            self.pieces[to, here, :] = total.astype(jnp.bfloat16)
            second.start()

    def receive(self):
        for one in self.seconds + self.stats:
            one.wait_recv()

    def finish(self):
        for one in self.firsts[0] + self.firsts[1] + self.seconds + self.stats:
            one.wait_send()


def split_rows(sum_ref, unit_ref, pieces_ref, stats_ref, start, size):
    count, _, width = pieces_ref.shape

    def part(here):
        values = sum_ref[here, :]
        stats_ref[:, here] = stats_of(values, unit_ref[here, :].astype(jnp.float32))
        for c in range(count):
            pieces_ref[c, here, :] = values[:, c * width : (c + 1) * width].astype(jnp.bfloat16)

    each_rows(start, size, 128, part)


def normed_grad(sum_ref, slots, stats_ref, stat_slots, own_ref, inverse_ref, here, width, col):
    piece = slots.shape[2]
    grad = sum_ref[here, pl.ds(pl.multiple_of(col * piece, piece), piece)]
    grad = grad + slots[0, here, :].astype(jnp.float32) + slots[2, here, :].astype(jnp.float32)
    stats = stats_ref[:, here]
    for by in range(stat_slots.shape[0]):
        stats = stats + stat_slots[by, :, here]
    sums, cross = columns_of(stats)
    return normalize_back(grad, sums, cross, own_ref[here, :], inverse_ref[here, :1], float(width))


class LineSum:
    def __init__(self, grads, cross, slots, groups_here, sems):
        self.grads, self.cross, self.slots, self.groups = grads, cross, slots, groups_here
        self.core_send, self.core_recv, self.hop_send, self.hop_recv = sems
        self.span = grads.shape[0] // groups_here
        row = lax.axis_index("row")
        self.me, self.group = row // groups_here, lax.rem(row, groups_here)
        self.partner = (row + 1 - 2 * self.group, lax.axis_index("col"))

    def owner(self, place, other):
        group = 1 - self.group if other else self.group
        return jnp.clip(place, 0, self.span - 1) * self.groups + group

    def across(self, place):
        return send(
            self.grads.at[self.owner(place, True)], self.cross.at[place], self.core_send.at[place],
            self.core_recv.at[place], self.partner,
        )

    def join(self, place):
        self.across(place).wait_recv()
        owner = self.owner(place, False)
        for k in range(self.grads.shape[1]):
            total = self.grads[owner, k].astype(jnp.float32) + self.cross[place, k].astype(jnp.float32)
            self.grads[owner, k] = total.astype(jnp.bfloat16)

    def hop(self, way, r):
        i = (1 - way) // 2
        to = self.me + way * (self.span - r)
        behind = self.me if way > 0 else self.span - 1 - self.me
        copy = send(
            self.grads.at[self.owner(to, False)], self.slots.at[i, r - 1], self.hop_send.at[i, r - 1],
            self.hop_recv.at[i, r - 1],
            place_of(jnp.clip(self.me + way, 0, self.span - 1), self.groups),
        )
        return behind <= r - 1, (behind >= 1) & (behind <= r), to, copy

    def start(self, r):
        for way in (1, -1):
            i = (1 - way) // 2
            sends, _, to, copy = self.hop(way, r)
            if r > 1:
                _, came, _, before = self.hop(way, r - 1)

                @pl.when(came)
                def _():
                    before.wait_recv()

                @pl.when(came & sends)
                def _():
                    owner = self.owner(to, False)
                    for k in range(self.grads.shape[1]):
                        total = self.grads[owner, k].astype(jnp.float32) + self.slots[
                            i, r - 2, k
                        ].astype(jnp.float32)
                        self.grads[owner, k] = total.astype(jnp.bfloat16)

            @pl.when(sends)
            def _():
                copy.start()

    def result(self, out_ref):
        last = self.span - 1
        own = self.owner(self.me, False)
        for k in range(self.grads.shape[1]):
            out_ref[k] = self.grads[own, k].astype(jnp.float32)
        for way in (1, -1):
            _, came, _, copy = self.hop(way, last)

            @pl.when(came)
            def _():
                copy.wait_recv()
                for k in range(self.grads.shape[1]):
                    out_ref[k] += self.slots[(1 - way) // 2, last - 1, k].astype(jnp.float32)

    def finish(self):
        for place in range(self.span):
            self.across(place).wait_send()
        for r in range(1, self.span):
            for way in (1, -1):
                sends, _, _, copy = self.hop(way, r)

                @pl.when(sends)
                def _():
                    copy.wait_send()


def leave_kernel(
    groups_here, d_raw_ref, weight_ref, unit_t_ref, unit_ref, own_ref, inverse_ref, d_middle_ref,
    out_ref, grad_ref,
    rows_ref, sum_ref, pieces_ref, slots_ref, stats_ref, stat_slots_ref, weights_ref, turned_ref,
    parts_ref, cross_ref, line_ref,
    sends, recvs, load, *line_sems,
):
    col = lax.axis_index("col")
    rows, width = unit_ref.shape
    heads, kinds = d_raw_ref.shape[:2]
    columns = heads * HEAD
    depth = parts_ref.shape[2]
    turned = pltpu.make_async_copy(unit_t_ref, turned_ref, load.at[kinds])
    turned.start()
    loads = [
        pltpu.make_async_copy(weight_ref.at[:, k], weights_ref.at[k], load.at[k]) for k in range(kinds)
    ]
    for one in loads:
        one.start()
    line = LineSum(parts_ref, cross_ref, line_ref, groups_here, line_sems)
    span = line.span
    barrier = pltpu.get_barrier_semaphore()
    pl.semaphore_signal(barrier, inc=1, device_id=line.partner, device_id_type=MESH)
    greet_all(line.me, span, groups_here, pieces_ref.shape[0], 1)
    for k in range(kinds):
        for h in range(heads):
            rows_ref[k, :, h * HEAD : (h + 1) * HEAD] = d_raw_ref[h, k]
    turned.wait()

    def part_of(owner):
        here = pl.ds(pl.multiple_of(owner * depth, depth), depth)
        for k in range(kinds):
            parts_ref[owner, k] = matmul(turned_ref[here, :], rows_ref[k]).astype(jnp.bfloat16)

    for place in range(span):
        part_of(line.owner(place, True))
        line.across(place).start()
    for place in range(span):
        part_of(line.owner(place, False))
    for place in (span - 1, 0):
        line.join(place)
    line.start(1)
    for place in range(1, span - 1):
        line.join(place)
    for one in loads:
        one.wait()
    count = sends.shape[0]
    size = rows // count
    moves = []
    for p in range(count):
        here = pl.ds(p * size, size)
        sum_ref[here, :] = matmul_nt(rows_ref[0, here, :], weights_ref[0].reshape(width, columns))
        for k in range(1, kinds):
            sum_ref[here, :] += matmul_nt(
                rows_ref[k, here, :], weights_ref[k].reshape(width, columns)
            )
        split_rows(sum_ref, unit_ref, pieces_ref, stats_ref, p * size, size)
        moves.append(
            Fold(pieces_ref, slots_ref, stats_ref, stat_slots_ref, p * size, size, sends.at[p], recvs.at[p])
        )
        moves[p].start()
        if p == 0:
            line.start(2)
    moves[0].forward()
    moves[1].forward()
    line.start(3)
    for p in range(count):
        moves[p].receive()

        def last_part(here):
            out_ref[here, :] = d_middle_ref[here, :] + normed_grad(
                sum_ref, slots_ref, stats_ref, stat_slots_ref, own_ref, inverse_ref, here, width, col
            )

        each_rows(p * size, size, 128, last_part)
    line.result(grad_ref)
    for one in moves:
        one.finish()
    line.finish()


def leave(d_raw, weight, unit_t, unit, own, inverse, d_middle, groups_here, count):
    rows, width = unit.shape
    heads, kinds = d_raw.shape[:2]
    owners, _, depth, columns = weight.shape
    span = owners // groups_here
    piece = width // count
    hbm = pl.BlockSpec(memory_space=pl.ANY)
    vmem = pl.BlockSpec(memory_space=pltpu.VMEM)
    dma = pltpu.SemaphoreType.DMA
    return pl.pallas_call(
        functools.partial(leave_kernel, groups_here),
        in_specs=[vmem, hbm, hbm] + [vmem] * 4,
        out_specs=[vmem, vmem],
        out_shape=[
            jax.ShapeDtypeStruct((rows, piece), jnp.float32),
            jax.ShapeDtypeStruct((kinds, depth, columns), jnp.float32),
        ],
        scratch_shapes=[
            pltpu.VMEM((kinds, rows, columns), jnp.bfloat16),
            pltpu.VMEM((rows, width), jnp.float32),
            pltpu.VMEM((count, rows, piece), jnp.bfloat16),
            pltpu.VMEM((count - 1, rows, piece), jnp.bfloat16),
            pltpu.VMEM((8, rows), jnp.float32),
            pltpu.VMEM((count - 1, 8, rows), jnp.float32),
            pltpu.VMEM((kinds, owners, depth, columns), jnp.bfloat16),
            pltpu.VMEM((width, rows), jnp.bfloat16),
            pltpu.VMEM((owners, kinds, depth, columns), jnp.bfloat16),
            pltpu.VMEM((span, kinds, depth, columns), jnp.bfloat16),
            pltpu.VMEM((2, span - 1, kinds, depth, columns), jnp.bfloat16),
            dma((2, 9)), dma((2, 9)), dma((kinds + 1,)),
            dma((span,)), dma((span,)), dma((2, span - 1)), dma((2, span - 1)),
        ],
        compiler_params=pltpu.CompilerParams(
            vmem_limit_bytes=63 * 2**20, collective_id=5, has_side_effects=True
        ),
        cost_estimate=pl.CostEstimate(
            flops=4 * rows * width * kinds * columns, bytes_accessed=100 * rows * width, transcendentals=0
        ),
        name="leave",
    )(d_raw, weight, unit_t, unit, own, inverse, d_middle)


def feed_front(unit_ref, cot_ref, weight_ref, two_ref, act, before=None):
    owners, _, _, depth, cols = weight_ref.shape
    rows, width = unit_ref.shape
    count, _, piece = cot_ref.shape
    gate_weight = weight_ref[:, 0, 0].reshape(width, cols)
    up_weight = weight_ref[:, 0, 1].reshape(width, cols)
    down_weight = weight_ref[:, 0, 2].reshape(width, cols)
    step = min(256, rows)
    for t in range(0, rows, step):
        here = pl.ds(t, step)
        unit = unit_ref[here, :]
        gate = matmul(unit, gate_weight)
        up_proj = matmul(unit, up_weight)
        d_hidden = sum(
            matmul(cot_ref[c, here, :], down_weight[c * piece : (c + 1) * piece])
            for c in range(count)
        )
        sigmoid_gate = jax.nn.sigmoid(gate)
        silu_gate = gate * sigmoid_gate
        act[0, here, :] = (silu_gate * up_proj).astype(jnp.bfloat16)
        act[1, here, :] = (
            d_hidden * up_proj * sigmoid_gate * (1.0 + gate * (1.0 - sigmoid_gate))
        ).astype(jnp.bfloat16)
        act[2, here, :] = (d_hidden * silu_gate).astype(jnp.bfloat16)
    if before is not None:
        before()
    for t in range(0, rows, step):
        here = pl.ds(t, step)
        two_ref[here, :] += matmul_nt(act[1, here, :], gate_weight) + matmul_nt(
            act[2, here, :], up_weight
        )


def feed_rear(unit_t_ref, cot_t_ref, grad_ref, act):
    owners, _, depth, cols = grad_ref.shape
    hidden, d_gate, d_up = act[0], act[1], act[2]
    for owner in range(owners):
        here = pl.ds(owner * depth, depth)
        unit_t = unit_t_ref[here, :]
        grad_ref[owner, 0] = matmul(unit_t, d_gate).astype(jnp.bfloat16)
        grad_ref[owner, 1] = matmul(unit_t, d_up).astype(jnp.bfloat16)
        grad_ref[owner, 2] = matmul(cot_t_ref[here, :], hidden).astype(jnp.bfloat16)


def feed_all_kernel(
    unit_ref, unit_t_ref, cot_ref, cot_t_ref, weight_ref, *refs
):
    old = refs[:-7]
    grad_ref, new_two_ref, new_out_ref, two_ref, out_ref, act_ref, sem = refs[-7:]
    tile = pl.program_id(0)

    loads = []
    if old:
        loads = [
            pltpu.make_async_copy(old[0], two_ref, sem.at[0]),
            pltpu.make_async_copy(old[1], out_ref, sem.at[1]),
        ]

    @pl.when(tile == 0)
    def _():
        for load in loads:
            load.start()
        if not old:
            two_ref[...] = jnp.zeros_like(two_ref)
            out_ref[...] = jnp.zeros_like(out_ref)

    def arrive():
        @pl.when(tile == 0)
        def _():
            for load in loads:
                load.wait()

    feed_front(unit_ref, cot_ref, weight_ref, two_ref, act_ref, arrive if old else None)
    final = tile == pl.num_programs(0) - 1
    copies = [
        pltpu.make_async_copy(two_ref, new_two_ref, sem.at[0]),
        pltpu.make_async_copy(out_ref, new_out_ref, sem.at[1]),
    ]

    @pl.when(final)
    def _():
        copies[0].start()

    down_weight = weight_ref[:, 0, 2].reshape(unit_ref.shape[1], weight_ref.shape[4])
    rows = unit_ref.shape[0]
    step = min(256, rows)
    for t in range(0, rows, step):
        here = pl.ds(t, step)
        out_ref[here, :] += matmul_nt(act_ref[0, here, :], down_weight)

    @pl.when(final)
    def _():
        copies[1].start()

    feed_rear(unit_t_ref, cot_t_ref, grad_ref, act_ref)

    @pl.when(final)
    def _():
        for copy in copies:
            copy.wait()


def feed_cost(rows, width, owners, tiles, depth, cols, matmuls):
    return pl.CostEstimate(
        flops=2 * matmuls * rows * width * tiles * cols,
        bytes_accessed=12 * owners * tiles * depth * cols,
        transcendentals=rows * tiles * cols,
    )


def feed_all(unit, unit_t, cot, cot_t, weights, tiles, old, blocks):
    rows, width = unit.shape
    owners, _, _, depth, cols = weights.shape
    hbm = pl.BlockSpec(memory_space=pl.ANY)
    return pl.pallas_call(
        feed_all_kernel,
        grid=(tiles,),
        in_specs=[
            resident((rows, width)), resident((width, rows)), resident(cot.shape),
            resident((width, rows)),
            pl.BlockSpec((owners, 1, 3, depth, cols), lambda i: (0, i, 0, 0, 0)),
        ] + [hbm] * len(old),
        out_specs=[pl.BlockSpec((owners, 3, depth, cols), lambda i: (0, i, 0, 0)), hbm, hbm],
        out_shape=[jax.ShapeDtypeStruct((owners, blocks, depth, cols), jnp.bfloat16)]
        + [jax.ShapeDtypeStruct((rows, width), jnp.float32)] * 2,
        scratch_shapes=[
            pltpu.VMEM((rows, width), jnp.float32),
            pltpu.VMEM((rows, width), jnp.float32),
            pltpu.VMEM((3, rows, cols), jnp.bfloat16),
            pltpu.SemaphoreType.DMA((2,)),
        ],
        compiler_params=pltpu.CompilerParams(vmem_limit_bytes=62 * 2**20),
        cost_estimate=feed_cost(rows, width, owners, tiles, depth, cols, 9),
        name="feed_all",
    )(unit, unit_t, cot, cot_t, weights, *old)


def feed_last_kernel(
    unit_hbm, unit_t_hbm, cots_hbm, cot_t_hbm, weight_hbm, old_two_hbm, old_out_hbm, own_ref,
    inverse_ref, out_t_hbm, back_ref, _,
    late_ref, ffn_ref, d_middle_ref, d_sent_ref,
    grad_ref, out_grad_ref, out_t_ref, unit_ref, turned_ref, cots_ref, weight_ref, two_ref, sum_ref, act_ref, pieces_ref, slots_ref,
    stats_ref, stat_slots_ref, d_pieces_ref,
    load, sends, recvs, g_sends, g_recvs,
):
    col = lax.axis_index("col")
    rows, width = unit_ref.shape
    count, _, piece = pieces_ref.shape
    owners, _, _, depth, cols = weight_ref.shape
    heads, _, size = back_ref.shape
    tile = weight_hbm.shape[1] - 1
    extra = late_ref.shape[1] - 3 - heads * size // cols

    def fetch(i, source, target):
        copy = pltpu.make_async_copy(source, target, load.at[i])
        copy.start()
        return copy

    loads = [
        fetch(0, unit_hbm, unit_ref), fetch(1, weight_hbm.at[:, pl.ds(tile, 1)], weight_ref), fetch(2, cots_hbm, cots_ref),
        fetch(3, old_two_hbm, two_ref), fetch(4, unit_t_hbm, turned_ref.at[0]),
        fetch(5, cot_t_hbm, turned_ref.at[1]), fetch(6, old_out_hbm.at[: rows // 4], sum_ref),
    ]
    greet_cols(count)
    for i in range(3):
        loads[i].wait()
    feed_front(unit_ref, cots_ref, weight_ref, two_ref, act_ref, loads[3].wait)
    turned_out = pltpu.make_async_copy(out_t_hbm.at[:, 3], out_t_ref, load.at[12])
    turned_out.start()
    parts = sends.shape[0]
    span = rows // parts
    moves, gathers = [], []
    for p in range(parts):
        split_rows(two_ref, unit_ref, pieces_ref, stats_ref, p * span, span)
        moves.append(
            Fold(pieces_ref, slots_ref, stats_ref, stat_slots_ref, p * span, span,
                 sends.at[p], recvs.at[p])
        )
        moves[p].start()
        own = d_pieces_ref.at[col]
        gathers.append(
            Gather(
                halves(own, p * span, span),
                lambda c, p=p: halves(d_pieces_ref.at[c], p * span, span),
                g_sends.at[p], g_recvs.at[p], None,
            )
        )
    quarter = rows // 4
    down_weight = weight_ref[:, 0, 2].reshape(width, cols)
    for p in range(4):
        here = pl.ds(p * quarter, quarter)
        loads[6 + p].wait()
        sum_ref[...] += matmul_nt(act_ref[0, here, :], down_weight)
        for c in range(count):
            ffn_ref[c, here, :] = sum_ref[:, c * piece : (c + 1) * piece].astype(jnp.bfloat16)
        if p < 3:
            loads.append(fetch(7 + p, old_out_hbm.at[pl.ds((p + 1) * quarter, quarter)], sum_ref))
    moves[0].forward()
    moves[1].forward()
    for i in range(4, 6):
        loads[i].wait()
    feed_rear(turned_ref.at[0], turned_ref.at[1], grad_ref, act_ref)
    stores = [fetch(10, grad_ref, late_ref.at[:, pl.ds(extra, 3)])]
    own_cot = cots_ref.at[col]
    for p in range(2, parts):
        moves[p].forward()
    for p in range(parts):
        moves[p].receive()

        def middle_part(here):
            d_middle = own_cot[here, :].astype(jnp.float32) + normed_grad(
                two_ref, slots_ref, stats_ref, stat_slots_ref, own_ref, inverse_ref, here, width, col
            )
            d_middle_ref[here, :] = d_middle
            d_pieces_ref[col, here, :] = d_middle.astype(jnp.bfloat16)

        each_rows(p * span, span, 128, middle_part)
        gathers[p].start()
        if p:
            gathers[p - 1].forward()
    gathers[parts - 1].forward()
    for one in moves:
        one.finish()
    for h in range(heads):
        pieces_ref[0, :, h * size : (h + 1) * size] = back_ref[h]
    turned_out.wait()
    out_t = out_t_ref[...].reshape(width, heads * size)
    for p in range(parts):
        gathers[p].receive()
        here = pl.ds(p * span, span)
        d_attended = sum(
            matmul(d_pieces_ref[c, here, :], out_t[c * piece : (c + 1) * piece]) for c in range(count)
        )
        for h in range(heads):
            d_sent_ref[h, here, :] = d_attended[:, h * size : (h + 1) * size].astype(jnp.bfloat16)
    per_piece = piece // depth
    for owner in range(owners):
        at = (owner % per_piece) * depth
        turned = lax.dot_general(
            d_pieces_ref[owner // per_piece, :, at : at + depth], pieces_ref[0],
            (((0,), (0,)), ((), ())), preferred_element_type=jnp.float32,
        ).astype(jnp.bfloat16)
        for j in range(heads * size // cols):
            out_grad_ref[owner, j] = turned[:, j * cols : (j + 1) * cols]
    stores.append(fetch(11, out_grad_ref, late_ref.at[:, pl.ds(extra + 3, heads * size // cols)]))
    for one in stores:
        one.wait()
    for one in gathers:
        one.finish()


def feed_last(unit, unit_t, cots, cot_t, weights, old, own, inverse, out_t, back, late):
    rows, width = unit.shape
    count, _, piece = cots.shape
    owners, _, _, depth, cols = weights.shape
    heads, _, size = back.shape
    hbm = pl.BlockSpec(memory_space=pl.ANY)
    vmem = pl.BlockSpec(memory_space=pltpu.VMEM)
    dma = pltpu.SemaphoreType.DMA
    shape = jax.ShapeDtypeStruct
    return pl.pallas_call(
        feed_last_kernel,
        in_specs=[hbm] * 7 + [vmem] * 2 + [hbm, vmem, hbm],
        out_specs=[hbm] + [vmem] * 3,
        input_output_aliases={11: 0},
        out_shape=[
            shape(late.shape, jnp.bfloat16),
            shape((count, rows, piece), jnp.bfloat16),
            shape((rows, piece), jnp.float32),
            shape((heads, rows, size), jnp.bfloat16),
        ],
        scratch_shapes=[
            pltpu.VMEM((owners, 3, depth, cols), jnp.bfloat16),
            pltpu.VMEM((owners, heads * size // cols, depth, cols), jnp.bfloat16),
            pltpu.VMEM((owners, depth, heads * size), jnp.bfloat16),
            pltpu.VMEM((rows, width), jnp.bfloat16),
            pltpu.VMEM((2, width, rows), jnp.bfloat16),
            pltpu.VMEM((count, rows, piece), jnp.bfloat16),
            pltpu.VMEM((owners, 1, 3, depth, cols), jnp.bfloat16),
            pltpu.VMEM((rows, width), jnp.float32),
            pltpu.VMEM((rows // 4, width), jnp.float32),
            pltpu.VMEM((3, rows, cols), jnp.bfloat16),
            pltpu.VMEM((count, rows, piece), jnp.bfloat16),
            pltpu.VMEM((count - 1, rows, piece), jnp.bfloat16),
            pltpu.VMEM((8, rows), jnp.float32),
            pltpu.VMEM((count - 1, 8, rows), jnp.float32),
            pltpu.VMEM((count, rows, piece), jnp.bfloat16),
            dma((13,)), dma((4, 9)), dma((4, 9)), dma((4, 6)), dma((4, 6)),
        ],
        compiler_params=pltpu.CompilerParams(
            vmem_limit_bytes=63 * 2**20 + 2**19, collective_id=6, has_side_effects=True
        ),
        cost_estimate=pl.CostEstimate(
            flops=18 * rows * width * cols, bytes_accessed=100 * rows * width,
            transcendentals=rows * cols,
        ),
        name="feed_last",
    )(unit, unit_t, cots, cot_t, weights, *old, own, inverse, out_t, back, late)


def unpack_kernel(blocks_ref, *refs):
    outs = refs[-3:]
    outs[0][...] = blocks_ref[0].astype(jnp.float32)
    outs[1][...] = blocks_ref[1].astype(jnp.float32)
    outs[2][...] = blocks_ref[2].astype(jnp.float32).T


def unpack(blocks, skip, count, hidden, old):
    _, depth, cols = blocks.shape
    shapes = [(depth, hidden), (depth, hidden), (hidden, depth)]
    wide = pl.BlockSpec((depth, cols), lambda i: (0, skip + i))
    return pl.pallas_call(
        unpack_kernel,
        grid=(count,),
        in_specs=[pl.BlockSpec((3, depth, cols), lambda i: (i, 0, 0))]
        + [pl.BlockSpec(memory_space=pl.ANY)] * len(old),
        out_specs=[wide, wide, pl.BlockSpec((cols, depth), lambda i: (skip + i, 0))],
        out_shape=[jax.ShapeDtypeStruct(one, jnp.float32) for one in shapes],
        input_output_aliases={1 + i: i for i in range(len(old))},
        name="unpack",
    )(blocks, *old)


def group_rows(lengths, group, begin, count):
    row_lengths = lax.dynamic_slice_in_dim(lengths, group, 1, 0)[0]
    local_index = begin + jnp.arange(count, dtype=jnp.int32)
    seg_ends = jnp.cumsum(row_lengths)
    seg_starts = seg_ends - row_lengths
    after_prompt = local_index - PROMPT
    inside = (after_prompt[:, None] >= seg_starts[None, :]) & (
        after_prompt[:, None] < seg_ends[None, :]
    )
    start = jnp.sum(jnp.where(inside, seg_starts[None, :], 0), axis=1)
    in_prompt = local_index < PROMPT
    start_row = jnp.where(in_prompt, 0, PROMPT + start)
    position = jnp.where(in_prompt, local_index, PROMPT + after_prompt - start)
    half = HEAD // 2
    frequency = jnp.exp(
        -math.log(rope_base) * (2.0 * jnp.arange(half, dtype=jnp.float32) / HEAD)
    )
    angles = position.astype(jnp.float32)[:, None] * frequency[None, :]
    cosine, sine = jnp.cos(angles), jnp.sin(angles)
    return (
        start_row,
        jnp.concatenate([cosine, cosine], axis=1),
        jnp.concatenate([sine, -sine], axis=1),
    )


def fast_body(
    inputs,
    cotangent,
    lengths,
    query_key_value_weight,
    out_weight,
    gate_weight,
    up_weight,
    down_weight,
):
    tok_rows, part_width = inputs.shape
    col_count = lax.axis_size("col")
    col_index = lax.axis_index("col")
    row_index = lax.axis_index("row")
    span = GROUP_LEN // tok_rows
    groups_here = lax.axis_size("row") // span
    heads_here = part_width // HEAD
    place = row_index // groups_here
    group = row_index % groups_here
    depth = gate_weight.shape[0]
    hidden_here = gate_weight.shape[1]
    tiles = hidden_here // min(256, depth)
    tile = hidden_here // tiles

    def gather(shard, after=None):
        if after is not None:
            shard, after = tied(shard, after)
        return lax.all_gather(shard, "row"), after

    def tied(value, *others):
        return lax.optimization_barrier((value, *others))

    mixed = jnp.concatenate([query_key_value_weight.transpose(1, 0, 2), out_weight.T[None]])
    weights, _ = gather(mixed)
    packed = jnp.stack([gate_weight, up_weight, down_weight.T]).reshape(3, depth, tiles, tile)
    packed = packed.transpose(2, 0, 1, 3)
    first = max(1, tiles // 2)
    early, later = lax.optimization_barrier((packed[:first], packed[first:]))
    pieces, cots, normed_one, unit_one_t, unit_one, inverse_one = enter(
        inputs, cotangent, col_count
    )
    normed_one, weights, lengths = tied(normed_one, weights, lengths)
    feed_one, weights = gather(early, weights)
    _, own_cos, own_sin = group_rows(lengths, group, place * tok_rows, tok_rows)
    start_rows = group_rows(lengths, group, 0, GROUP_LEN)[0].reshape(-1, 1, BLOCK)
    sent = project(normed_one, weights, own_cos, own_sin)
    back, held, attended_head, lse, out_t = attend(
        sent, start_rows, weights, groups_here, col_count
    )
    out_t = out_t.reshape(col_count, -1, part_width)
    back, feed_one = tied(back, feed_one)
    feed_two, feed_one = gather(later, feed_one)
    cots, back = tied(cots, back)
    cot_t = cots.transpose(0, 2, 1).reshape(-1, tok_rows)
    normed_two, unit_t, middle, unit_two, inverse_two = branch(back, out_t, pieces)
    rows_two = (normed_two, unit_t, cots, cot_t)

    def owned(part):
        return lax.psum_scatter(part, "row", scatter_dimension=0, tiled=True)[0]

    grads_one, *sums = feed_all(*rows_two, feed_one, first, (), 3 * first)
    lengths, sums[0] = tied(lengths, sums[0])
    _, cosine, sine = lax.optimization_barrier(group_rows(lengths, group, 0, GROUP_LEN))
    sums[0], grads_one, feed_two, cosine = tied(sums[0], grads_one, feed_two, cosine)
    grads_one = owned(grads_one)
    rest = tiles - first - 1
    blocks = 3 * (rest + 1) + part_width // tile
    late, *sums = feed_all(*rows_two, feed_two, rest, sums, blocks)
    late, ffn_pieces, d_middle, d_sent = feed_last(
        *rows_two, feed_two, sums, unit_two, inverse_two, weights, back, late
    )
    late, grads_one = tied(late, grads_one)
    late = owned(late)
    grads = unpack(grads_one, 0, first, hidden_here, ())
    d_sent, *grads = tied(d_sent, *grads)
    d_raw, output = attend_back(
        d_sent, held, attended_head, lse, start_rows, cosine, sine, ffn_pieces, middle, groups_here
    )
    input_grad, own_grads = leave(
        d_raw, weights, unit_one_t, normed_one, unit_one, inverse_one, d_middle, groups_here, col_count
    )
    qkv_grad = own_grads.transpose(1, 0, 2)
    grads = unpack(late, first, tiles - first, hidden_here, grads)
    out_grad = late[3 * (rest + 1) :].transpose(0, 2, 1).reshape(part_width, depth).astype(jnp.float32)
    return (output, input_grad, qkv_grad, out_grad, *grads)


def body(
    inputs,
    cotangent,
    lengths,
    query_key_value_weight,
    out_weight,
    gate_weight,
    up_weight,
    down_weight,
):
    tok_rows = inputs.shape[0]
    part_width = inputs.shape[1]
    col_count = lax.axis_size("col")
    col_index = lax.axis_index("col")
    row_index = lax.axis_index("row")
    full_width = float(part_width * col_count)
    group_span = GROUP_LEN // tok_rows
    groups_here = lax.axis_size("row") // group_span
    head_size = HEAD
    heads_here = part_width // head_size
    score_scale = head_size ** (-0.5)
    block_place = row_index // groups_here
    full_inputs, full_cotangent = (
        lax.all_gather(inputs, "col", axis=1, tiled=True),
        lax.all_gather(cotangent, "col", axis=1, tiled=True),
    )
    projection_full_rows, out_full, gate_full, up_full, down_full = (
        lax.all_gather(query_key_value_weight, "row", axis=0, tiled=True),
        lax.all_gather(out_weight, "row", axis=1, tiled=True),
        lax.all_gather(gate_weight, "row", axis=0, tiled=True),
        lax.all_gather(up_weight, "row", axis=0, tiled=True),
        lax.all_gather(down_weight, "row", axis=1, tiled=True),
    )
    unit_one, inverse_one = normalize_rows(full_inputs.astype(jnp.float32))
    first_normed_input = unit_one.astype(jnp.bfloat16)
    raw_projection_output = jnp.einsum(
        "cu,ufk->cfk", first_normed_input, projection_full_rows, preferred_element_type=jnp.float32
    )
    raw_projection_output = raw_projection_output.reshape(tok_rows, 3, heads_here, head_size)
    own_meta = token_layout(lengths, row_index, groups_here, tok_rows)
    cosine, sine = rotation_angles(own_meta[3], head_size)
    queries = rotate(raw_projection_output[:, 0], cosine, sine, False).astype(jnp.bfloat16)
    key_rows = rotate(raw_projection_output[:, 1], cosine, sine, False).astype(jnp.bfloat16)
    value_rows = raw_projection_output[:, 2].astype(jnp.bfloat16)
    pieces = [(key_rows, value_rows)]
    for shift_by in range(1, group_span):
        pieces.append(passed_along((key_rows, value_rows), "row", shift_by * groups_here))
    visibility = [
        visible_mask(
            own_meta,
            token_layout(lengths, row_index - shift_by * groups_here, groups_here, tok_rows),
        )
        for shift_by in range(group_span)
    ]
    live_piece = [shift_by <= block_place for shift_by in range(group_span)]
    first_scores = score_block(queries, pieces[0][0], visibility[0], score_scale)
    top_rows = jnp.max(first_scores, axis=-1, keepdims=True)
    total_rows = jnp.sum(jnp.exp(first_scores - top_rows), axis=-1, keepdims=True)
    for shift_by in range(1, group_span):

        def add_stats(carry, shift_by=shift_by):
            old_top, old_total = carry
            scores = score_block(queries, pieces[shift_by][0], visibility[shift_by], score_scale)
            new_top = jnp.maximum(old_top, jnp.max(scores, axis=-1, keepdims=True))
            new_total = old_total * jnp.exp(old_top - new_top) + jnp.sum(
                jnp.exp(scores - new_top), axis=-1, keepdims=True
            )
            return (new_top, new_total)

        top_rows, total_rows = lax.cond(
            live_piece[shift_by], add_stats, lambda carry: carry, (top_rows, total_rows)
        )
    log_total = top_rows + jnp.log(total_rows)
    attended = jnp.zeros((tok_rows, heads_here, head_size), jnp.float32)
    for shift_by in range(group_span):

        def add_values(total, shift_by=shift_by):
            scores = score_block(queries, pieces[shift_by][0], visibility[shift_by], score_scale)
            probs_low = jnp.exp(scores - log_total).astype(jnp.bfloat16)
            return total + jnp.einsum(
                "hqk,khd->qhd", probs_low, pieces[shift_by][1], preferred_element_type=jnp.float32
            )

        attended = lax.cond(live_piece[shift_by], add_values, lambda total: total, attended)
    attended_flat = attended.reshape(tok_rows, part_width).astype(jnp.bfloat16)
    branch_terms = jnp.dot(attended_flat, out_full, preferred_element_type=jnp.float32)
    branch_full = lax.psum(branch_terms, "col")
    middle_full = full_inputs.astype(jnp.float32) + branch_full
    middle = lax.dynamic_slice_in_dim(middle_full, col_index * part_width, part_width, 1)
    unit_two, inverse_two = normalize_rows(middle_full)
    normed_two = unit_two.astype(jnp.bfloat16)
    gate = jnp.dot(normed_two, gate_full, preferred_element_type=jnp.float32)
    up_proj = jnp.dot(normed_two, up_full, preferred_element_type=jnp.float32)
    sigmoid_gate = jax.nn.sigmoid(gate)
    silu_gate = gate * sigmoid_gate
    hidden = (silu_gate * up_proj).astype(jnp.bfloat16)
    ffn_terms = jnp.dot(hidden, down_full, preferred_element_type=jnp.float32)
    ffn_part = lax.psum_scatter(
        ffn_terms.astype(jnp.bfloat16), "col", scatter_dimension=1, tiled=True
    ).astype(jnp.float32)
    output = (middle + ffn_part).astype(jnp.bfloat16)
    projection_full_rows, out_full, gate_full, up_full, down_full = (
        lax.all_gather(query_key_value_weight, "row", axis=0, tiled=True),
        lax.all_gather(out_weight, "row", axis=1, tiled=True),
        lax.all_gather(gate_weight, "row", axis=0, tiled=True),
        lax.all_gather(up_weight, "row", axis=0, tiled=True),
        lax.all_gather(down_weight, "row", axis=1, tiled=True),
    )
    d_hidden = jnp.einsum(
        "td,fd->tf", full_cotangent, down_full, preferred_element_type=jnp.float32
    )
    down_part = jnp.einsum("tf,td->fd", hidden, full_cotangent, preferred_element_type=jnp.float32)
    d_gate = (d_hidden * up_proj * sigmoid_gate * (1.0 + gate * (1.0 - sigmoid_gate))).astype(
        jnp.bfloat16
    )
    d_up = (d_hidden * silu_gate).astype(jnp.bfloat16)
    gate_part = jnp.einsum("td,tf->df", normed_two, d_gate, preferred_element_type=jnp.float32)
    up_part = jnp.einsum("td,tf->df", normed_two, d_up, preferred_element_type=jnp.float32)
    d_normed_two = jnp.einsum(
        "tf,df->td", d_gate, gate_full, preferred_element_type=jnp.float32
    ) + jnp.einsum("tf,df->td", d_up, up_full, preferred_element_type=jnp.float32)
    grad_two, sum_two, cross_two = (
        lax.psum_scatter(
            d_normed_two.astype(jnp.bfloat16), "col", scatter_dimension=1, tiled=True
        ).astype(jnp.float32),
        lax.psum_scatter(
            spread_cols(jnp.sum(d_normed_two, axis=1), col_count).astype(jnp.bfloat16),
            "col",
            scatter_dimension=1,
            tiled=True,
        ).astype(jnp.float32),
        lax.psum_scatter(
            spread_cols(jnp.sum(d_normed_two * unit_two, axis=1), col_count).astype(jnp.bfloat16),
            "col",
            scatter_dimension=1,
            tiled=True,
        ).astype(jnp.float32),
    )
    unit_two_here = lax.dynamic_slice_in_dim(unit_two, col_index * part_width, part_width, 1)
    d_middle = cotangent.astype(jnp.float32) + normalize_back(
        grad_two, sum_two, cross_two, unit_two_here, inverse_two, full_width
    )
    d_branch = d_middle.astype(jnp.bfloat16)
    d_branch_full = lax.all_gather(d_branch, "col", axis=1, tiled=True)
    out_part = jnp.einsum(
        "tc,td->cd", attended_flat, d_branch_full, preferred_element_type=jnp.float32
    )
    d_attended = jnp.einsum(
        "td,cd->tc", d_branch_full, out_full, preferred_element_type=jnp.float32
    )
    d_attended = d_attended.astype(jnp.bfloat16).reshape(tok_rows, heads_here, head_size)
    delta_rows = jnp.zeros((heads_here, tok_rows, 1), jnp.float32)
    for shift_by in range(group_span):

        def add_delta(total, shift_by=shift_by):
            scores = score_block(queries, pieces[shift_by][0], visibility[shift_by], score_scale)
            probs_full = jnp.exp(scores - log_total)
            d_probs = jnp.einsum(
                "qhd,khd->hqk", d_attended, pieces[shift_by][1], preferred_element_type=jnp.float32
            )
            return total + jnp.sum(probs_full * d_probs, axis=-1, keepdims=True)

        delta_rows = lax.cond(live_piece[shift_by], add_delta, lambda total: total, delta_rows)
    zero_rows = jnp.zeros((tok_rows, heads_here, head_size), jnp.float32)
    d_queries = zero_rows
    for shift_by in range(group_span):

        def piece_grads(query_total, shift_by=shift_by):
            key_part, value_part = pieces[shift_by]
            scores = score_block(queries, key_part, visibility[shift_by], score_scale)
            probs_full = jnp.exp(scores - log_total)
            d_probs = jnp.einsum(
                "qhd,khd->hqk", d_attended, value_part, preferred_element_type=jnp.float32
            )
            d_scores = (probs_full * (d_probs - delta_rows)).astype(jnp.bfloat16)
            query_total = (
                query_total
                + jnp.einsum("hqk,khd->qhd", d_scores, key_part, preferred_element_type=jnp.float32)
                * score_scale
            )
            d_key_part = (
                jnp.einsum("hqk,qhd->khd", d_scores, queries, preferred_element_type=jnp.float32)
                * score_scale
            )
            d_value_part = jnp.einsum(
                "hqk,qhd->khd",
                probs_full.astype(jnp.bfloat16),
                d_attended,
                preferred_element_type=jnp.float32,
            )
            return (query_total, d_key_part, d_value_part)

        d_queries, d_key_part, d_value_part = lax.cond(
            live_piece[shift_by],
            piece_grads,
            lambda query_total: (query_total, zero_rows, zero_rows),
            d_queries,
        )
        if shift_by == 0:
            d_keys = d_key_part
            d_values = d_value_part
        else:
            back_keys, back_values = (
                passed_along(
                    d_key_part.astype(jnp.bfloat16), "row", -shift_by * groups_here
                ).astype(d_key_part.dtype),
                passed_along(
                    d_value_part.astype(jnp.bfloat16), "row", -shift_by * groups_here
                ).astype(d_value_part.dtype),
            )
            d_keys = d_keys + back_keys
            d_values = d_values + back_values
    raw_score_gradient = jnp.stack(
        [rotate(d_queries, cosine, sine, True), rotate(d_keys, cosine, sine, True), d_values],
        axis=1,
    )
    raw_score_gradient = raw_score_gradient.reshape(tok_rows, 3, part_width).astype(jnp.bfloat16)
    projection_part_rows = jnp.einsum(
        "lo,lbw->obw", first_normed_input, raw_score_gradient, preferred_element_type=jnp.float32
    )
    first_normed_gradient = jnp.einsum(
        "xzq,vzq->xv", raw_score_gradient, projection_full_rows, preferred_element_type=jnp.float32
    )
    grad_one, sum_one, cross_one = (
        lax.psum_scatter(
            first_normed_gradient.astype(jnp.bfloat16), "col", scatter_dimension=1, tiled=True
        ).astype(jnp.float32),
        lax.psum_scatter(
            spread_cols(jnp.sum(first_normed_gradient, axis=1), col_count).astype(jnp.bfloat16),
            "col",
            scatter_dimension=1,
            tiled=True,
        ).astype(jnp.float32),
        lax.psum_scatter(
            spread_cols(jnp.sum(first_normed_gradient * unit_one, axis=1), col_count).astype(
                jnp.bfloat16
            ),
            "col",
            scatter_dimension=1,
            tiled=True,
        ).astype(jnp.float32),
    )
    unit_one_here = lax.dynamic_slice_in_dim(unit_one, col_index * part_width, part_width, 1)
    input_grad = d_middle + normalize_back(
        grad_one, sum_one, cross_one, unit_one_here, inverse_one, full_width
    )
    owned_grads = (
        lax.psum_scatter(
            projection_part_rows.astype(jnp.bfloat16), "row", scatter_dimension=0, tiled=True
        ).astype(jnp.float32),
        lax.psum_scatter(
            out_part.astype(jnp.bfloat16), "row", scatter_dimension=1, tiled=True
        ).astype(jnp.float32),
        lax.psum_scatter(
            gate_part.astype(jnp.bfloat16), "row", scatter_dimension=0, tiled=True
        ).astype(jnp.float32),
        lax.psum_scatter(
            up_part.astype(jnp.bfloat16), "row", scatter_dimension=0, tiled=True
        ).astype(jnp.float32),
        lax.psum_scatter(
            down_part.astype(jnp.bfloat16), "row", scatter_dimension=1, tiled=True
        ).astype(jnp.float32),
    )
    return (
        output,
        input_grad,
        owned_grads[0],
        owned_grads[1],
        owned_grads[2],
        owned_grads[3],
        owned_grads[4],
    )


def step(inputs, *rest):
    span = GROUP_LEN // inputs.shape[0]
    heads_here = inputs.shape[1] // HEAD
    fast = heads_here == span and lax.axis_size("col") == 4 and lax.axis_size("row") == 2 * span
    return (fast_body if fast else body)(inputs, *rest)


def solution(mesh):
    placed = (
        P("row", "col"),
        P("row", "col"),
        P(),
        P("row", None, "col"),
        P("col", "row"),
        P("row", "col"),
        P("row", "col"),
        P("col", "row"),
    )
    return jax.shard_map(
        step,
        mesh=mesh,
        in_specs=placed,
        out_specs=(
            P("row", "col"),
            P("row", "col"),
            P("row", None, "col"),
            P("col", "row"),
            P("row", "col"),
            P("row", "col"),
            P("col", "row"),
        ),
        check_vma=False,
    )
```

```python
import functools
import math

import jax
import jax.numpy as jnp
from jax import lax
from jax.experimental import pallas as pl
from jax.experimental.pallas import tpu as pltpu
from jax.sharding import PartitionSpec as P

HEAD = 128
PROMPT = 2048
GROUP_LEN = 4096


rope_base = 10000.0
norm_eps = 1e-05
masked_score = -1e30


def passed_along(shard, axis, by):
    size = lax.axis_size(axis)
    pairs = [(i, i + by) for i in range(size) if 0 <= i + by < size]
    return lax.ppermute(shard, axis, pairs)


def normalize_rows(values):
    centre = values - jnp.mean(values, axis=-1, keepdims=True)
    spread = jnp.mean(centre * centre, axis=-1, keepdims=True)
    inverse = lax.rsqrt(spread + norm_eps)
    return (centre * inverse, inverse)


def normalize_back(grad_rows, sum_grad, sum_cross, unit_rows, inverse, row_width):
    return inverse * (grad_rows - sum_grad / row_width - unit_rows * (sum_cross / row_width))


def spread_cols(values, copies):
    return jnp.broadcast_to(values[:, None], (values.shape[0], copies))


def token_layout(lengths, source_row, groups_count, row_count):
    valid_source = source_row >= 0
    safe_source = jnp.maximum(source_row, 0)
    group_id = jnp.where(valid_source, safe_source % groups_count, -1)
    place_here = safe_source // groups_count
    safe_group = jnp.clip(group_id, 0, lengths.shape[0] - 1)
    row_lengths = lax.dynamic_slice_in_dim(lengths, safe_group, 1, 0)[0]
    local_index = place_here * row_count + jnp.arange(row_count, dtype=jnp.int32)
    after_prompt = local_index - PROMPT
    seg_ends = jnp.cumsum(row_lengths)
    in_prompt = local_index < PROMPT
    counted = jnp.sum((after_prompt[:, None] >= seg_ends[None, :]).astype(jnp.int32), axis=1)
    segment = jnp.where(in_prompt, 0, 1 + counted)
    seg_starts = seg_ends - row_lengths
    picked = (segment - 1)[:, None] == jnp.arange(row_lengths.shape[0], dtype=jnp.int32)[None, :]
    seg_start = jnp.sum(jnp.where(picked, seg_starts[None, :], 0), axis=1)
    position = jnp.where(in_prompt, local_index, PROMPT + after_prompt - seg_start)
    return (group_id, local_index, segment, position)


def rotation_angles(position, head_size):
    half_size = head_size // 2
    frequency = jnp.exp(
        -math.log(rope_base) * (2.0 * jnp.arange(half_size, dtype=jnp.float32) / head_size)
    )
    angles = position.astype(jnp.float32)[:, None] * frequency[None, :]
    return (jnp.cos(angles)[:, None, :], jnp.sin(angles)[:, None, :])


def rotate(values, cosine, sine, inverse_turn):
    half_size = values.shape[-1] // 2
    first_half = values[..., :half_size]
    second_half = values[..., half_size:]
    if inverse_turn:
        sine = -sine
    return jnp.concatenate(
        [first_half * cosine - second_half * sine, second_half * cosine + first_half * sine],
        axis=-1,
    )


def visible_mask(query_meta, key_meta):
    query_group, query_index, query_segment, query_position = query_meta
    key_group, key_index, key_segment, key_position = key_meta
    causal = key_index[None, :] <= query_index[:, None]
    shared = (key_segment[None, :] == 0) | (key_segment[None, :] == query_segment[:, None])
    return (query_group == key_group) & causal & shared


def score_block(queries, key_part, allowed, score_scale):
    raw_scores = (
        jnp.einsum("qhd,khd->hqk", queries, key_part, preferred_element_type=jnp.float32)
        * score_scale
    )
    return jnp.where(allowed[None], raw_scores, masked_score)


BLOCK = 512
log2e = 1.4426950408889634


def turn(values, cosine, sine):
    return values * cosine + pltpu.roll(values, values.shape[1] // 2, 1) * sine


def block_mask(key_block, query_block, start_row):
    key_index = key_block * BLOCK + lax.broadcasted_iota(jnp.int32, (BLOCK, BLOCK), 0)
    query_index = query_block * BLOCK + lax.broadcasted_iota(jnp.int32, (BLOCK, BLOCK), 1)
    return (key_index <= query_index) & (key_index >= start_row)


def each_block(block, visit):
    prompt_blocks = PROMPT // BLOCK

    def whole(j, carry):
        visit(j, False)
        return carry

    lax.fori_loop(0, jnp.minimum(block, prompt_blocks), whole, 0)

    @pl.when(block > prompt_blocks)
    def _():
        visit(block - 1, True)

    visit(block, True)


MESH = pl.DeviceIdType.MESH


def place_of(place, groups_here):
    row = lax.axis_index("row")
    return (place * groups_here + lax.rem(row, groups_here), lax.axis_index("col"))


def send(source, target, send_sem, recv_sem, device):
    return pltpu.make_async_remote_copy(
        src_ref=source, dst_ref=target, send_sem=send_sem, recv_sem=recv_sem,
        device_id=device, device_id_type=MESH,
    )


def block_rows(block):
    return pl.ds(pl.multiple_of(block * BLOCK, BLOCK), BLOCK)


def col_device(by):
    return (lax.axis_index("row"), lax.axis_index("col") ^ by)


def greet_cols(count):
    barrier = pltpu.get_barrier_semaphore()
    for by in range(1, count):
        pl.semaphore_signal(barrier, inc=1, device_id=col_device(by), device_id_type=MESH)
    pl.semaphore_wait(barrier, count - 1)


class Gather:
    def __init__(self, source, slots, sends, recvs, local):
        me = lax.axis_index("col")
        a, b = source[0], source[1]
        self.own = []
        if local is not None:
            self.own = [
                pltpu.make_async_copy(a, slots(me)[0], local.at[0]),
                pltpu.make_async_copy(b, slots(me)[1], local.at[1]),
            ]

        def copy(i, what, where, by):
            return send(what, where, sends.at[i], recvs.at[i], col_device(by))

        self.first = [
            copy(0, a, slots(me)[0], 1),
            copy(3, b, slots(me)[1], 2),
            copy(1, b, slots(me)[1], 1),
            copy(2, a, slots(me)[0], 2),
        ]
        across, along = me ^ 1, me ^ 2
        self.second = [
            copy(4, slots(across)[0], slots(across)[0], 2),
            copy(5, slots(along)[1], slots(along)[1], 1),
        ]

    def start(self):
        for one in self.own + self.first:
            one.start()

    def forward(self):
        self.first[0].wait_recv()
        self.second[0].start()
        self.first[1].wait_recv()
        self.second[1].start()

    def receive(self):
        for one in self.first[2:] + self.second:
            one.wait_recv()
        for one in self.own:
            one.wait()

    def finish(self):
        for one in self.first + self.second:
            one.wait_send()


def halves(ref, start, size):
    half = size // 2
    return ref.at[pl.ds(start, half)], ref.at[pl.ds(start + half, half)]


def greet_all(me, span, groups_here, count, others=0):
    barrier = pltpu.get_barrier_semaphore()
    for by in range(1, span):
        pl.semaphore_signal(
            barrier, inc=1, device_id=place_of(lax.rem(me + by, span), groups_here), device_id_type=MESH
        )
    for by in range(1, count):
        pl.semaphore_signal(barrier, inc=1, device_id=col_device(by), device_id_type=MESH)
    pl.semaphore_wait(barrier, span + count - 2 + others)


def attend_kernel(
    groups_here, sent_ref, start_ref, rider_ref, back_ref, held_ref, o_ref, lse_ref, riders_ref,
    qkv_ref, top_ref, total_ref, sum_ref,
    in_send, in_recv, out_send, out_recv, keep_sem, own_sem, ride_send, ride_recv, ride_local,
):
    span, _, tokens, _ = sent_ref.shape
    me = lax.axis_index("row") // groups_here
    blocks = start_ref.shape[0]
    per_place = tokens // BLOCK
    scale = HEAD**-0.5 * log2e
    greet_all(me, span, groups_here, riders_ref.shape[0])
    half = rider_ref.shape[0] // 2
    ride = Gather(
        (rider_ref.at[:half, 3], rider_ref.at[half:, 3]),
        lambda c: (riders_ref.at[c, :half], riders_ref.at[c, half:]),
        ride_send, ride_recv, ride_local,
    )

    def qkv_copy(by):
        peer = lax.rem(me + by, span)
        return send(
            sent_ref.at[peer], qkv_ref.at[:, pl.ds(pl.multiple_of(me * tokens, tokens), tokens)],
            in_send.at[by], in_recv.at[by], place_of(peer, groups_here),
        )

    own_rows = pl.ds(pl.multiple_of(me * tokens, tokens), tokens)
    own_copy = pltpu.make_async_copy(sent_ref.at[me], qkv_ref.at[:, own_rows], in_recv.at[0])
    own_copy.start()
    for by in range(1, span):
        qkv_copy(by).start()
    ride.start()

    def out_copy(block):
        to = block // per_place
        half = lax.rem(block, per_place)
        by = lax.rem(to - me + span, span)
        return send(
            o_ref.at[block_rows(block)], back_ref.at[me, block_rows(half)],
            out_send.at[block], out_recv.at[by, half], place_of(to, groups_here),
        )

    def own_out(block):
        return pltpu.make_async_copy(
            o_ref.at[block_rows(block)],
            back_ref.at[me, block_rows(lax.rem(block, per_place))],
            own_sem.at[lax.rem(block, per_place)],
        )

    def keep_copy(place):
        rows = pl.ds(pl.multiple_of(place * tokens, tokens), tokens)
        return pltpu.make_async_copy(qkv_ref.at[:, rows], held_ref.at[:, rows], keep_sem.at[place])

    def one_block(block, carry):
        place = block // per_place

        @pl.when(lax.rem(block, per_place) == 0)
        def _():
            @pl.when(place == me)
            def _():
                own_copy.wait()

            for by in range(1, span):

                @pl.when(lax.rem(place + by, span) == me)
                def _():
                    qkv_copy(by).wait_recv()

            keep_copy(place).start()

        top_ref[...] = jnp.full_like(top_ref, masked_score)
        total_ref[...] = jnp.zeros_like(total_ref)
        sum_ref[...] = jnp.zeros_like(sum_ref)
        queries = qkv_ref[0, block_rows(block), :]
        start_row = start_ref[block]

        def visit(j, masked):
            rows = block_rows(j)
            scores = scale * matmul_nt(qkv_ref[1, rows, :], queries)
            if masked:
                scores = jnp.where(block_mask(j, block, start_row), scores, masked_score)
            old_top = top_ref[...]
            new_top = jnp.maximum(old_top, jnp.max(scores, axis=0, keepdims=True))
            shrink = jnp.exp2(old_top - new_top)
            probs = jnp.exp2(scores - new_top)
            if masked:
                probs = jnp.where(scores > 0.5 * masked_score, probs, 0.0)
            total_ref[...] = total_ref[...] * shrink + jnp.sum(probs, axis=0, keepdims=True)
            sum_ref[...] = sum_ref[...] * shrink + lax.dot_general(
                qkv_ref[2, rows, :],
                probs.astype(jnp.bfloat16),
                (((0,), (0,)), ((), ())),
                preferred_element_type=jnp.float32,
            )
            top_ref[...] = new_top

        each_block(block, visit)
        total = total_ref[...]
        o_ref[block_rows(block), :] = (sum_ref[...] / total).T.astype(jnp.bfloat16)
        lse_ref[block] = top_ref[...] + jnp.log2(total)

        @pl.when(place == me)
        def _():
            own_out(block).start()

        @pl.when(place != me)
        def _():
            out_copy(block).start()

        @pl.when(block == blocks // 2)
        def _():
            ride.forward()

        return carry

    lax.fori_loop(0, blocks, one_block, 0)
    ride.receive()
    ride.finish()

    for by in range(1, span):
        qkv_copy(by).wait_send()

    def finish(block, carry):
        place = block // per_place

        @pl.when(place == me)
        def _():
            own_out(block).wait()

        @pl.when(place != me)
        def _():
            out_copy(block).wait_send()

        return carry

    lax.fori_loop(0, blocks, finish, 0)
    for by in range(1, span):
        for half in range(per_place):
            send(
                o_ref.at[block_rows(half)], back_ref.at[lax.rem(me - by + span, span), block_rows(half)],
                out_send.at[half], out_recv.at[by, half], place_of(me, groups_here),
            ).wait_recv()
    for place in range(span):
        keep_copy(place).wait()


def attend(sent, start_rows, rider, groups_here, count):
    span, _, tokens, size = sent.shape
    blocks = start_rows.shape[0]
    length = span * tokens
    hbm = pl.BlockSpec(memory_space=pl.ANY)
    vmem = pl.BlockSpec(memory_space=pltpu.VMEM)
    per_place = tokens // BLOCK
    dma = pltpu.SemaphoreType.DMA
    return pl.pallas_call(
        functools.partial(attend_kernel, groups_here),
        in_specs=[hbm, vmem, hbm],
        out_specs=[hbm, hbm, vmem, vmem, hbm],
        out_shape=[
            jax.ShapeDtypeStruct((span, tokens, size), jnp.bfloat16),
            jax.ShapeDtypeStruct((3, length, size), jnp.bfloat16),
            jax.ShapeDtypeStruct((length, size), jnp.bfloat16),
            jax.ShapeDtypeStruct((blocks, 1, BLOCK), jnp.float32),
            jax.ShapeDtypeStruct((count, rider.shape[0], *rider.shape[2:]), jnp.bfloat16),
        ],
        scratch_shapes=[
            pltpu.VMEM((3, length, size), jnp.bfloat16),
            pltpu.VMEM((1, BLOCK), jnp.float32),
            pltpu.VMEM((1, BLOCK), jnp.float32),
            pltpu.VMEM((size, BLOCK), jnp.float32),
            dma((span,)), dma((span,)), dma((blocks,)), dma((span, per_place)), dma((span,)),
            dma((per_place,)), dma((6,)), dma((6,)), dma((2,)),
        ],
        compiler_params=pltpu.CompilerParams(
            vmem_limit_bytes=32 * 2**20, collective_id=1, has_side_effects=True
        ),
        cost_estimate=pl.CostEstimate(
            flops=length * length * size * 2, bytes_accessed=length * size * 200,
            transcendentals=length * length // 2,
        ),
        name="attend",
    )(sent, start_rows, rider)


def back_tables(position):
    lane = lax.broadcasted_iota(jnp.int32, (1, HEAD), 1)
    half = HEAD // 2
    frequency = jnp.exp(-math.log(rope_base) * (2.0 * (lane % half).astype(jnp.float32) / HEAD))
    angles = jnp.broadcast_to(position, (HEAD, BLOCK)).T * frequency
    sine = jnp.sin(angles)
    return jnp.cos(angles), jnp.where(lane < half, sine, -sine)


def attend_back_kernel(
    groups_here, d_sent_ref, qkv_ref, o_ref, lse_ref, start_ref, place_ref, rider_ref,
    middle_ref, d_raw_ref, output_ref, cos_ref, sin_ref, riders_ref, own_ride_ref, do_ref, stage_ref, dq_sum, dk_sum, dv_sum,
    in_send, in_recv, q_send, q_recv, kv_send, kv_recv, own_sem, ride_send, ride_recv, ride_own,
):
    span, tokens, _ = d_sent_ref.shape
    me = lax.axis_index("row") // groups_here
    blocks = start_ref.shape[0]
    per_place = tokens // BLOCK
    after = blocks - PROMPT // BLOCK
    scale = HEAD**-0.5
    greet_all(me, span, groups_here, rider_ref.shape[0])
    ride = Scatter(
        rider_ref, riders_ref, None, None, pl.ds(0, tokens), ride_send, ride_recv
    )
    own_rows = pl.ds(pl.multiple_of(me * tokens, tokens), tokens)

    def do_copy(by):
        peer = lax.rem(me + by, span)
        return send(
            d_sent_ref.at[peer], do_ref.at[own_rows], in_send.at[by], in_recv.at[by],
            place_of(peer, groups_here),
        )

    own_copy = pltpu.make_async_copy(d_sent_ref.at[me], do_ref.at[own_rows], in_recv.at[0])
    own_copy.start()
    for by in range(1, span):
        do_copy(by).start()
    ride.start()
    own_ride = pltpu.make_async_copy(rider_ref.at[lax.axis_index("col")], own_ride_ref, ride_own)
    own_ride.start()
    dk_sum[...] = jnp.zeros_like(dk_sum)
    dv_sum[...] = jnp.zeros_like(dv_sum)

    def moved(block, which):
        to = block // per_place
        half = lax.rem(block, per_place)
        by = lax.rem(to - me + span, span)
        kinds = pl.ds(1, 2) if which else pl.ds(0, 1)
        source = stage_ref.at[kinds, block_rows(block)]
        target = d_raw_ref.at[me, kinds, block_rows(half)]
        sends, recvs = (kv_send, kv_recv) if which else (q_send, q_recv)
        return (
            to == me,
            pltpu.make_async_copy(source, target, own_sem.at[which, half]),
            send(source, target, sends.at[block], recvs.at[by, half], place_of(to, groups_here)),
        )

    def start_move(block, which):
        mine, local, remote = moved(block, which)

        @pl.when(mine)
        def _():
            local.start()

        @pl.when(jnp.logical_not(mine))
        def _():
            remote.start()

    def close(j):
        rows = block_rows(j)
        stage_ref[1, rows, :] = turn(
            dk_sum[rows, :] * scale, cos_ref[rows, :], sin_ref[rows, :]
        ).astype(jnp.bfloat16)
        stage_ref[2, rows, :] = dv_sum[rows, :].astype(jnp.bfloat16)
        start_move(j, 1)

    def one_block(n, carry):
        block = jnp.where(n < after, blocks - after + n, blocks - 1 - n)
        place = block // per_place

        @pl.when(lax.rem(n, per_place) == 0)
        def _():
            @pl.when(place == me)
            def _():
                own_copy.wait()

            for by in range(1, span):

                @pl.when(lax.rem(place + by, span) == me)
                def _():
                    do_copy(by).wait_recv()

        dq_sum[...] = jnp.zeros_like(dq_sum)
        here = block_rows(block)
        cos_ref[here, :], sin_ref[here, :] = back_tables(place_ref[block])
        queries = qkv_ref[0, here, :]
        d_out = do_ref[here, :]
        lse = lse_ref[block]
        start_row = start_ref[block]
        delta = jnp.sum(
            (d_out.astype(jnp.float32) * o_ref[here, :].astype(jnp.float32)).T, axis=0, keepdims=True
        )

        def visit(j, masked):
            rows = block_rows(j)
            key_part = qkv_ref[1, rows, :]
            scores = (scale * log2e) * matmul_nt(key_part, queries)
            if masked:
                scores = jnp.where(block_mask(j, block, start_row), scores, masked_score)
            probs = jnp.exp2(scores - lse)
            d_probs = matmul_nt(qkv_ref[2, rows, :], d_out)
            d_scores = (probs * (d_probs - delta)).astype(jnp.bfloat16)
            dv_sum[rows, :] += matmul(probs.astype(jnp.bfloat16), d_out)
            dk_sum[rows, :] += matmul(d_scores, queries)
            dq_sum[...] += lax.dot_general(
                key_part, d_scores, (((0,), (0,)), ((), ())), preferred_element_type=jnp.float32
            )

        each_block(block, visit)
        stage_ref[0, here, :] = turn(
            dq_sum[...].T * scale, cos_ref[here, :], sin_ref[here, :]
        ).astype(jnp.bfloat16)
        start_move(block, 0)

        @pl.when((n >= 1) & (n < after))
        def _():
            close(block - 1)

        @pl.when(n >= after - 1)
        def _():
            close(block)

        return carry

    lax.fori_loop(0, blocks, one_block, 0)
    ride.receive()
    own_ride.wait()

    def add_up(here):
        total = middle_ref[here, :] + own_ride_ref[here, :].astype(jnp.float32)
        for by in range(riders_ref.shape[0]):
            total = total + riders_ref[by, here, :].astype(jnp.float32)
        output_ref[here, :] = total.astype(jnp.bfloat16)

    each_rows(0, tokens, 128, add_up)
    ride.finish()
    for by in range(1, span):
        do_copy(by).wait_send()

    def finish(block, carry):
        for which in range(2):
            mine, local, remote = moved(block, which)

            @pl.when(mine)
            def _():
                local.wait()

            @pl.when(jnp.logical_not(mine))
            def _():
                remote.wait_send()

        return carry

    lax.fori_loop(0, blocks, finish, 0)
    for by in range(1, span):
        source = lax.rem(me - by + span, span)
        for half in range(per_place):
            for which in range(2):
                kinds = pl.ds(1, 2) if which else pl.ds(0, 1)
                sends, recvs = (kv_send, kv_recv) if which else (q_send, q_recv)
                send(
                    stage_ref.at[kinds, block_rows(half)], d_raw_ref.at[source, kinds, block_rows(half)],
                    sends.at[half], recvs.at[by, half], place_of(me, groups_here),
                ).wait_recv()


def attend_back(d_sent, held, out, lse, start_rows, positions, rider, middle, groups_here):
    span, tokens, size = d_sent.shape
    blocks = start_rows.shape[0]
    length = span * tokens
    hbm = pl.BlockSpec(memory_space=pl.ANY)
    vmem = pl.BlockSpec(memory_space=pltpu.VMEM)
    per_place = tokens // BLOCK
    dma = pltpu.SemaphoreType.DMA
    return pl.pallas_call(
        functools.partial(attend_back_kernel, groups_here),
        in_specs=[hbm] + [vmem] * 5 + [hbm, vmem],
        out_specs=[hbm, vmem],
        out_shape=[
            jax.ShapeDtypeStruct((span, 3, tokens, size), jnp.bfloat16),
            jax.ShapeDtypeStruct(rider.shape[1:], jnp.bfloat16),
        ],
        scratch_shapes=[
            pltpu.VMEM((length, size), jnp.float32),
            pltpu.VMEM((length, size), jnp.float32),
            pltpu.VMEM((rider.shape[0] - 1, *rider.shape[1:]), jnp.bfloat16),
            pltpu.VMEM(rider.shape[1:], jnp.bfloat16),
            pltpu.VMEM((length, size), jnp.bfloat16),
            pltpu.VMEM((3, length, size), jnp.bfloat16),
            pltpu.VMEM((size, BLOCK), jnp.float32),
            pltpu.VMEM((length, size), jnp.float32),
            pltpu.VMEM((length, size), jnp.float32),
            dma((span,)), dma((span,)), dma((blocks,)), dma((span, per_place)), dma((blocks,)),
            dma((span, per_place)), dma((2, per_place)), dma((1, rider.shape[0] - 1)),
            dma((1, rider.shape[0] - 1)), dma,
        ],
        compiler_params=pltpu.CompilerParams(
            vmem_limit_bytes=48 * 2**20, collective_id=2, has_side_effects=True
        ),
        cost_estimate=pl.CostEstimate(
            flops=length * length * size * 5, bytes_accessed=length * size * 200,
            transcendentals=length * length // 2,
        ),
        name="attend_back",
    )(d_sent, held, out, lse, start_rows, positions, rider, middle)


def matmul(a, b):
    return jnp.dot(a, b, preferred_element_type=jnp.float32)


def matmul_nt(a, b):
    return lax.dot_general(a, b, (((1,), (1,)), ((), ())), preferred_element_type=jnp.float32)


def resident(shape):
    zeros = (0,) * len(shape)
    return pl.BlockSpec(shape, lambda *_: zeros, pipeline_mode=pl.Buffered(1))


def own_width(ref, width, col):
    return ref[:, pl.ds(pl.multiple_of(col * width, width), width)]


def enter_kernel(
    inputs_ref, cot_ref, pieces_ref, cots_ref, unit_ref, unit_t_ref, own_ref, inverse_ref,
    held_ref, rows_ref, sends, recvs, local, keep,
):
    count, rows, piece = held_ref.shape
    col = lax.axis_index("col")
    greet_cols(count)
    first = Gather(
        halves(inputs_ref, 0, rows), lambda c: halves(held_ref.at[c], 0, rows),
        sends.at[0], recvs.at[0], local.at[0],
    )
    second = Gather(
        halves(cot_ref, 0, rows), lambda c: halves(cots_ref.at[c], 0, rows),
        sends.at[1], recvs.at[1], local.at[1],
    )
    first.start()
    first.forward()
    second.start()
    first.receive()
    out = pltpu.make_async_copy(held_ref, pieces_ref, keep)
    out.start()

    def norm(t, carry):
        here = pl.ds(pl.multiple_of(t * 128, 128), 128)
        parts = [held_ref[c, here, :].astype(jnp.float32) for c in range(count)]
        unit, inverse = normalize_rows(jnp.concatenate(parts, axis=1))
        rows_ref[...] = unit
        unit = unit.astype(jnp.bfloat16)
        unit_ref[here, :] = unit
        unit_t_ref[:, here] = unit.T
        own_ref[here, :] = own_width(rows_ref, piece, col)
        inverse_ref[here, :] = jnp.broadcast_to(inverse, (128, 128))
        return carry

    lax.fori_loop(0, rows // 128, norm, 0)
    second.forward()
    second.receive()
    first.finish()
    second.finish()
    out.wait()


def enter(inputs, cotangent, count):
    rows, piece = inputs.shape
    width = count * piece
    hbm = pl.BlockSpec(memory_space=pl.ANY)
    vmem = pl.BlockSpec(memory_space=pltpu.VMEM)
    dma = pltpu.SemaphoreType.DMA
    shape = jax.ShapeDtypeStruct
    return pl.pallas_call(
        enter_kernel,
        in_specs=[hbm, hbm],
        out_specs=[hbm, hbm, vmem, vmem, vmem, vmem],
        out_shape=[
            shape((count, rows, piece), jnp.bfloat16),
            shape((count, rows, piece), jnp.bfloat16),
            shape((rows, width), jnp.bfloat16),
            shape((width, rows), jnp.bfloat16),
            shape((rows, piece), jnp.float32),
            shape((rows, 128), jnp.float32),
        ],
        scratch_shapes=[
            pltpu.VMEM((count, rows, piece), jnp.bfloat16),
            pltpu.VMEM((128, width), jnp.float32),
            dma((2, 6)), dma((2, 6)), dma((2, 2)), dma,
        ],
        compiler_params=pltpu.CompilerParams(
            vmem_limit_bytes=40 * 2**20, collective_id=3, has_side_effects=True
        ),
        cost_estimate=pl.CostEstimate(
            flops=10 * rows * width, bytes_accessed=100 * rows * width, transcendentals=0
        ),
        name="enter",
    )(inputs, cotangent)


def own_width(ref, width, col):
    return ref[:, pl.ds(pl.multiple_of(col * width, width), width)]


def project_kernel(unit_ref, weight_ref, cos_ref, sin_ref, out_ref):
    kind = pl.program_id(0)
    rows, width = unit_ref.shape
    heads = out_ref.shape[0]
    weight = weight_ref[:, 0].reshape(width, heads * HEAD)
    step = min(256, rows)
    for t in range(0, rows, step):
        here = pl.ds(t, step)
        raw = matmul(unit_ref[here, :], weight)

        @pl.when(kind < 2)
        def _():
            cosine, sine = cos_ref[here, :], sin_ref[here, :]
            for h in range(heads):
                part = turn(raw[:, h * HEAD : (h + 1) * HEAD], cosine, -sine)
                out_ref[h, 0, here, :] = part.astype(jnp.bfloat16)

        @pl.when(kind == 2)
        def _():
            for h in range(heads):
                out_ref[h, 0, here, :] = raw[:, h * HEAD : (h + 1) * HEAD].astype(jnp.bfloat16)


def project(unit, weight, cosine, sine):
    rows, width = unit.shape
    owners, _, depth, columns = weight.shape
    kinds = 3
    heads = columns // HEAD
    return pl.pallas_call(
        project_kernel,
        grid=(kinds,),
        in_specs=[
            resident((rows, width)),
            pl.BlockSpec((owners, 1, depth, columns), lambda k: (0, k, 0, 0)),
            resident((rows, HEAD)),
            resident((rows, HEAD)),
        ],
        out_specs=pl.BlockSpec((heads, 1, rows, HEAD), lambda k: (0, k, 0, 0)),
        out_shape=jax.ShapeDtypeStruct((heads, kinds, rows, HEAD), jnp.bfloat16),
        compiler_params=pltpu.CompilerParams(vmem_limit_bytes=40 * 2**20),
        cost_estimate=pl.CostEstimate(
            flops=2 * rows * width * kinds * columns, bytes_accessed=2 * width * kinds * columns,
            transcendentals=0,
        ),
        name="project",
    )(unit, weight, cosine, sine)


def branch_kernel(
    back_ref, weight_ref, pieces_ref, unit_ref, unit_t_ref, middle_ref, own_ref, inverse_ref,
    heads_ref, flat_ref, rows_ref, terms_ref, sends, recvs, local,
):
    col = lax.axis_index("col")
    count, heads, rows, size = heads_ref.shape
    piece = pieces_ref.shape[2]
    greet_cols(count)
    parts = 2
    span = rows // parts

    def cut(ref, p):
        half = span // 2
        return (
            ref.at[:, pl.ds(p * span, half)],
            ref.at[:, pl.ds(p * span + half, half)],
        )

    gathers = [
        Gather(
            cut(back_ref, p), lambda c, p=p: cut(heads_ref.at[c], p),
            sends.at[p], recvs.at[p], local.at[p],
        )
        for p in range(parts)
    ]
    gathers[0].start()
    for p in range(parts):
        gathers[p].forward()
        if p + 1 < parts:
            gathers[p + 1].start()
        gathers[p].receive()
        for c in range(count):
            for h in range(heads):
                at = (c * heads + h) * size
                flat_ref[:, at : at + size] = heads_ref[c, h, pl.ds(p * span, span), :]
        terms_ref[...] = jnp.zeros_like(terms_ref)

        def add_col(c, carry):
            part = flat_ref[:, pl.ds(pl.multiple_of(c * piece, piece), piece)]
            terms_ref[...] += matmul_nt(part, weight_ref[c])
            return carry

        lax.fori_loop(0, count, add_col, 0)

        def finish(t, carry):
            inner = pl.ds(pl.multiple_of(t * 128, 128), 128)
            here = pl.ds(pl.multiple_of(p * span + t * 128, 128), 128)
            rest = [pieces_ref[c, here, :].astype(jnp.float32) for c in range(count)]
            middle = jnp.concatenate(rest, axis=1) + terms_ref[inner, :]
            rows_ref[...] = middle
            middle_ref[here, :] = own_width(rows_ref, piece, col)
            unit, inverse = normalize_rows(middle)
            rows_ref[...] = unit
            own_ref[here, :] = own_width(rows_ref, piece, col)
            inverse_ref[here, :] = jnp.broadcast_to(inverse, (128, 128))
            unit = unit.astype(jnp.bfloat16)
            unit_ref[here, :] = unit
            unit_t_ref[:, here] = unit.T
            return carry

        lax.fori_loop(0, span // 128, finish, 0)
    for one in gathers:
        one.finish()


def branch(back, weight, pieces):
    heads, rows, size = back.shape
    count, _, piece = pieces.shape
    width = count * piece
    hbm = pl.BlockSpec(memory_space=pl.ANY)
    vmem = pl.BlockSpec(memory_space=pltpu.VMEM)
    dma = pltpu.SemaphoreType.DMA
    shape = jax.ShapeDtypeStruct
    return pl.pallas_call(
        branch_kernel,
        in_specs=[hbm, vmem, vmem],
        out_specs=[vmem] * 5,
        out_shape=[
            shape((rows, width), jnp.bfloat16),
            shape((width, rows), jnp.bfloat16),
            shape((rows, piece), jnp.float32),
            shape((rows, piece), jnp.float32),
            shape((rows, 128), jnp.float32),
        ],
        scratch_shapes=[
            pltpu.VMEM((count, heads, rows, size), jnp.bfloat16),
            pltpu.VMEM((rows // 2, width), jnp.bfloat16),
            pltpu.VMEM((128, width), jnp.float32),
            pltpu.VMEM((rows // 2, width), jnp.float32),
            dma((2, 6)), dma((2, 6)), dma((2, 2)),
        ],
        compiler_params=pltpu.CompilerParams(
            vmem_limit_bytes=56 * 2**20, collective_id=4, has_side_effects=True
        ),
        cost_estimate=pl.CostEstimate(
            flops=2 * rows * width * width, bytes_accessed=40 * width * width, transcendentals=0
        ),
        name="branch",
    )(back, weight, pieces)


def each_rows(start, size, step, visit):
    def body(t, carry):
        visit(pl.ds(pl.multiple_of(start + t * step, step), step))
        return carry

    lax.fori_loop(0, size // step, body, 0)


def stats_of(values, unit):
    rows = values.shape[0]
    lane = lax.broadcasted_iota(jnp.int32, (rows, 128), 1)
    both = jnp.where(
        lane % 8 < 4,
        jnp.sum(values, axis=1, keepdims=True),
        jnp.sum(values * unit, axis=1, keepdims=True),
    )
    return both.T[:8]


def columns_of(stats):
    back = jnp.concatenate([stats] * 16, axis=0).T
    return back[:, :1], back[:, 4:5]


class Scatter:
    def __init__(self, pieces, slots, stats, stat_slots, here, sends, recvs):
        me = lax.axis_index("col")
        self.copies = []
        for by in range(1, pieces.shape[0]):
            device = col_device(by)
            self.copies.append(
                send(pieces.at[me ^ by, here], slots.at[by - 1, here],
                     sends.at[0, by - 1], recvs.at[0, by - 1], device)
            )
            if stats is not None:
                self.copies.append(
                    send(stats.at[:, here], stat_slots.at[by - 1, :, here],
                         sends.at[1, by - 1], recvs.at[1, by - 1], device)
                )

    def start(self):
        for one in self.copies:
            one.start()

    def receive(self):
        for one in self.copies:
            one.wait_recv()

    def finish(self):
        for one in self.copies:
            one.wait_send()


class Fold:
    def __init__(self, pieces, slots, stats, stat_slots, start, size, sends, recvs):
        me = lax.axis_index("col")
        half = size // 2
        self.pieces, self.slots = pieces, slots
        self.firsts, self.sums, self.seconds, self.stats = [], [], [], []

        def copy(i, source, target, by):
            return send(source, target, sends.at[i], recvs.at[i], col_device(by))

        for i, (by, then) in enumerate(((1, 2), (2, 1))):
            here = pl.ds(pl.multiple_of(start + i * half, half), half)
            self.firsts.append(
                [
                    copy(3 * i, pieces.at[me ^ by, here], slots.at[0, here], by),
                    copy(3 * i + 1, pieces.at[me ^ 3, here], slots.at[1, here], by),
                ]
            )
            self.sums.append((me ^ then, here))
            self.seconds.append(copy(3 * i + 2, pieces.at[me ^ then, here], slots.at[2, here], then))
        rows = pl.ds(pl.multiple_of(start, size), size)
        for by in (1, 2, 3):
            self.stats.append(copy(5 + by, stats.at[:, rows], stat_slots.at[by - 1, :, rows], by))

    def start(self):
        for one in self.firsts[0] + self.firsts[1] + self.stats:
            one.start()

    def forward(self):
        for first, (to, here), second in zip(self.firsts, self.sums, self.seconds):
            for one in first:
                one.wait_recv()
            total = self.pieces[to, here, :].astype(jnp.float32) + self.slots[1, here, :].astype(
                jnp.float32
            )
            self.pieces[to, here, :] = total.astype(jnp.bfloat16)
            second.start()

    def receive(self):
        for one in self.seconds + self.stats:
            one.wait_recv()

    def finish(self):
        for one in self.firsts[0] + self.firsts[1] + self.seconds + self.stats:
            one.wait_send()


def split_rows(sum_ref, unit_ref, pieces_ref, stats_ref, start, size):
    count, _, width = pieces_ref.shape

    def part(here):
        values = sum_ref[here, :]
        stats_ref[:, here] = stats_of(values, unit_ref[here, :].astype(jnp.float32))
        for c in range(count):
            pieces_ref[c, here, :] = values[:, c * width : (c + 1) * width].astype(jnp.bfloat16)

    each_rows(start, size, 128, part)


def normed_grad(sum_ref, slots, stats_ref, stat_slots, own_ref, inverse_ref, here, width, col):
    piece = slots.shape[2]
    grad = sum_ref[here, pl.ds(pl.multiple_of(col * piece, piece), piece)]
    grad = grad + slots[0, here, :].astype(jnp.float32) + slots[2, here, :].astype(jnp.float32)
    stats = stats_ref[:, here]
    for by in range(stat_slots.shape[0]):
        stats = stats + stat_slots[by, :, here]
    sums, cross = columns_of(stats)
    return normalize_back(grad, sums, cross, own_ref[here, :], inverse_ref[here, :1], float(width))


class LineSum:
    def __init__(self, grads, cross, slots, groups_here, sems):
        self.grads, self.cross, self.slots, self.groups = grads, cross, slots, groups_here
        self.core_send, self.core_recv, self.hop_send, self.hop_recv = sems
        self.span = grads.shape[0] // groups_here
        row = lax.axis_index("row")
        self.me, self.group = row // groups_here, lax.rem(row, groups_here)
        self.partner = (row + 1 - 2 * self.group, lax.axis_index("col"))

    def owner(self, place, other):
        group = 1 - self.group if other else self.group
        return jnp.clip(place, 0, self.span - 1) * self.groups + group

    def across(self, place):
        return send(
            self.grads.at[self.owner(place, True)], self.cross.at[place], self.core_send.at[place],
            self.core_recv.at[place], self.partner,
        )

    def join(self, place):
        self.across(place).wait_recv()
        owner = self.owner(place, False)
        for k in range(self.grads.shape[1]):
            total = self.grads[owner, k].astype(jnp.float32) + self.cross[place, k].astype(jnp.float32)
            self.grads[owner, k] = total.astype(jnp.bfloat16)

    def hop(self, way, r):
        i = (1 - way) // 2
        to = self.me + way * (self.span - r)
        behind = self.me if way > 0 else self.span - 1 - self.me
        copy = send(
            self.grads.at[self.owner(to, False)], self.slots.at[i, r - 1], self.hop_send.at[i, r - 1],
            self.hop_recv.at[i, r - 1],
            place_of(jnp.clip(self.me + way, 0, self.span - 1), self.groups),
        )
        return behind <= r - 1, (behind >= 1) & (behind <= r), to, copy

    def start(self, r):
        for way in (1, -1):
            i = (1 - way) // 2
            sends, _, to, copy = self.hop(way, r)
            if r > 1:
                _, came, _, before = self.hop(way, r - 1)

                @pl.when(came)
                def _():
                    before.wait_recv()

                @pl.when(came & sends)
                def _():
                    owner = self.owner(to, False)
                    for k in range(self.grads.shape[1]):
                        total = self.grads[owner, k].astype(jnp.float32) + self.slots[
                            i, r - 2, k
                        ].astype(jnp.float32)
                        self.grads[owner, k] = total.astype(jnp.bfloat16)

            @pl.when(sends)
            def _():
                copy.start()

    def result(self, out_ref):
        last = self.span - 1
        own = self.owner(self.me, False)
        for k in range(self.grads.shape[1]):
            out_ref[k] = self.grads[own, k].astype(jnp.float32)
        for way in (1, -1):
            _, came, _, copy = self.hop(way, last)

            @pl.when(came)
            def _():
                copy.wait_recv()
                for k in range(self.grads.shape[1]):
                    out_ref[k] += self.slots[(1 - way) // 2, last - 1, k].astype(jnp.float32)

    def finish(self):
        for place in range(self.span):
            self.across(place).wait_send()
        for r in range(1, self.span):
            for way in (1, -1):
                sends, _, _, copy = self.hop(way, r)

                @pl.when(sends)
                def _():
                    copy.wait_send()


def leave_kernel(
    groups_here, d_raw_ref, weight_ref, unit_t_ref, unit_ref, own_ref, inverse_ref, d_middle_ref,
    out_ref, grad_ref,
    rows_ref, sum_ref, pieces_ref, slots_ref, stats_ref, stat_slots_ref, weights_ref, turned_ref,
    parts_ref, cross_ref, line_ref,
    sends, recvs, load, *line_sems,
):
    col = lax.axis_index("col")
    rows, width = unit_ref.shape
    heads, kinds = d_raw_ref.shape[:2]
    columns = heads * HEAD
    depth = parts_ref.shape[2]
    turned = pltpu.make_async_copy(unit_t_ref, turned_ref, load.at[kinds])
    turned.start()
    loads = [
        pltpu.make_async_copy(weight_ref.at[:, k], weights_ref.at[k], load.at[k]) for k in range(kinds)
    ]
    for one in loads:
        one.start()
    line = LineSum(parts_ref, cross_ref, line_ref, groups_here, line_sems)
    span = line.span
    barrier = pltpu.get_barrier_semaphore()
    pl.semaphore_signal(barrier, inc=1, device_id=line.partner, device_id_type=MESH)
    greet_all(line.me, span, groups_here, pieces_ref.shape[0], 1)
    for k in range(kinds):
        for h in range(heads):
            rows_ref[k, :, h * HEAD : (h + 1) * HEAD] = d_raw_ref[h, k]
    turned.wait()

    def part_of(owner):
        here = pl.ds(pl.multiple_of(owner * depth, depth), depth)
        for k in range(kinds):
            parts_ref[owner, k] = matmul(turned_ref[here, :], rows_ref[k]).astype(jnp.bfloat16)

    def for_partner(place, carry):
        part_of(line.owner(place, True))
        line.across(place).start()
        return carry

    def for_own(place, carry):
        part_of(line.owner(place, False))
        return carry

    lax.fori_loop(0, span, for_partner, 0)
    lax.fori_loop(0, span, for_own, 0)
    for place in (span - 1, 0):
        line.join(place)
    line.start(1)
    for place in range(1, span - 1):
        line.join(place)
    for one in loads:
        one.wait()
    count = sends.shape[0]
    size = rows // count
    moves = []
    for p in range(count):
        here = pl.ds(p * size, size)
        sum_ref[here, :] = matmul_nt(rows_ref[0, here, :], weights_ref[0].reshape(width, columns))
        for k in range(1, kinds):
            sum_ref[here, :] += matmul_nt(
                rows_ref[k, here, :], weights_ref[k].reshape(width, columns)
            )
        split_rows(sum_ref, unit_ref, pieces_ref, stats_ref, p * size, size)
        moves.append(
            Fold(pieces_ref, slots_ref, stats_ref, stat_slots_ref, p * size, size, sends.at[p], recvs.at[p])
        )
        moves[p].start()
        if p == 0:
            line.start(2)
    moves[0].forward()
    moves[1].forward()
    line.start(3)
    for p in range(count):
        moves[p].receive()

        def last_part(here):
            out_ref[here, :] = d_middle_ref[here, :] + normed_grad(
                sum_ref, slots_ref, stats_ref, stat_slots_ref, own_ref, inverse_ref, here, width, col
            )

        each_rows(p * size, size, 128, last_part)
    line.result(grad_ref)
    for one in moves:
        one.finish()
    line.finish()


def leave(d_raw, weight, unit_t, unit, own, inverse, d_middle, groups_here, count):
    rows, width = unit.shape
    heads, kinds = d_raw.shape[:2]
    owners, _, depth, columns = weight.shape
    span = owners // groups_here
    piece = width // count
    hbm = pl.BlockSpec(memory_space=pl.ANY)
    vmem = pl.BlockSpec(memory_space=pltpu.VMEM)
    dma = pltpu.SemaphoreType.DMA
    return pl.pallas_call(
        functools.partial(leave_kernel, groups_here),
        in_specs=[vmem, hbm, hbm] + [vmem] * 4,
        out_specs=[vmem, vmem],
        out_shape=[
            jax.ShapeDtypeStruct((rows, piece), jnp.float32),
            jax.ShapeDtypeStruct((kinds, depth, columns), jnp.float32),
        ],
        scratch_shapes=[
            pltpu.VMEM((kinds, rows, columns), jnp.bfloat16),
            pltpu.VMEM((rows, width), jnp.float32),
            pltpu.VMEM((count, rows, piece), jnp.bfloat16),
            pltpu.VMEM((count - 1, rows, piece), jnp.bfloat16),
            pltpu.VMEM((8, rows), jnp.float32),
            pltpu.VMEM((count - 1, 8, rows), jnp.float32),
            pltpu.VMEM((kinds, owners, depth, columns), jnp.bfloat16),
            pltpu.VMEM((width, rows), jnp.bfloat16),
            pltpu.VMEM((owners, kinds, depth, columns), jnp.bfloat16),
            pltpu.VMEM((span, kinds, depth, columns), jnp.bfloat16),
            pltpu.VMEM((2, span - 1, kinds, depth, columns), jnp.bfloat16),
            dma((2, 9)), dma((2, 9)), dma((kinds + 1,)),
            dma((span,)), dma((span,)), dma((2, span - 1)), dma((2, span - 1)),
        ],
        compiler_params=pltpu.CompilerParams(
            vmem_limit_bytes=63 * 2**20, collective_id=5, has_side_effects=True
        ),
        cost_estimate=pl.CostEstimate(
            flops=4 * rows * width * kinds * columns, bytes_accessed=100 * rows * width, transcendentals=0
        ),
        name="leave",
    )(d_raw, weight, unit_t, unit, own, inverse, d_middle)


def feed_front(unit_ref, cot_ref, weight_ref, two_ref, act, before=None):
    owners, _, _, depth, cols = weight_ref.shape
    rows, width = unit_ref.shape
    count, _, piece = cot_ref.shape
    gate_weight = weight_ref[:, 0, 0].reshape(width, cols)
    up_weight = weight_ref[:, 0, 1].reshape(width, cols)
    down_weight = weight_ref[:, 0, 2].reshape(width, cols)
    step = min(256, rows)
    for t in range(0, rows, step):
        here = pl.ds(t, step)
        unit = unit_ref[here, :]
        gate = matmul(unit, gate_weight)
        up_proj = matmul(unit, up_weight)
        d_hidden = sum(
            matmul(cot_ref[c, here, :], down_weight[c * piece : (c + 1) * piece])
            for c in range(count)
        )
        sigmoid_gate = jax.nn.sigmoid(gate)
        silu_gate = gate * sigmoid_gate
        act[0, here, :] = (silu_gate * up_proj).astype(jnp.bfloat16)
        act[1, here, :] = (
            d_hidden * up_proj * sigmoid_gate * (1.0 + gate * (1.0 - sigmoid_gate))
        ).astype(jnp.bfloat16)
        act[2, here, :] = (d_hidden * silu_gate).astype(jnp.bfloat16)
    if before is not None:
        before()
    for t in range(0, rows, step):
        here = pl.ds(t, step)
        two_ref[here, :] += matmul_nt(act[1, here, :], gate_weight) + matmul_nt(
            act[2, here, :], up_weight
        )


def feed_rear(unit_t_ref, cot_t_ref, grad_ref, act):
    owners, _, depth, cols = grad_ref.shape
    hidden, d_gate, d_up = act[0], act[1], act[2]
    for owner in range(owners):
        here = pl.ds(owner * depth, depth)
        unit_t = unit_t_ref[here, :]
        grad_ref[owner, 0] = matmul(unit_t, d_gate).astype(jnp.bfloat16)
        grad_ref[owner, 1] = matmul(unit_t, d_up).astype(jnp.bfloat16)
        grad_ref[owner, 2] = matmul(cot_t_ref[here, :], hidden).astype(jnp.bfloat16)


def feed_all_kernel(
    unit_ref, unit_t_ref, cot_ref, cot_t_ref, weight_ref, *refs
):
    old = refs[:-7]
    grad_ref, new_two_ref, new_out_ref, two_ref, out_ref, act_ref, sem = refs[-7:]
    tile = pl.program_id(0)

    loads = []
    if old:
        loads = [
            pltpu.make_async_copy(old[0], two_ref, sem.at[0]),
            pltpu.make_async_copy(old[1], out_ref, sem.at[1]),
        ]

    @pl.when(tile == 0)
    def _():
        for load in loads:
            load.start()
        if not old:
            two_ref[...] = jnp.zeros_like(two_ref)
            out_ref[...] = jnp.zeros_like(out_ref)

    def arrive():
        @pl.when(tile == 0)
        def _():
            for load in loads:
                load.wait()

    feed_front(unit_ref, cot_ref, weight_ref, two_ref, act_ref, arrive if old else None)
    final = tile == pl.num_programs(0) - 1
    copies = [
        pltpu.make_async_copy(two_ref, new_two_ref, sem.at[0]),
        pltpu.make_async_copy(out_ref, new_out_ref, sem.at[1]),
    ]

    @pl.when(final)
    def _():
        copies[0].start()

    down_weight = weight_ref[:, 0, 2].reshape(unit_ref.shape[1], weight_ref.shape[4])
    rows = unit_ref.shape[0]
    step = min(256, rows)
    for t in range(0, rows, step):
        here = pl.ds(t, step)
        out_ref[here, :] += matmul_nt(act_ref[0, here, :], down_weight)

    @pl.when(final)
    def _():
        copies[1].start()

    feed_rear(unit_t_ref, cot_t_ref, grad_ref, act_ref)

    @pl.when(final)
    def _():
        for copy in copies:
            copy.wait()


def feed_cost(rows, width, owners, tiles, depth, cols, matmuls):
    return pl.CostEstimate(
        flops=2 * matmuls * rows * width * tiles * cols,
        bytes_accessed=12 * owners * tiles * depth * cols,
        transcendentals=rows * tiles * cols,
    )


def feed_all(unit, unit_t, cot, cot_t, weights, tiles, old, blocks):
    rows, width = unit.shape
    owners, _, _, depth, cols = weights.shape
    hbm = pl.BlockSpec(memory_space=pl.ANY)
    return pl.pallas_call(
        feed_all_kernel,
        grid=(tiles,),
        in_specs=[
            resident((rows, width)), resident((width, rows)), resident(cot.shape),
            resident((width, rows)),
            pl.BlockSpec((owners, 1, 3, depth, cols), lambda i: (0, i, 0, 0, 0)),
        ] + [hbm] * len(old),
        out_specs=[pl.BlockSpec((owners, 3, depth, cols), lambda i: (0, i, 0, 0)), hbm, hbm],
        out_shape=[jax.ShapeDtypeStruct((owners, blocks, depth, cols), jnp.bfloat16)]
        + [jax.ShapeDtypeStruct((rows, width), jnp.float32)] * 2,
        scratch_shapes=[
            pltpu.VMEM((rows, width), jnp.float32),
            pltpu.VMEM((rows, width), jnp.float32),
            pltpu.VMEM((3, rows, cols), jnp.bfloat16),
            pltpu.SemaphoreType.DMA((2,)),
        ],
        compiler_params=pltpu.CompilerParams(vmem_limit_bytes=62 * 2**20),
        cost_estimate=feed_cost(rows, width, owners, tiles, depth, cols, 9),
        name="feed_all",
    )(unit, unit_t, cot, cot_t, weights, *old)


def feed_last_kernel(
    unit_hbm, unit_t_hbm, cots_hbm, cot_t_hbm, weight_hbm, old_two_hbm, old_out_hbm, own_ref,
    inverse_ref, out_t_hbm, back_ref, _,
    late_ref, ffn_ref, d_middle_ref, d_sent_ref,
    grad_ref, out_grad_ref, out_t_ref, unit_ref, turned_ref, cots_ref, weight_ref, two_ref, sum_ref, act_ref, pieces_ref, slots_ref,
    stats_ref, stat_slots_ref, d_pieces_ref,
    load, sends, recvs, g_sends, g_recvs,
):
    col = lax.axis_index("col")
    rows, width = unit_ref.shape
    count, _, piece = pieces_ref.shape
    owners, _, _, depth, cols = weight_ref.shape
    heads, _, size = back_ref.shape
    tile = weight_hbm.shape[1] - 1
    extra = late_ref.shape[1] - 3 - heads * size // cols

    def fetch(i, source, target):
        copy = pltpu.make_async_copy(source, target, load.at[i])
        copy.start()
        return copy

    loads = [
        fetch(0, unit_hbm, unit_ref), fetch(1, weight_hbm.at[:, pl.ds(tile, 1)], weight_ref), fetch(2, cots_hbm, cots_ref),
        fetch(3, old_two_hbm, two_ref), fetch(4, unit_t_hbm, turned_ref.at[0]),
        fetch(5, cot_t_hbm, turned_ref.at[1]), fetch(6, old_out_hbm.at[: rows // 4], sum_ref),
    ]
    greet_cols(count)
    for i in range(3):
        loads[i].wait()
    feed_front(unit_ref, cots_ref, weight_ref, two_ref, act_ref, loads[3].wait)
    turned_out = pltpu.make_async_copy(out_t_hbm.at[:, 3], out_t_ref, load.at[12])
    turned_out.start()
    parts = sends.shape[0]
    span = rows // parts
    moves, gathers = [], []
    for p in range(parts):
        split_rows(two_ref, unit_ref, pieces_ref, stats_ref, p * span, span)
        moves.append(
            Fold(pieces_ref, slots_ref, stats_ref, stat_slots_ref, p * span, span,
                 sends.at[p], recvs.at[p])
        )
        moves[p].start()
        own = d_pieces_ref.at[col]
        gathers.append(
            Gather(
                halves(own, p * span, span),
                lambda c, p=p: halves(d_pieces_ref.at[c], p * span, span),
                g_sends.at[p], g_recvs.at[p], None,
            )
        )
    quarter = rows // 4
    down_weight = weight_ref[:, 0, 2].reshape(width, cols)
    for p in range(4):
        here = pl.ds(p * quarter, quarter)
        loads[6 + p].wait()
        sum_ref[...] += matmul_nt(act_ref[0, here, :], down_weight)
        for c in range(count):
            ffn_ref[c, here, :] = sum_ref[:, c * piece : (c + 1) * piece].astype(jnp.bfloat16)
        if p < 3:
            loads.append(fetch(7 + p, old_out_hbm.at[pl.ds((p + 1) * quarter, quarter)], sum_ref))
    moves[0].forward()
    moves[1].forward()
    for i in range(4, 6):
        loads[i].wait()
    feed_rear(turned_ref.at[0], turned_ref.at[1], grad_ref, act_ref)
    stores = [fetch(10, grad_ref, late_ref.at[:, pl.ds(extra, 3)])]
    own_cot = cots_ref.at[col]
    for p in range(2, parts):
        moves[p].forward()
    for p in range(parts):
        moves[p].receive()

        def middle_part(here):
            d_middle = own_cot[here, :].astype(jnp.float32) + normed_grad(
                two_ref, slots_ref, stats_ref, stat_slots_ref, own_ref, inverse_ref, here, width, col
            )
            d_middle_ref[here, :] = d_middle
            d_pieces_ref[col, here, :] = d_middle.astype(jnp.bfloat16)

        each_rows(p * span, span, 128, middle_part)
        gathers[p].start()
        if p:
            gathers[p - 1].forward()
    gathers[parts - 1].forward()
    for one in moves:
        one.finish()
    for h in range(heads):
        pieces_ref[0, :, h * size : (h + 1) * size] = back_ref[h]
    turned_out.wait()
    out_t = out_t_ref[...].reshape(width, heads * size)
    for p in range(parts):
        gathers[p].receive()
        here = pl.ds(p * span, span)
        d_attended = sum(
            matmul(d_pieces_ref[c, here, :], out_t[c * piece : (c + 1) * piece]) for c in range(count)
        )
        for h in range(heads):
            d_sent_ref[h, here, :] = d_attended[:, h * size : (h + 1) * size].astype(jnp.bfloat16)
    per_piece = piece // depth
    for owner in range(owners):
        at = (owner % per_piece) * depth
        turned = lax.dot_general(
            d_pieces_ref[owner // per_piece, :, at : at + depth], pieces_ref[0],
            (((0,), (0,)), ((), ())), preferred_element_type=jnp.float32,
        ).astype(jnp.bfloat16)
        for j in range(heads * size // cols):
            out_grad_ref[owner, j] = turned[:, j * cols : (j + 1) * cols]
    stores.append(fetch(11, out_grad_ref, late_ref.at[:, pl.ds(extra + 3, heads * size // cols)]))
    for one in stores:
        one.wait()
    for one in gathers:
        one.finish()


def feed_last(unit, unit_t, cots, cot_t, weights, old, own, inverse, out_t, back, late):
    rows, width = unit.shape
    count, _, piece = cots.shape
    owners, _, _, depth, cols = weights.shape
    heads, _, size = back.shape
    hbm = pl.BlockSpec(memory_space=pl.ANY)
    vmem = pl.BlockSpec(memory_space=pltpu.VMEM)
    dma = pltpu.SemaphoreType.DMA
    shape = jax.ShapeDtypeStruct
    return pl.pallas_call(
        feed_last_kernel,
        in_specs=[hbm] * 7 + [vmem] * 2 + [hbm, vmem, hbm],
        out_specs=[hbm] + [vmem] * 3,
        input_output_aliases={11: 0},
        out_shape=[
            shape(late.shape, jnp.bfloat16),
            shape((count, rows, piece), jnp.bfloat16),
            shape((rows, piece), jnp.float32),
            shape((heads, rows, size), jnp.bfloat16),
        ],
        scratch_shapes=[
            pltpu.VMEM((owners, 3, depth, cols), jnp.bfloat16),
            pltpu.VMEM((owners, heads * size // cols, depth, cols), jnp.bfloat16),
            pltpu.VMEM((owners, depth, heads * size), jnp.bfloat16),
            pltpu.VMEM((rows, width), jnp.bfloat16),
            pltpu.VMEM((2, width, rows), jnp.bfloat16),
            pltpu.VMEM((count, rows, piece), jnp.bfloat16),
            pltpu.VMEM((owners, 1, 3, depth, cols), jnp.bfloat16),
            pltpu.VMEM((rows, width), jnp.float32),
            pltpu.VMEM((rows // 4, width), jnp.float32),
            pltpu.VMEM((3, rows, cols), jnp.bfloat16),
            pltpu.VMEM((count, rows, piece), jnp.bfloat16),
            pltpu.VMEM((count - 1, rows, piece), jnp.bfloat16),
            pltpu.VMEM((8, rows), jnp.float32),
            pltpu.VMEM((count - 1, 8, rows), jnp.float32),
            pltpu.VMEM((count, rows, piece), jnp.bfloat16),
            dma((13,)), dma((4, 9)), dma((4, 9)), dma((4, 6)), dma((4, 6)),
        ],
        compiler_params=pltpu.CompilerParams(
            vmem_limit_bytes=63 * 2**20 + 2**19, collective_id=6, has_side_effects=True
        ),
        cost_estimate=pl.CostEstimate(
            flops=18 * rows * width * cols, bytes_accessed=100 * rows * width,
            transcendentals=rows * cols,
        ),
        name="feed_last",
    )(unit, unit_t, cots, cot_t, weights, *old, own, inverse, out_t, back, late)


def unpack_kernel(with_out, blocks_ref, *refs):
    outs = refs[-4:] if with_out else refs[-3:]
    outs[0][...] = blocks_ref[0].astype(jnp.float32)
    outs[1][...] = blocks_ref[1].astype(jnp.float32)
    outs[2][...] = blocks_ref[2].astype(jnp.float32).T
    if with_out:

        @pl.when(pl.program_id(0) == 0)
        def _():
            extra, cols = refs[0].shape[0], refs[0].shape[2]
            for j in range(extra):
                outs[3][j * cols : (j + 1) * cols, :] = refs[0][j].astype(jnp.float32).T


def unpack(blocks, skip, count, hidden, old, extra=0):
    _, depth, cols = blocks.shape
    shapes = [(depth, hidden), (depth, hidden), (hidden, depth)]
    wide = pl.BlockSpec((depth, cols), lambda i: (0, skip + i))
    in_specs = [pl.BlockSpec((3, depth, cols), lambda i: (i, 0, 0))]
    out_specs = [wide, wide, pl.BlockSpec((cols, depth), lambda i: (skip + i, 0))]
    given = [blocks]
    if extra:
        assert 3 * count % extra == 0
        in_specs.append(pl.BlockSpec((extra, depth, cols), lambda i: (3 * count // extra, 0, 0)))
        out_specs.append(pl.BlockSpec((extra * cols, depth), lambda i: (0, 0)))
        shapes.append((extra * cols, depth))
        given.append(blocks)
    return pl.pallas_call(
        functools.partial(unpack_kernel, bool(extra)),
        grid=(count,),
        in_specs=in_specs + [pl.BlockSpec(memory_space=pl.ANY)] * len(old),
        out_specs=out_specs,
        out_shape=[jax.ShapeDtypeStruct(one, jnp.float32) for one in shapes],
        input_output_aliases={len(given) + i: i for i in range(len(old))},
        name="unpack",
    )(*given, *old)


def group_rows(lengths, group, begin, count):
    row_lengths = lax.dynamic_slice_in_dim(lengths, group, 1, 0)[0]
    local_index = begin + jnp.arange(count, dtype=jnp.int32)
    seg_ends = jnp.cumsum(row_lengths)
    seg_starts = seg_ends - row_lengths
    after_prompt = local_index - PROMPT
    inside = (after_prompt[:, None] >= seg_starts[None, :]) & (
        after_prompt[:, None] < seg_ends[None, :]
    )
    start = jnp.sum(jnp.where(inside, seg_starts[None, :], 0), axis=1)
    in_prompt = local_index < PROMPT
    start_row = jnp.where(in_prompt, 0, PROMPT + start)
    position = jnp.where(in_prompt, local_index, PROMPT + after_prompt - start)
    return start_row, position


def rotary(position):
    half = HEAD // 2
    frequency = jnp.exp(
        -math.log(rope_base) * (2.0 * jnp.arange(half, dtype=jnp.float32) / HEAD)
    )
    angles = position.astype(jnp.float32)[:, None] * frequency[None, :]
    cosine, sine = jnp.cos(angles), jnp.sin(angles)
    return jnp.concatenate([cosine, cosine], axis=1), jnp.concatenate([sine, -sine], axis=1)


def fast_body(
    inputs,
    cotangent,
    lengths,
    query_key_value_weight,
    out_weight,
    gate_weight,
    up_weight,
    down_weight,
):
    tok_rows, part_width = inputs.shape
    col_count = lax.axis_size("col")
    col_index = lax.axis_index("col")
    row_index = lax.axis_index("row")
    span = GROUP_LEN // tok_rows
    groups_here = lax.axis_size("row") // span
    heads_here = part_width // HEAD
    place = row_index // groups_here
    group = row_index % groups_here
    depth = gate_weight.shape[0]
    hidden_here = gate_weight.shape[1]
    tiles = hidden_here // min(256, depth)
    tile = hidden_here // tiles

    def gather(shard, after=None):
        if after is not None:
            shard, after = tied(shard, after)
        return lax.all_gather(shard, "row"), after

    def tied(value, *others):
        return lax.optimization_barrier((value, *others))

    mixed = jnp.concatenate([query_key_value_weight.transpose(1, 0, 2), out_weight.T[None]])
    weights, _ = gather(mixed)
    packed = jnp.stack([gate_weight, up_weight, down_weight.T]).reshape(3, depth, tiles, tile)
    packed = packed.transpose(2, 0, 1, 3)
    first = max(1, tiles // 2)
    early, later = lax.optimization_barrier((packed[:first], packed[first:]))
    pieces, cots, normed_one, unit_one_t, unit_one, inverse_one = enter(
        inputs, cotangent, col_count
    )
    normed_one, weights, lengths = tied(normed_one, weights, lengths)
    feed_one, weights = gather(early, weights)
    own_cos, own_sin = rotary(group_rows(lengths, group, place * tok_rows, tok_rows)[1])
    start_rows, positions = group_rows(lengths, group, 0, GROUP_LEN)
    start_rows = start_rows.reshape(-1, 1, BLOCK)
    positions = positions.astype(jnp.float32).reshape(-1, 1, BLOCK)
    sent = project(normed_one, weights, own_cos, own_sin)
    back, held, attended_head, lse, out_t = attend(
        sent, start_rows, weights, groups_here, col_count
    )
    out_t = out_t.reshape(col_count, -1, part_width)
    back, feed_one = tied(back, feed_one)
    feed_two, feed_one = gather(later, feed_one)
    cots, back = tied(cots, back)
    cot_t = cots.transpose(0, 2, 1).reshape(-1, tok_rows)
    normed_two, unit_t, middle, unit_two, inverse_two = branch(back, out_t, pieces)
    rows_two = (normed_two, unit_t, cots, cot_t)

    def owned(part):
        return lax.psum_scatter(part, "row", scatter_dimension=0, tiled=True)[0]

    grads_one, *sums = feed_all(*rows_two, feed_one, first, (), 3 * first)
    sums[0], grads_one, feed_two = tied(sums[0], grads_one, feed_two)
    grads_one = owned(grads_one)
    rest = tiles - first - 1
    blocks = 3 * (rest + 1) + part_width // tile
    late, *sums = feed_all(*rows_two, feed_two, rest, sums, blocks)
    late, ffn_pieces, d_middle, d_sent = feed_last(
        *rows_two, feed_two, sums, unit_two, inverse_two, weights, back, late
    )
    late, grads_one = tied(late, grads_one)
    late = owned(late)
    grads = unpack(grads_one, 0, first, hidden_here, ())
    d_sent, *grads = tied(d_sent, *grads)
    d_raw, output = attend_back(
        d_sent, held, attended_head, lse, start_rows, positions, ffn_pieces, middle, groups_here
    )
    input_grad, own_grads = leave(
        d_raw, weights, unit_one_t, normed_one, unit_one, inverse_one, d_middle, groups_here, col_count
    )
    qkv_grad = own_grads.transpose(1, 0, 2)
    *grads, out_grad = unpack(late, first, rest + 1, hidden_here, grads, part_width // tile)
    return (output, input_grad, qkv_grad, out_grad, *grads)


def body(
    inputs,
    cotangent,
    lengths,
    query_key_value_weight,
    out_weight,
    gate_weight,
    up_weight,
    down_weight,
):
    tok_rows = inputs.shape[0]
    part_width = inputs.shape[1]
    col_count = lax.axis_size("col")
    col_index = lax.axis_index("col")
    row_index = lax.axis_index("row")
    full_width = float(part_width * col_count)
    group_span = GROUP_LEN // tok_rows
    groups_here = lax.axis_size("row") // group_span
    head_size = HEAD
    heads_here = part_width // head_size
    score_scale = head_size ** (-0.5)
    block_place = row_index // groups_here
    full_inputs, full_cotangent = (
        lax.all_gather(inputs, "col", axis=1, tiled=True),
        lax.all_gather(cotangent, "col", axis=1, tiled=True),
    )
    projection_full_rows, out_full, gate_full, up_full, down_full = (
        lax.all_gather(query_key_value_weight, "row", axis=0, tiled=True),
        lax.all_gather(out_weight, "row", axis=1, tiled=True),
        lax.all_gather(gate_weight, "row", axis=0, tiled=True),
        lax.all_gather(up_weight, "row", axis=0, tiled=True),
        lax.all_gather(down_weight, "row", axis=1, tiled=True),
    )
    unit_one, inverse_one = normalize_rows(full_inputs.astype(jnp.float32))
    first_normed_input = unit_one.astype(jnp.bfloat16)
    raw_projection_output = jnp.einsum(
        "cu,ufk->cfk", first_normed_input, projection_full_rows, preferred_element_type=jnp.float32
    )
    raw_projection_output = raw_projection_output.reshape(tok_rows, 3, heads_here, head_size)
    own_meta = token_layout(lengths, row_index, groups_here, tok_rows)
    cosine, sine = rotation_angles(own_meta[3], head_size)
    queries = rotate(raw_projection_output[:, 0], cosine, sine, False).astype(jnp.bfloat16)
    key_rows = rotate(raw_projection_output[:, 1], cosine, sine, False).astype(jnp.bfloat16)
    value_rows = raw_projection_output[:, 2].astype(jnp.bfloat16)
    pieces = [(key_rows, value_rows)]
    for shift_by in range(1, group_span):
        pieces.append(passed_along((key_rows, value_rows), "row", shift_by * groups_here))
    visibility = [
        visible_mask(
            own_meta,
            token_layout(lengths, row_index - shift_by * groups_here, groups_here, tok_rows),
        )
        for shift_by in range(group_span)
    ]
    live_piece = [shift_by <= block_place for shift_by in range(group_span)]
    first_scores = score_block(queries, pieces[0][0], visibility[0], score_scale)
    top_rows = jnp.max(first_scores, axis=-1, keepdims=True)
    total_rows = jnp.sum(jnp.exp(first_scores - top_rows), axis=-1, keepdims=True)
    for shift_by in range(1, group_span):

        def add_stats(carry, shift_by=shift_by):
            old_top, old_total = carry
            scores = score_block(queries, pieces[shift_by][0], visibility[shift_by], score_scale)
            new_top = jnp.maximum(old_top, jnp.max(scores, axis=-1, keepdims=True))
            new_total = old_total * jnp.exp(old_top - new_top) + jnp.sum(
                jnp.exp(scores - new_top), axis=-1, keepdims=True
            )
            return (new_top, new_total)

        top_rows, total_rows = lax.cond(
            live_piece[shift_by], add_stats, lambda carry: carry, (top_rows, total_rows)
        )
    log_total = top_rows + jnp.log(total_rows)
    attended = jnp.zeros((tok_rows, heads_here, head_size), jnp.float32)
    for shift_by in range(group_span):

        def add_values(total, shift_by=shift_by):
            scores = score_block(queries, pieces[shift_by][0], visibility[shift_by], score_scale)
            probs_low = jnp.exp(scores - log_total).astype(jnp.bfloat16)
            return total + jnp.einsum(
                "hqk,khd->qhd", probs_low, pieces[shift_by][1], preferred_element_type=jnp.float32
            )

        attended = lax.cond(live_piece[shift_by], add_values, lambda total: total, attended)
    attended_flat = attended.reshape(tok_rows, part_width).astype(jnp.bfloat16)
    branch_terms = jnp.dot(attended_flat, out_full, preferred_element_type=jnp.float32)
    branch_full = lax.psum(branch_terms, "col")
    middle_full = full_inputs.astype(jnp.float32) + branch_full
    middle = lax.dynamic_slice_in_dim(middle_full, col_index * part_width, part_width, 1)
    unit_two, inverse_two = normalize_rows(middle_full)
    normed_two = unit_two.astype(jnp.bfloat16)
    gate = jnp.dot(normed_two, gate_full, preferred_element_type=jnp.float32)
    up_proj = jnp.dot(normed_two, up_full, preferred_element_type=jnp.float32)
    sigmoid_gate = jax.nn.sigmoid(gate)
    silu_gate = gate * sigmoid_gate
    hidden = (silu_gate * up_proj).astype(jnp.bfloat16)
    ffn_terms = jnp.dot(hidden, down_full, preferred_element_type=jnp.float32)
    ffn_part = lax.psum_scatter(
        ffn_terms.astype(jnp.bfloat16), "col", scatter_dimension=1, tiled=True
    ).astype(jnp.float32)
    output = (middle + ffn_part).astype(jnp.bfloat16)
    projection_full_rows, out_full, gate_full, up_full, down_full = (
        lax.all_gather(query_key_value_weight, "row", axis=0, tiled=True),
        lax.all_gather(out_weight, "row", axis=1, tiled=True),
        lax.all_gather(gate_weight, "row", axis=0, tiled=True),
        lax.all_gather(up_weight, "row", axis=0, tiled=True),
        lax.all_gather(down_weight, "row", axis=1, tiled=True),
    )
    d_hidden = jnp.einsum(
        "td,fd->tf", full_cotangent, down_full, preferred_element_type=jnp.float32
    )
    down_part = jnp.einsum("tf,td->fd", hidden, full_cotangent, preferred_element_type=jnp.float32)
    d_gate = (d_hidden * up_proj * sigmoid_gate * (1.0 + gate * (1.0 - sigmoid_gate))).astype(
        jnp.bfloat16
    )
    d_up = (d_hidden * silu_gate).astype(jnp.bfloat16)
    gate_part = jnp.einsum("td,tf->df", normed_two, d_gate, preferred_element_type=jnp.float32)
    up_part = jnp.einsum("td,tf->df", normed_two, d_up, preferred_element_type=jnp.float32)
    d_normed_two = jnp.einsum(
        "tf,df->td", d_gate, gate_full, preferred_element_type=jnp.float32
    ) + jnp.einsum("tf,df->td", d_up, up_full, preferred_element_type=jnp.float32)
    grad_two, sum_two, cross_two = (
        lax.psum_scatter(
            d_normed_two.astype(jnp.bfloat16), "col", scatter_dimension=1, tiled=True
        ).astype(jnp.float32),
        lax.psum_scatter(
            spread_cols(jnp.sum(d_normed_two, axis=1), col_count).astype(jnp.bfloat16),
            "col",
            scatter_dimension=1,
            tiled=True,
        ).astype(jnp.float32),
        lax.psum_scatter(
            spread_cols(jnp.sum(d_normed_two * unit_two, axis=1), col_count).astype(jnp.bfloat16),
            "col",
            scatter_dimension=1,
            tiled=True,
        ).astype(jnp.float32),
    )
    unit_two_here = lax.dynamic_slice_in_dim(unit_two, col_index * part_width, part_width, 1)
    d_middle = cotangent.astype(jnp.float32) + normalize_back(
        grad_two, sum_two, cross_two, unit_two_here, inverse_two, full_width
    )
    d_branch = d_middle.astype(jnp.bfloat16)
    d_branch_full = lax.all_gather(d_branch, "col", axis=1, tiled=True)
    out_part = jnp.einsum(
        "tc,td->cd", attended_flat, d_branch_full, preferred_element_type=jnp.float32
    )
    d_attended = jnp.einsum(
        "td,cd->tc", d_branch_full, out_full, preferred_element_type=jnp.float32
    )
    d_attended = d_attended.astype(jnp.bfloat16).reshape(tok_rows, heads_here, head_size)
    delta_rows = jnp.zeros((heads_here, tok_rows, 1), jnp.float32)
    for shift_by in range(group_span):

        def add_delta(total, shift_by=shift_by):
            scores = score_block(queries, pieces[shift_by][0], visibility[shift_by], score_scale)
            probs_full = jnp.exp(scores - log_total)
            d_probs = jnp.einsum(
                "qhd,khd->hqk", d_attended, pieces[shift_by][1], preferred_element_type=jnp.float32
            )
            return total + jnp.sum(probs_full * d_probs, axis=-1, keepdims=True)

        delta_rows = lax.cond(live_piece[shift_by], add_delta, lambda total: total, delta_rows)
    zero_rows = jnp.zeros((tok_rows, heads_here, head_size), jnp.float32)
    d_queries = zero_rows
    for shift_by in range(group_span):

        def piece_grads(query_total, shift_by=shift_by):
            key_part, value_part = pieces[shift_by]
            scores = score_block(queries, key_part, visibility[shift_by], score_scale)
            probs_full = jnp.exp(scores - log_total)
            d_probs = jnp.einsum(
                "qhd,khd->hqk", d_attended, value_part, preferred_element_type=jnp.float32
            )
            d_scores = (probs_full * (d_probs - delta_rows)).astype(jnp.bfloat16)
            query_total = (
                query_total
                + jnp.einsum("hqk,khd->qhd", d_scores, key_part, preferred_element_type=jnp.float32)
                * score_scale
            )
            d_key_part = (
                jnp.einsum("hqk,qhd->khd", d_scores, queries, preferred_element_type=jnp.float32)
                * score_scale
            )
            d_value_part = jnp.einsum(
                "hqk,qhd->khd",
                probs_full.astype(jnp.bfloat16),
                d_attended,
                preferred_element_type=jnp.float32,
            )
            return (query_total, d_key_part, d_value_part)

        d_queries, d_key_part, d_value_part = lax.cond(
            live_piece[shift_by],
            piece_grads,
            lambda query_total: (query_total, zero_rows, zero_rows),
            d_queries,
        )
        if shift_by == 0:
            d_keys = d_key_part
            d_values = d_value_part
        else:
            back_keys, back_values = (
                passed_along(
                    d_key_part.astype(jnp.bfloat16), "row", -shift_by * groups_here
                ).astype(d_key_part.dtype),
                passed_along(
                    d_value_part.astype(jnp.bfloat16), "row", -shift_by * groups_here
                ).astype(d_value_part.dtype),
            )
            d_keys = d_keys + back_keys
            d_values = d_values + back_values
    raw_score_gradient = jnp.stack(
        [rotate(d_queries, cosine, sine, True), rotate(d_keys, cosine, sine, True), d_values],
        axis=1,
    )
    raw_score_gradient = raw_score_gradient.reshape(tok_rows, 3, part_width).astype(jnp.bfloat16)
    projection_part_rows = jnp.einsum(
        "lo,lbw->obw", first_normed_input, raw_score_gradient, preferred_element_type=jnp.float32
    )
    first_normed_gradient = jnp.einsum(
        "xzq,vzq->xv", raw_score_gradient, projection_full_rows, preferred_element_type=jnp.float32
    )
    grad_one, sum_one, cross_one = (
        lax.psum_scatter(
            first_normed_gradient.astype(jnp.bfloat16), "col", scatter_dimension=1, tiled=True
        ).astype(jnp.float32),
        lax.psum_scatter(
            spread_cols(jnp.sum(first_normed_gradient, axis=1), col_count).astype(jnp.bfloat16),
            "col",
            scatter_dimension=1,
            tiled=True,
        ).astype(jnp.float32),
        lax.psum_scatter(
            spread_cols(jnp.sum(first_normed_gradient * unit_one, axis=1), col_count).astype(
                jnp.bfloat16
            ),
            "col",
            scatter_dimension=1,
            tiled=True,
        ).astype(jnp.float32),
    )
    unit_one_here = lax.dynamic_slice_in_dim(unit_one, col_index * part_width, part_width, 1)
    input_grad = d_middle + normalize_back(
        grad_one, sum_one, cross_one, unit_one_here, inverse_one, full_width
    )
    owned_grads = (
        lax.psum_scatter(
            projection_part_rows.astype(jnp.bfloat16), "row", scatter_dimension=0, tiled=True
        ).astype(jnp.float32),
        lax.psum_scatter(
            out_part.astype(jnp.bfloat16), "row", scatter_dimension=1, tiled=True
        ).astype(jnp.float32),
        lax.psum_scatter(
            gate_part.astype(jnp.bfloat16), "row", scatter_dimension=0, tiled=True
        ).astype(jnp.float32),
        lax.psum_scatter(
            up_part.astype(jnp.bfloat16), "row", scatter_dimension=0, tiled=True
        ).astype(jnp.float32),
        lax.psum_scatter(
            down_part.astype(jnp.bfloat16), "row", scatter_dimension=1, tiled=True
        ).astype(jnp.float32),
    )
    return (
        output,
        input_grad,
        owned_grads[0],
        owned_grads[1],
        owned_grads[2],
        owned_grads[3],
        owned_grads[4],
    )


def step(inputs, *rest):
    span = GROUP_LEN // inputs.shape[0]
    heads_here = inputs.shape[1] // HEAD
    fast = heads_here == span and lax.axis_size("col") == 4 and lax.axis_size("row") == 2 * span
    return (fast_body if fast else body)(inputs, *rest)


def solution(mesh):
    placed = (
        P("row", "col"),
        P("row", "col"),
        P(),
        P("row", None, "col"),
        P("col", "row"),
        P("row", "col"),
        P("row", "col"),
        P("col", "row"),
    )
    return jax.shard_map(
        step,
        mesh=mesh,
        in_specs=placed,
        out_specs=(
            P("row", "col"),
            P("row", "col"),
            P("row", None, "col"),
            P("col", "row"),
            P("row", "col"),
            P("row", "col"),
            P("col", "row"),
        ),
        check_vma=False,
    )
```
